32 devices in a mesh: dp: 8 (over y, x, core), tensor: 4 (over z).
Axes of the slice: x: 2, y: 2, z: 4, core: 2. Of those that a mesh axis runs over, the one named last changes fastest.
Arguments:
- tokens: bfloat16 [8192, 1536], P('dp'), may hold values from -6 to 6
- teacher_feats: bfloat16 [8192, 256], P('dp'), may hold values from -12 to 12
- masks: int32 [32, 256], P('dp'), may hold values from 0 to 1, as said below
- w_in: bfloat16 [1536, 2048], P('dp'), may hold values from -0.15625 to 0.15625
- w_out: bfloat16 [2048, 256], P('dp'), may hold values from -0.125 to 0.125
- proto_student: bfloat16 [256, 131072], P(None, ('dp', 'tensor')), may hold values from -0.375 to 0.375
- proto_teacher: bfloat16 [256, 131072], P(None, ('dp', 'tensor')), may hold values from -1 to 1
Outputs:
- d_tokens: bfloat16 [8192, 1536], P('dp')
- grad_in: float32 [1536, 2048], P('dp')
- grad_out: float32 [2048, 256], P('dp')
- grad_proto: float32 [256, 131072], P(None, ('dp', 'tensor'))
- crop_loss: float32 [32], P('dp')
The draws below stay inside these ranges and needn't reach their ends.
Inputs may be any that keep to these rules, and one draw needn't show every extreme that they name: `masks`: the crops of one index of dp hold 256 or fewer masked patches together, exactly 256 on some index; a crop holds at most 129.
All inputs are finite; a program needn't handle non-finite values.
Results may differ from the reference program's by a relative error of at most 0.02.
Values may be sent and summed in bfloat16 or wider, within the bound.
A program may use at most 192 MiB of HBM per device.

```python
import math
import jax
import jax.numpy as jnp
from jax import lax

D = 1536
HID = 2048
BOT = 256
PROTOS = 131072
PATCHES = 256
ROUNDS = 3
CROPS_DEV = 4
CAP = 256
CROPS = 32
N_DP = 8
N_TENSOR = 4


def draw_masks(key, part):
    crops = CROPS_DEV * N_DP
    base_key = jax.random.fold_in(key, 4241)
    key_total, key_full, key_move, key_perm = jax.random.split(base_key, 4)
    totals = jax.random.randint(key_total, (N_DP,), CAP // 4, CAP + 1)
    fullest = jax.random.randint(key_full, (), 0, N_DP)
    totals = jnp.where(jnp.arange(N_DP) == fullest, CAP, totals)
    base = totals // CROPS_DEV
    extra = totals % CROPS_DEV
    counts = base[:, None] + (jnp.arange(CROPS_DEV)[None, :] < extra[:, None]).astype(jnp.int32)
    pairs = counts.reshape(N_DP, CROPS_DEV // 2, 2)
    moved = jax.random.randint(key_move, (N_DP, CROPS_DEV // 2), 0, base[:, None] + 1)
    pairs = pairs + jnp.stack([moved, -moved], axis=-1)
    counts = pairs.reshape(crops)
    orders = jax.vmap(lambda sub: jax.random.permutation(sub, PATCHES))(jax.random.split(key_perm, crops))
    return (orders < counts[:, None]).astype(jnp.int32)


def cluster_layout(key, spread):
    cluster_total = 24
    base_key = jax.random.fold_in(key, 7001)
    key_dir, key_rows, key_cols = jax.random.split(base_key, 3)
    centres = jax.random.normal(key_dir, (cluster_total, BOT), jnp.float32)
    centres = centres / jnp.sqrt(jnp.sum(centres * centres, axis=1, keepdims=True))
    ladder = jnp.arange(cluster_total).astype(jnp.float32) / (cluster_total - 1.0)
    row_logits = spread * jnp.take(ladder, jax.random.permutation(key_rows, cluster_total))
    col_logits = spread * jnp.take(ladder, jax.random.permutation(key_cols, cluster_total))
    return (centres, row_logits, col_logits)


def draw_teacher_feats(key, part):
    patch_total = CROPS_DEV * N_DP * PATCHES
    spread = math.log(10.0)
    centres, row_logits, col_logits = cluster_layout(key, spread)
    own_key = jax.random.fold_in(key, 7103)
    key_pick, key_noise = jax.random.split(own_key, 2)
    chosen = jax.random.categorical(key_pick, row_logits, shape=(patch_total,))
    root_bot = math.sqrt(BOT)
    noise = jax.random.normal(key_noise, (patch_total, BOT), jnp.float32)
    values = jnp.take(centres, chosen, axis=0) * root_bot + 1.1 * noise
    return jnp.clip(values, -12.0, 12.0).astype(jnp.bfloat16)


def draw_proto_teacher(key, part):
    spread = math.log(10.0)
    centres, row_logits, col_logits = cluster_layout(key, spread)
    own_key = jax.random.fold_in(key, 7207)
    key_pick, key_noise = jax.random.split(own_key, 2)
    shard_cols = PROTOS // (N_DP * N_TENSOR)
    owner = jnp.arange(PROTOS) // shard_cols % N_TENSOR
    tied = (jnp.arange(24)[None, :] % N_TENSOR == owner[:, None]).astype(jnp.float32)
    logits = col_logits[None, :] + 4.0 * tied
    chosen = jax.random.categorical(key_pick, logits, axis=1)
    root_bot = math.sqrt(BOT)
    noise = jax.random.normal(key_noise, (BOT, PROTOS), jnp.float32)
    values = (jnp.take(centres, chosen, axis=0).T * root_bot + 1.1 * noise) / root_bot
    return jnp.clip(values, -1.0, 1.0).astype(jnp.bfloat16)


def spiked(drawn, key, source, target, blocks, factor):
    owner, partner = [(jnp.arange(drawn.shape[axis_at]) // (drawn.shape[axis_at] // blocks)).reshape([-1 if axis == axis_at else 1 for axis in range(drawn.ndim)]) for axis_at in (source, target)]
    chosen = jax.random.permutation(key, blocks)[partner]
    strong = (owner == chosen) | (owner == (partner + blocks // 2) % blocks)
    return jnp.where(strong, factor * drawn, drawn)


def block_scale(stream_key, shape, cuts, least, top_value):
    def one(position, blocks):
        steps = jax.random.uniform(jax.random.fold_in(jax.random.fold_in(stream_key, 6), position), (blocks,), jnp.float32, least / len(cuts), top_value / len(cuts))
        return jnp.repeat(jnp.exp(steps), shape[position] // blocks).reshape((-1,) + (1,) * (len(shape) - position - 1))

    gain = one(*cuts[0])
    for cut in cuts[1:]:
        gain = gain * one(*cut)
    return gain


def gaussian(key, extent, scale, bound, cuts=(), dtype=jnp.bfloat16):
    values = jax.random.normal(key, extent, jnp.float32) * scale
    if len(cuts) > 0:
        values = block_scale(key, extent, cuts, -0.22, 0.18) * values
    return jnp.clip(values, min=-bound, max=bound).astype(dtype)


def noise_with(stream_key, shape, deviation, reach, cuts, heavy, held_as=jnp.bfloat16):
    result = deviation * jax.random.normal(stream_key, shape, jnp.float32)
    if cuts:
        result = result * block_scale(stream_key, shape, cuts, -0.22, 0.18)
    return jnp.clip(spiked(result, jax.random.fold_in(stream_key, 3), *heavy), -reach, reach).astype(held_as)


def setup_inputs(seed: int = 0) -> dict:
    streams_of = jax.random.split(jax.random.key(seed), 8)
    return {
        "tokens": noise_with(streams_of[0], (CROPS * PATCHES, D), 1.0, 6.0, ((0, 8),), (0, 1, 8, 2.0)),
        "teacher_feats": draw_teacher_feats(jax.random.fold_in(streams_of[7], 71), 0),
        "masks": draw_masks(jax.random.fold_in(streams_of[7], 71), 0),
        "w_in": gaussian(streams_of[3], (D, HID), D ** -0.5, 0.15625, ((0, 8),)),
        "w_out": gaussian(streams_of[4], (HID, BOT), HID ** -0.5, 0.125, ((0, 8),)),
        "proto_student": gaussian(streams_of[5], (BOT, PROTOS), BOT ** -0.5, 0.375, ((1, 32),)),
        "proto_teacher": draw_proto_teacher(jax.random.fold_in(streams_of[7], 71), 0),
    }


TEACHER_TEMP = 0.07
STUDENT_TEMP = 0.1
EPS = 1e-06
GRAD_SCALE = 65536.0

def gelu_parts(pre):
    cdf = 0.5 * (1.0 + lax.erf(pre * 0.7071067811865476))
    pdf = jnp.exp(-0.5 * pre * pre) * 0.3989422804014327
    return (pre * cdf, cdf + pre * pdf)

def unit_rows(feats):
    inverse = lax.rsqrt(lax.optimization_barrier(jnp.sum(feats * feats, axis=1, keepdims=True)) + EPS)
    return (feats * inverse, inverse)

def unit_columns(protos):
    wide = protos.astype(jnp.float32)
    norms = jnp.sqrt(lax.optimization_barrier(jnp.sum(wide * wide, axis=0, keepdims=True)) + EPS)
    return (wide / norms, norms)

def matmul(left, right):
    return jnp.dot(left.astype(jnp.float32), right.astype(jnp.float32), precision=lax.Precision.HIGHEST)

def rounded(value):
    return lax.optimization_barrier(value.astype(jnp.bfloat16)).astype(jnp.float32)

def reference(tokens, teacher_feats, masks, w_in, w_out, proto_student, proto_teacher):
    groups = N_DP
    per_dev = CROPS_DEV * PATCHES
    total = groups * CAP
    flat = masks.reshape(groups, per_dev)

    def pick(bits):
        return jnp.nonzero(bits, size=CAP, fill_value=0)[0].astype(jnp.int32)
    index = jax.vmap(pick)(flat)
    count = lax.optimization_barrier(jnp.sum(flat, axis=1))
    livef = (jnp.arange(CAP)[None, :] < count[:, None]).astype(jnp.float32)
    crop_count = lax.optimization_barrier(jnp.sum(masks, axis=1)).reshape(groups, CROPS_DEV)
    inverse = 1.0 / jnp.maximum(crop_count, 1).astype(jnp.float32)
    member = (index[:, :, None] // PATCHES == jnp.arange(CROPS_DEV)[None, None, :]).astype(jnp.float32) * livef[:, :, None]
    weight = (GRAD_SCALE * lax.optimization_barrier(jnp.sum(member * inverse[:, None, :], axis=2))).astype(jnp.bfloat16)

    def take_rows(table, idx):
        return table[idx]
    rows = jax.vmap(take_rows)(tokens.reshape(groups, per_dev, D), index).reshape(total, D)
    teacher_pick = jax.vmap(take_rows)(teacher_feats.reshape(groups, per_dev, BOT), index).reshape(total, BOT)
    live_all = livef.reshape(total)
    weight_all = weight.reshape(total).astype(jnp.float32)
    pre = matmul(rows, w_in)
    act, slope = gelu_parts(pre)
    hidden = act.astype(jnp.bfloat16)
    feats = matmul(hidden, w_out)
    unit, inv = unit_rows(feats)
    student_rows = unit.astype(jnp.bfloat16).astype(jnp.float32)
    teacher_rows = unit_rows(teacher_pick.astype(jnp.float32))[0].astype(jnp.bfloat16).astype(jnp.float32)
    s_cols, s_norm = unit_columns(proto_student)
    t_cols, _ = unit_columns(proto_teacher)
    width = min(8192, PROTOS)
    count_blocks = PROTOS // width

    def blocks(matrix):
        return matrix.reshape(BOT, count_blocks, width).transpose(1, 0, 2)
    s_blocks = blocks(s_cols.astype(jnp.bfloat16).astype(jnp.float32))
    t_blocks = blocks(t_cols.astype(jnp.bfloat16).astype(jnp.float32))

    def teacher_exp(tcol):
        return jnp.exp(matmul(teacher_rows, tcol) / TEACHER_TEMP) * live_all[:, None]
    scale_row = live_all
    for turn in range(ROUNDS - 1):

        def step(acc, tcol):
            expo = teacher_exp(tcol)
            col_scale = 1.0 / lax.optimization_barrier(jnp.sum(expo * scale_row[:, None], axis=0))
            return (acc + lax.optimization_barrier(jnp.sum(expo * col_scale[None, :], axis=1)), col_scale)
        row_sum, _ = lax.scan(step, jnp.zeros((total,), jnp.float32), t_blocks)
        scale_row = live_all / (row_sum + 1.0 - live_all)

    def last_step(acc, both):
        tcol, scol = both
        expo = teacher_exp(tcol)
        col_scale = 1.0 / lax.optimization_barrier(jnp.sum(expo * scale_row[:, None], axis=0))
        balanced = expo * col_scale[None, :]
        scores = matmul(student_rows, scol) / STUDENT_TEMP
        acc = (acc[0] + lax.optimization_barrier(jnp.sum(balanced, axis=1)), acc[1] + lax.optimization_barrier(jnp.sum(jnp.exp(scores), axis=1)), acc[2] + lax.optimization_barrier(jnp.sum(balanced * scores, axis=1)))
        return (acc, col_scale)
    zero = jnp.zeros((total,), jnp.float32)
    (row_sum, norm_sum, cross), col_last = lax.scan(last_step, (zero, zero, zero), (t_blocks, s_blocks))
    scale_last = live_all / (row_sum + 1.0 - live_all)
    row_loss = jnp.log(norm_sum) - scale_last * cross
    crop_loss = (lax.optimization_barrier(jnp.sum(member * row_loss.reshape(groups, CAP)[:, :, None], axis=1)) * inverse).reshape(groups * CROPS_DEV)

    def back_step(grad_acc, three):
        tcol, scol, col_scale = three
        expo = teacher_exp(tcol)
        balanced = expo * col_scale[None, :]
        target = balanced * scale_last[:, None]
        scores = matmul(student_rows, scol) / STUDENT_TEMP
        probs = jnp.exp(scores) / norm_sum[:, None]
        grad_score = (weight_all[:, None] * (probs - target) / STUDENT_TEMP).astype(jnp.bfloat16).astype(jnp.float32)
        grad_acc = grad_acc + matmul(grad_score, scol.T)
        parts = jnp.einsum('grb,grk->gbk', student_rows.reshape(groups, CAP, BOT), grad_score.reshape(groups, CAP, width), precision=lax.Precision.HIGHEST)
        return (grad_acc, lax.optimization_barrier(jnp.sum(rounded(parts), axis=0)))
    grad_unit, grad_blocks = lax.scan(back_step, jnp.zeros((total, BOT), jnp.float32), (t_blocks, s_blocks, col_last))
    grad_cols = grad_blocks.transpose(1, 0, 2).reshape(BOT, PROTOS)
    grad_proto = (grad_cols - s_cols * lax.optimization_barrier(jnp.sum(s_cols * grad_cols, axis=0, keepdims=True))) / s_norm
    inner = lax.optimization_barrier(jnp.sum(unit * grad_unit, axis=1, keepdims=True))
    grad_feats = (inv * (grad_unit - unit * inner)).astype(jnp.bfloat16).astype(jnp.float32)
    hidden_wide = hidden.astype(jnp.float32)
    out_parts = jnp.einsum('grh,grb->ghb', hidden_wide.reshape(groups, CAP, HID), grad_feats.reshape(groups, CAP, BOT), precision=lax.Precision.HIGHEST)
    grad_out = lax.optimization_barrier(jnp.sum(rounded(out_parts), axis=0))
    grad_pre = (matmul(grad_feats, w_out.T) * slope).astype(jnp.bfloat16).astype(jnp.float32)
    in_parts = jnp.einsum('grd,grh->gdh', rows.astype(jnp.float32).reshape(groups, CAP, D), grad_pre.reshape(groups, CAP, HID), precision=lax.Precision.HIGHEST)
    grad_in = lax.optimization_barrier(jnp.sum(rounded(in_parts), axis=0))
    grad_rows = (matmul(grad_pre, w_in.T) * live_all[:, None]).reshape(groups, CAP, D)

    def place(idx, values):
        return jnp.zeros((per_dev, D), jnp.float32).at[idx].add(values)
    d_tokens = jax.vmap(place)(index, grad_rows).reshape(groups * per_dev, D).astype(jnp.bfloat16)
    return (d_tokens, grad_in, grad_out, grad_proto, crop_loss)
```

```python
import functools

import jax
import jax.numpy as jnp
from jax import lax
from jax.experimental import pallas as pl
from jax.experimental.pallas import tpu as pltpu
from jax.sharding import PartitionSpec as P

ROUNDS = 3
CAP = 256

TEACHER_TEMP = 0.07
STUDENT_TEMP = 0.1
EPS = 1e-06
GRAD_SCALE = 65536.0
LOG2E = 1.4426950408889634
LANES = 128
BLOCK = 1024
ROW_TILE = 64
MESH = pl.DeviceIdType.MESH
F32 = jnp.float32
BF16 = jnp.bfloat16


def gelu_parts(pre):
    cdf = 0.5 * (1.0 + lax.erf(pre * 0.7071067811865476))
    pdf = jnp.exp(-0.5 * pre * pre) * 0.3989422804014327
    return (pre * cdf, cdf + pre * pdf)


def unit_rows(feats):
    inverse = lax.rsqrt(jnp.sum(feats * feats, axis=1, keepdims=True) + EPS)
    return (feats * inverse, inverse)


def unit_columns(protos):
    wide = protos.astype(F32)
    norms = jnp.sqrt(jnp.sum(wide * wide, axis=0, keepdims=True) + EPS)
    return (wide / norms, norms)


def spread(dense, out_ref):
    for c in range(dense.shape[0]):
        row = jnp.broadcast_to(dense[c : c + 1, :], (LANES, LANES))
        out_ref[c * LANES : (c + 1) * LANES, :] = row.T


def gathered(acc_ref, out_ref, base):
    for c in range(acc_ref.shape[0] // LANES):
        turned = acc_ref[c * LANES : (c + 1) * LANES, :].T
        out_ref[base + c : base + c + 1, :] = jnp.sum(turned, axis=0, keepdims=True)


def fold_lanes(values):
    total = values[:, :LANES]
    for start in range(LANES, values.shape[1], LANES):
        total = total + values[:, start : start + LANES]
    return total


def widen(values, cols):
    return jnp.concatenate([values] * (cols // LANES), axis=1)


def two_terms(row):
    high = row.astype(BF16)
    low = (row - high.astype(F32)).astype(BF16)
    return jnp.concatenate([high, low, jnp.zeros((14, row.shape[1]), BF16)], axis=0)


def flatten(dense):
    return jnp.concatenate([dense[c : c + 1, :] for c in range(dense.shape[0])], axis=1)


def row_scale(live, row_sum):
    return live / (row_sum + 1.0 - live)


def greet(groups, many):
    barrier = pltpu.get_barrier_semaphore()
    for axis in ("dp", "tensor"):
        me = lax.axis_index(axis)
        for step in range(1, groups[axis]):
            peer = lax.rem(me + step, groups[axis])
            pl.semaphore_signal(barrier, inc=1, device_id={axis: peer}, device_id_type=MESH)
    pl.semaphore_wait(barrier, many)


def copies(axis, n, source, landing, send, recv):
    me = lax.axis_index(axis)

    def copy(peer, slot):
        return pltpu.make_async_remote_copy(
            src_ref=source(peer),
            dst_ref=landing(slot),
            send_sem=send(peer),
            recv_sem=recv(slot),
            device_id={axis: peer},
            device_id_type=MESH,
        )

    def start():
        for step in range(1, n):
            copy(lax.rem(me + step, n), me).start()

    def wait():
        for step in range(1, n):
            peer = lax.rem(me + step, n)
            copy(peer, peer).wait()

    return start, wait


def remote(source, target, send, recv, where):
    return pltpu.make_async_remote_copy(
        src_ref=source, dst_ref=target, send_sem=send, recv_sem=recv, device_id=where, device_id_type=MESH
    )


class PairGather:
    def __init__(self, n, own, slot, send, recv):
        self.me = lax.axis_index("dp")
        self.flip = 1 - 2 * lax.rem(self.me, 2)
        self.partner = self.me + self.flip
        self.peers = [lax.rem(self.me + step, n) for step in range(2, n, 2)]
        self.own, self.slot, self.send, self.recv = own, slot, send, recv

    def copy(self, source, slot, sender, peer):
        return remote(source, self.slot(slot), self.send.at[sender], self.recv.at[slot], {"dp": peer})

    def start(self):
        for peer in self.peers + [self.partner]:
            self.copy(self.own, self.me, peer, peer).start()

    def arrive(self, slot):
        self.copy(self.own, slot, slot, slot).wait_recv()

    def forward(self, peer):
        self.copy(self.slot(peer), peer, peer + self.flip, self.partner).start()

    def relay(self):
        for peer in self.peers:
            self.arrive(peer)
            self.forward(peer)

    def finish(self):
        self.arrive(self.partner)
        for peer in self.peers:
            self.arrive(peer + self.flip)

    def drain(self):
        for peer in self.peers:
            self.copy(self.own, self.me, peer, peer).wait_send()
            self.copy(self.slot(peer), peer, peer + self.flip, self.partner).wait_send()
        self.copy(self.own, self.me, self.partner, self.partner).wait_send()


class Exchange:
    def __init__(self, axis, n, source, landing, send, recv):
        self.me = lax.axis_index(axis)
        self.axis, self.source, self.landing, self.send, self.recv = axis, source, landing, send, recv
        self.peers = [lax.rem(self.me + step, n) for step in range(1, n)]

    def copy(self, peer, slot):
        return remote(self.source(peer), self.landing(slot), self.send.at[peer], self.recv.at[slot], {self.axis: peer})

    def start(self):
        for peer in self.peers:
            self.copy(peer, self.me).start()

    def arrive(self):
        for peer in self.peers:
            self.copy(peer, peer).wait_recv()

    def drain(self):
        for peer in self.peers:
            self.copy(peer, self.me).wait_send()


class Total:
    def __init__(self, n, m, value, near, part, far, sems_n, sems_m):
        self.n, self.m = n, m
        self.value, self.near, self.part, self.far = value, near, part, far
        self.first = Exchange("dp", n, lambda peer: value, lambda slot: near.at[slot], *sems_n)
        self.second = Exchange("tensor", m, lambda peer: part, lambda slot: far.at[slot], *sems_m)

    def start(self):
        self.first.start()
        self.near[self.first.me] = self.value[...]

    def turn(self):
        self.first.arrive()
        total = self.near[0]
        for slot in range(1, self.n):
            total = total + self.near[slot]
        self.part[...] = total
        self.second.start()
        self.far[self.second.me] = total

    def finish(self):
        self.second.arrive()
        total = self.far[0]
        for slot in range(1, self.m):
            total = total + self.far[slot]
        return total

    def drain(self):
        self.first.drain()
        self.second.drain()


def plan(groups, rows, columns, width, depth, hidden):
    n, m = groups["dp"], groups["tensor"]
    dense = rows // LANES
    own = CAP // LANES
    part = CAP // m
    block = min(BLOCK, columns)
    vmem = pltpu.VMEM
    shapes = dict(
        expo=vmem((rows, columns), BF16),
        raised=vmem((rows, columns), BF16),
        cols=vmem((width, columns), BF16),
        protos=vmem((width, columns), BF16),
        teach=vmem((n, CAP, width), BF16),
        weight=vmem((n, own, LANES), F32),
        weights=vmem((dense, LANES), F32),
        w_slice=vmem((depth, hidden // m), BF16),
        featp=vmem((CAP, width), F32),
        near_f=vmem((m, part, width), F32),
        feats=vmem((part, width), F32),
        stud=vmem((n, CAP, width), BF16),
        s_prob=vmem((width, rows), BF16),
        s_target=vmem((width, rows), BF16),
        acc_a=vmem((rows, width), F32),
        acc_b=vmem((rows, width), F32),
        g_out=vmem((n, CAP, width), BF16),
        g_own=vmem((CAP, width), F32),
        g_near=vmem((n, CAP, width), BF16),
        g_part=vmem((CAP, width), BF16),
        g_far=vmem((m, part, width), BF16),
        c_out=vmem((n, own, LANES), F32),
        c_near=vmem((n, own, LANES), F32),
        c_part=vmem((own, LANES), F32),
        c_far=vmem((m, own, LANES), F32),
        colacc=vmem((8, columns), F32),
        scale=vmem((8, columns), F32),
        inverse=vmem((8, columns), F32),
        u_terms=vmem((16, rows), BF16),
        acc=vmem((CAP, LANES), F32),
        spread_a=vmem((CAP, LANES), F32),
        spread_b=vmem((CAP, LANES), F32),
        probs=vmem((dense, LANES), F32),
        targets=vmem((dense, LANES), F32),
        last=vmem((2 * dense, LANES), F32),
        stage=vmem((2, width, block), F32),
        pair_send=pltpu.SemaphoreType.DMA((10 + m, n)),
        pair_recv=pltpu.SemaphoreType.DMA((10 + m, n)),
        line_send=pltpu.SemaphoreType.DMA((8, m)),
        line_recv=pltpu.SemaphoreType.DMA((8, m)),
        local=pltpu.SemaphoreType.DMA((8,)),
    )
    for turn in range(ROUNDS):
        size = 2 * dense if turn == ROUNDS - 1 else dense
        shapes[f"value{turn}"] = vmem((size, LANES), F32)
        shapes[f"near{turn}"] = vmem((n, size, LANES), F32)
        shapes[f"part{turn}"] = vmem((size, LANES), F32)
        shapes[f"far{turn}"] = vmem((m, size, LANES), F32)
    return shapes


FOLD_T = LOG2E / TEACHER_TEMP
FOLD_S = LOG2E / STUDENT_TEMP


def balance_kernel(groups, names, *refs):
    n, m = groups["dp"], groups["tensor"]
    teach_own, weight_own, rows_in, w_in, w_out, proto_t, proto_s = refs[:7]
    grad_proto, grad_feats, loss, w_all, wo_all, hidden_all, slope_all = refs[7:14]
    r = dict(zip(names, refs[14:]))
    expo, raised, cols, protos = r["expo"], r["raised"], r["cols"], r["protos"]
    teach, weight, stud, acc, scale = r["teach"], r["weight"], r["stud"], r["acc"], r["scale"]
    acc_a, acc_b, local = r["acc_a"], r["acc_b"], r["local"]
    rows, columns = expo.shape
    width = cols.shape[0]
    dense = rows // LANES
    own = CAP // LANES
    block = r["stage"].shape[2]
    depth = w_in.shape[0]
    slab = r["w_slice"].shape[1]
    part = CAP // m
    me, z = lax.axis_index("dp"), lax.axis_index("tensor")
    half = n // 2
    flip = 1 - 2 * lax.rem(me, 2)

    def pair(k):
        return r["pair_send"].at[k], r["pair_recv"].at[k]

    def line(k):
        return r["line_send"].at[k], r["line_recv"].at[k]

    def place(step):
        return lax.rem(me + 2 * lax.rem(step, half), n) + flip * (step // half)

    def of_block(j):
        return pl.ds(pl.multiple_of(j * block, block), block)

    def of_slot(slot):
        return pl.ds(pl.multiple_of(slot * CAP, CAP), CAP)

    def each(low, high, body):
        def step(j, carry):
            body(j)
            return carry

        lax.fori_loop(low, high, step, 0)

    teach_g = PairGather(n, teach_own, lambda s: teach.at[s], *pair(0))
    weight_g = PairGather(n, weight_own, lambda s: weight.at[s], *pair(1))

    def of_slab(k):
        return pl.ds(pl.multiple_of(k * slab, slab), slab)

    def w_gather(k, index):
        lanes = of_slab(k)
        return PairGather(
            n, w_in.at[:, lanes], lambda s: w_all.at[pl.ds(pl.multiple_of(s * depth, depth), depth), lanes], *pair(index)
        )

    w_now = w_gather(z, 2)
    w_later = [w_gather(lax.rem(z + k, m), 9 + k) for k in range(1, m)]
    tall = w_out.shape[0]
    wo_g = PairGather(n, w_out, lambda s: wo_all.at[pl.ds(pl.multiple_of(s * tall, tall), tall), :], *pair(3))
    stud_g = PairGather(n, stud.at[me], lambda s: stud.at[s], *pair(4))
    totals = [
        Total(n, m, r[f"value{k}"], r[f"near{k}"], r[f"part{k}"], r[f"far{k}"], pair(5 + k), line(2 + k))
        for k in range(ROUNDS)
    ]
    grads = Exchange("dp", n, lambda p: r["g_out"].at[p], lambda s: r["g_near"].at[s], *pair(8))
    crosses = Exchange("dp", n, lambda p: r["c_out"].at[p], lambda s: r["c_near"].at[s], *pair(9))

    def of_part(k):
        return pl.ds(pl.multiple_of(k * part, part), part)

    feat_x = Exchange("tensor", m, lambda p: r["featp"].at[of_part(p), :], lambda s: r["near_f"].at[s], *line(0))
    stud_x = Exchange(
        "tensor", m, lambda p: stud.at[me, of_part(z), :], lambda s: stud.at[me, of_part(s), :], *line(1)
    )
    grad_x = Exchange("tensor", m, lambda p: r["g_part"].at[of_part(p), :], lambda s: r["g_far"].at[s], *line(5))
    cross_x = Exchange("tensor", m, lambda p: r["c_part"], lambda s: r["c_far"].at[s], *line(6))
    back_x = Exchange(
        "tensor", m, lambda p: grad_feats.at[of_part(z), :], lambda s: grad_feats.at[of_part(s), :], *line(7)
    )

    def unit_cols(source, factor, keep):
        def one(j):
            here = of_block(j)
            wide = source[:, here].astype(F32)
            inv = 1.0 / jnp.sqrt(jnp.sum(wide * wide, axis=0, keepdims=True) + EPS)
            if keep is not None:
                keep[:, here] = jnp.broadcast_to(inv, (8, block))
            cols[:, here] = (wide * (inv * factor)).astype(BF16)

        each(0, columns // block, one)

    def teacher_chunk(slot):
        bias = jnp.where(weight[slot] > 0, 0.0, -1e4)
        spread(bias, r["spread_a"])

        def one(j):
            here = of_block(j)
            dots = jnp.dot(teach[slot], cols[:, here], preferred_element_type=F32)
            power = jnp.exp2(dots + widen(r["spread_a"][...], block))
            expo[of_slot(slot), here] = power.astype(BF16)
            total = power[:8, :]
            for start in range(8, CAP, 8):
                total = total + power[start : start + 8, :]
            r["colacc"][:, here] += total

        each(0, columns // block, one)

    def row_pass(store, out):
        def one(k):
            def tile(i):
                here = pl.ds(pl.multiple_of(k * CAP + i * ROW_TILE, ROW_TILE), ROW_TILE)
                total = None
                for start in range(0, columns, LANES):
                    lanes = slice(start, start + LANES)
                    value = expo[here, lanes].astype(F32) * jnp.concatenate([scale[:, lanes]] * (ROW_TILE // 8), axis=0)
                    if store:
                        expo[here, lanes] = value.astype(BF16)
                    total = value if total is None else total + value
                acc[pl.ds(pl.multiple_of(i * ROW_TILE, ROW_TILE), ROW_TILE), :] = total

            each(0, CAP // ROW_TILE, tile)
            gather_rows(out, k * own)

        each(0, n, one)

    def gather_rows(out, base):
        for c in range(own):
            turned = acc[c * LANES : (c + 1) * LANES, :].T
            out[pl.ds(base + c, 1), :] = jnp.sum(turned, axis=0, keepdims=True)

    def column_pass(u):
        r["u_terms"][...] = two_terms(flatten(u))

        def one(j):
            here = of_block(j)
            total = jnp.dot(r["u_terms"][...], expo[:, here], preferred_element_type=F32)
            scale[:, here] = jnp.broadcast_to(1.0 / (total[0:1, :] + total[1:2, :]), (8, block))

        each(0, columns // block, one)

    def student_chunk(slot):
        acc[...] = jnp.zeros_like(acc)

        def one(j):
            here = of_block(j)
            power = jnp.exp2(jnp.dot(stud[slot], cols[:, here], preferred_element_type=F32))
            raised[of_slot(slot), here] = power.astype(BF16)
            acc[...] += fold_lanes(power)

        each(0, columns // block, one)
        gather_rows(r[f"value{ROUNDS - 1}"], dense + slot * own)
        acc_a[of_slot(slot), :] = lax.dot_general(
            raised[of_slot(slot), :], cols[...], (((1,), (1,)), ((), ())), preferred_element_type=F32
        )

    def target_chunk(slot):
        term = lax.dot_general(
            expo[of_slot(slot), :], cols[...], (((1,), (1,)), ((), ())), preferred_element_type=F32
        )
        acc_b[of_slot(slot), :] = term
        acc[...] = fold_lanes(stud[slot].astype(F32) * term)
        gather_rows(r["c_out"].at[slot], 0)

    load_t = pltpu.make_async_copy(proto_t, cols, local.at[0])
    load_s = pltpu.make_async_copy(proto_s, protos, local.at[1])
    load_w = pltpu.make_async_copy(
        w_in, w_all.at[pl.ds(pl.multiple_of(me * depth, depth), depth), :], local.at[2]
    )
    for load in (load_t, load_s, load_w):
        load.start()
    greet(groups, n + m - 2)
    teach_g.start()
    weight_g.start()
    w_now.start()
    wo_g.start()
    teach[me] = teach_own[...]
    weight[me] = weight_own[...]
    wo_all[pl.ds(pl.multiple_of(me * tall, tall), tall), :] = w_out[...]
    r["colacc"][...] = jnp.zeros_like(r["colacc"])
    load_t.wait()
    unit_cols(cols, 1.0, None)
    teacher_chunk(me)
    teach_g.relay()
    weight_g.relay()
    each(1, half, lambda step: teacher_chunk(place(step)))
    w_now.relay()
    wo_g.relay()

    def teacher_late(step):
        teach_g.arrive(place(step))
        weight_g.arrive(place(step))
        teacher_chunk(place(step))

    each(half, n, teacher_late)
    weights = jnp.concatenate([weight[slot] for slot in range(n)], axis=0)
    r["weights"][...] = weights
    live = (weights > 0).astype(F32)
    scale[...] = jnp.broadcast_to(1.0 / jnp.sum(r["colacc"][...], axis=0, keepdims=True), scale.shape)
    row_pass(False, r["value0"])
    totals[0].start()

    load_s.wait()
    unit_cols(protos, FOLD_S, r["inverse"])
    w_now.finish()
    wo_g.finish()
    load_w.wait()
    load_slice = pltpu.make_async_copy(w_all.at[:, of_slab(z)], r["w_slice"], local.at[3])
    load_slice.start()
    load_slice.wait()
    pre = jnp.dot(rows_in[...], r["w_slice"][...], preferred_element_type=F32)
    hidden = gelu_parts(pre)[0].astype(BF16)
    r["featp"][...] = jnp.dot(hidden, wo_all[of_slab(z), :], preferred_element_type=F32)
    feat_x.start()
    totals[0].turn()
    feat_x.arrive()
    feats = r["featp"][of_part(z), :]
    for peer in feat_x.peers:
        feats = feats + r["near_f"][peer]
    r["feats"][...] = feats
    stud[me, of_part(z), :] = unit_rows(feats)[0].astype(BF16)
    stud_x.start()
    total = totals[0].finish()
    stud_x.arrive()
    stud_g.start()
    for gather in w_later:
        gather.start()
    for turn in range(1, ROUNDS - 1):
        column_pass(row_scale(live, total))
        if turn == ROUNDS - 2:
            stud_g.relay()
        row_pass(False, r[f"value{turn}"])
        totals[turn].start()
        if turn < ROUNDS - 2:
            totals[turn].turn()
            total = totals[turn].finish()

    student_chunk(me)
    totals[ROUNDS - 2].turn()
    each(1, half, lambda step: student_chunk(place(step)))

    def student_late(step):
        stud_g.arrive(place(step))
        student_chunk(place(step))

    each(half, n, student_late)
    total = totals[ROUNDS - 2].finish()
    column_pass(row_scale(live, total))
    row_pass(True, r[f"value{ROUNDS - 1}"])
    final = totals[ROUNDS - 1]
    final.start()
    for gather in w_later:
        gather.relay()

    def turn_rows(slot):
        r["s_prob"][:, of_slot(slot)] = stud[slot].astype(F32).T.astype(BF16)

    each(0, n, turn_rows)
    each(0, half, target_chunk)
    final.turn()
    each(half, n, target_chunk)
    crosses.start()
    sums = final.finish()
    r["last"][...] = sums
    live = (r["weights"][...] > 0).astype(F32)
    factor = r["weights"][...] * (1.0 / STUDENT_TEMP)
    u = row_scale(live, sums[:dense])
    r["probs"][...] = factor / sums[dense:]
    r["targets"][...] = factor * u

    def mix(slot):
        spread(r["probs"][pl.ds(slot * own, own), :], r["spread_a"])
        spread(r["targets"][pl.ds(slot * own, own), :], r["spread_b"])
        return acc_a[of_slot(slot), :] * widen(r["spread_a"][...], width) - acc_b[of_slot(slot), :] * widen(
            r["spread_b"][...], width
        )

    def send_mix(step):
        peer = lax.rem(me + step, n)
        r["g_out"][peer] = mix(peer).astype(BF16)
        grads.copy(peer, me).start()

    each(1, n, send_mix)
    r["g_own"][...] = mix(me)

    def scale_rows(slot):
        here = of_slot(slot)
        turned = r["s_prob"][:, here].astype(F32)
        base = pl.ds(slot * own, own)
        r["s_target"][:, here] = (turned * flatten(r["targets"][base, :])).astype(BF16)
        r["s_prob"][:, here] = (turned * flatten(r["probs"][base, :])).astype(BF16)

    each(0, n, scale_rows)

    def out_copy(j):
        return pltpu.make_async_copy(
            r["stage"].at[lax.rem(j, 2)], grad_proto.at[:, of_block(j)], local.at[4 + lax.rem(j, 2)]
        )

    def column_grad(j):
        @pl.when(j >= 2)
        def _():
            out_copy(j - 2).wait()

        here = of_block(j)
        grad = jnp.dot(r["s_prob"][...], raised[:, here], preferred_element_type=F32) - jnp.dot(
            r["s_target"][...], expo[:, here], preferred_element_type=F32
        )
        inv = r["inverse"][0:1, here]
        unit = protos[:, here].astype(F32) * inv
        r["stage"][lax.rem(j, 2)] = (grad - unit * jnp.sum(unit * grad, axis=0, keepdims=True)) * inv
        out_copy(j).start()

    blocks = columns // block
    each(0, blocks, column_grad)

    for gather in w_later:
        gather.finish()

    def load_slab(k):
        return pltpu.make_async_copy(w_all.at[:, of_slab(k)], expo.at[0 : w_all.shape[0], (k % 2) * slab : (k % 2 + 1) * slab], local.at[6 + k % 2])

    load_slab(0).start()
    for k in range(m):
        if k + 1 < m:
            load_slab(k + 1).start()
        load_slab(k).wait()
        pre = jnp.dot(
            rows_in[...], expo[0 : w_all.shape[0], (k % 2) * slab : (k % 2 + 1) * slab], preferred_element_type=F32
        )
        act, slope = gelu_parts(pre)
        hidden_all[:, k * slab : (k + 1) * slab] = act.astype(BF16)
        slope_all[:, k * slab : (k + 1) * slab] = slope

    crosses.arrive()
    cross = r["c_out"][me]
    for peer in crosses.peers:
        cross = cross + r["c_near"][peer]
    r["c_part"][...] = cross
    cross_x.start()
    grads.arrive()
    grad = r["g_own"][...]
    for peer in grads.peers:
        grad = grad + r["g_near"][peer].astype(F32)
    r["g_own"][...] = grad
    r["g_part"][...] = grad.astype(BF16)
    grad_x.start()
    cross_x.arrive()
    for peer in cross_x.peers:
        cross = cross + r["c_far"][peer]
    mine = pl.ds(me * own, own)
    u = row_scale((r["weights"][mine, :] > 0).astype(F32), r["last"][mine, :])
    loss[...] = jnp.log(r["last"][pl.ds(dense + me * own, own), :]) - u * cross * (1.0 / LOG2E)
    grad_x.arrive()
    grad = r["g_own"][of_part(z), :]
    for peer in grad_x.peers:
        grad = grad + r["g_far"][peer].astype(F32)
    unit, inv = unit_rows(r["feats"][...])
    grad = grad * (1.0 / FOLD_S)
    inner = jnp.sum(unit * grad, axis=1, keepdims=True)
    grad_feats[of_part(z), :] = (inv * (grad - unit * inner)).astype(BF16)
    back_x.start()

    for gather in [teach_g, weight_g, w_now, wo_g, stud_g] + w_later:
        gather.drain()
    for one in totals + [grads, crosses, feat_x, stud_x, grad_x, cross_x]:
        one.drain()
    for j in range(max(0, blocks - 2), blocks):
        out_copy(j).wait()
    back_x.arrive()
    back_x.drain()


def balance(groups, teach, weight, rows_in, w_in, w_out, proto_t, proto_s, ident):
    n, m = groups["dp"], groups["tensor"]
    rows, width = n * teach.shape[0], teach.shape[1]
    columns = proto_s.shape[1]
    depth, hidden = n * w_in.shape[0], w_in.shape[1]
    shapes = plan(groups, rows, columns, width, depth, hidden)
    vmem, hbm = pl.BlockSpec(memory_space=pltpu.VMEM), pl.BlockSpec(memory_space=pl.ANY)
    return pl.pallas_call(
        functools.partial(balance_kernel, groups, list(shapes)),
        name="balance",
        in_specs=[vmem, vmem, vmem, hbm, vmem, hbm, hbm],
        out_specs=[hbm, vmem, vmem, hbm, vmem, vmem, vmem],
        out_shape=[
            jax.ShapeDtypeStruct((width, columns), F32),
            jax.ShapeDtypeStruct((CAP, width), BF16),
            jax.ShapeDtypeStruct((CAP // LANES, LANES), F32),
            jax.ShapeDtypeStruct((depth, hidden), BF16),
            jax.ShapeDtypeStruct((hidden, width), BF16),
            jax.ShapeDtypeStruct((CAP, hidden), BF16),
            jax.ShapeDtypeStruct((CAP, hidden), F32),
        ],
        scratch_shapes=list(shapes.values()),
        compiler_params=pltpu.CompilerParams(
            collective_id=ident, has_side_effects=True, vmem_limit_bytes=62 * 1024 * 1024
        ),
    )(teach, weight, rows_in, w_in, w_out, proto_t, proto_s)


def run_jobs(groups, jobs, send_a, recv_a, send_b, recv_b):
    n, m = groups["dp"], groups["tensor"]
    me = lax.axis_index("dp")
    greet(groups, n + m - 2)
    firsts, seconds = [], []
    for k, (source, near, part, far) in enumerate(jobs):
        start, wait = copies(
            "dp", n, source, near, lambda peer, k=k: send_a.at[k, peer], lambda slot, k=k: recv_a.at[k, slot]
        )
        start()
        firsts.append(wait)
    for k, (source, near, part, far) in enumerate(jobs):
        firsts[k]()
        total = source(me)[...].astype(F32)
        for step in range(1, n):
            total = total + near(lax.rem(me + step, n))[...].astype(F32)
        part[...] = total.astype(BF16)
        start, wait = copies(
            "tensor",
            m,
            lambda peer, part=part: part,
            far,
            lambda peer, k=k: send_b.at[k, peer],
            lambda slot, k=k: recv_b.at[k, slot],
        )
        start()
        far(lax.axis_index("tensor"))[...] = part[...]
        seconds.append(wait)
    for wait in seconds:
        wait()


def job_semaphores(groups, jobs):
    n, m = groups["dp"], groups["tensor"]
    return [pltpu.SemaphoreType.DMA((jobs, n))] * 2 + [pltpu.SemaphoreType.DMA((jobs, m))] * 2


def head_kernel(groups, wide, narrow, wide_out, narrow_out, wide_near, narrow_near, wide_part, narrow_part, *semaphores):
    mine = lax.axis_index("tensor")
    jobs = [
        (
            lambda peer: narrow.at[peer, mine],
            lambda slot: narrow_near.at[slot],
            narrow_part,
            lambda slot: narrow_out.at[slot],
        )
    ]
    for k in range(wide.shape[2] // LANES):
        piece = pl.ds(k * LANES, LANES)
        jobs.append(
            (
                lambda peer, piece=piece: wide.at[peer, :, piece],
                lambda slot, piece=piece: wide_near.at[slot, :, piece],
                wide_part.at[:, piece],
                lambda slot, piece=piece: wide_out.at[slot, :, piece],
            )
        )
    run_jobs(groups, jobs, *semaphores)


def head_totals(wide, narrow, groups, ident):
    n, m = groups["dp"], groups["tensor"]
    wide_own, narrow_own = wide.shape[1:], narrow.shape[2:]
    return pl.pallas_call(
        functools.partial(head_kernel, groups),
        name="head_totals",
        in_specs=[pl.BlockSpec(memory_space=pltpu.VMEM)] * 2,
        out_specs=[pl.BlockSpec(memory_space=pltpu.VMEM)] * 2,
        out_shape=[jax.ShapeDtypeStruct((m,) + wide_own, BF16), jax.ShapeDtypeStruct((m,) + narrow_own, BF16)],
        scratch_shapes=[
            pltpu.VMEM((n,) + wide_own, BF16),
            pltpu.VMEM((n,) + narrow_own, BF16),
            pltpu.VMEM(wide_own, BF16),
            pltpu.VMEM(narrow_own, BF16),
        ]
        + job_semaphores(groups, 1 + wide.shape[2] // LANES),
        compiler_params=pltpu.CompilerParams(collective_id=ident, has_side_effects=True),
    )(wide, narrow)


def head_backward(rows, hidden, slope, grad_feats, w_in_all, w_out_all):
    grad_out_part = lax.dot_general(
        hidden, grad_feats, (((0,), (0,)), ((), ())), preferred_element_type=F32
    )
    grad_hidden = lax.dot_general(
        grad_feats, w_out_all, (((1,), (1,)), ((), ())), preferred_element_type=F32
    )
    grad_pre = (grad_hidden * slope).astype(BF16)
    width = grad_pre.shape[1] // lax.axis_size("tensor")
    own_pre = lax.dynamic_slice_in_dim(grad_pre, lax.axis_index("tensor") * width, width, axis=1)
    grad_in_part = lax.dot_general(
        rows, own_pre, (((0,), (0,)), ((), ())), preferred_element_type=F32
    )
    grad_rows = lax.dot_general(
        grad_pre, w_in_all, (((1,), (1,)), ((), ())), preferred_element_type=F32
    )
    return (grad_in_part, grad_out_part, grad_rows)


def selection(masks):
    crops, patches = masks.shape
    size = crops * patches
    flat = masks.reshape(1, size)
    before = (
        lax.broadcasted_iota(jnp.int32, (size, size), 0) < lax.broadcasted_iota(jnp.int32, (size, size), 1)
    ).astype(BF16)
    place = jnp.dot(flat.astype(BF16), before, preferred_element_type=F32).astype(jnp.int32)
    slots = lax.broadcasted_iota(jnp.int32, (CAP, size), 0)
    picked = (place == slots) & (flat > 0)
    dead = slots >= jnp.sum(flat)
    first = lax.broadcasted_iota(jnp.int32, (CAP, size), 1) == 0
    return (picked | (dead & first)).astype(BF16), picked.astype(BF16)


def shards(groups, tokens, teacher_feats, masks, w_in, w_out, proto_student, proto_teacher):
    pick, place = selection(masks)
    counts = jnp.sum(masks, axis=1)
    ends = jnp.sum(
        jnp.where(jnp.arange(counts.shape[0])[:, None] <= jnp.arange(counts.shape[0])[None, :], counts[:, None], 0),
        axis=0,
    )
    slot = jnp.arange(CAP)[:, None]
    member = ((slot >= (ends - counts)[None, :]) & (slot < ends[None, :])).astype(F32)
    inverse = 1.0 / jnp.maximum(counts, 1).astype(F32)
    weight = (GRAD_SCALE * jnp.sum(member * inverse[None, :], axis=1)).astype(BF16)
    teacher_pick = jnp.dot(pick, teacher_feats, preferred_element_type=F32)
    teacher_rows = (unit_rows(teacher_pick)[0] * FOLD_T).astype(BF16)
    rows = jnp.dot(pick, tokens, preferred_element_type=F32).astype(BF16)
    grad_proto, grad_feats, row_loss, w_in_all, w_out_all, hidden, slope = balance(
        groups, teacher_rows, weight.astype(F32).reshape(-1, LANES), rows, w_in, w_out, proto_teacher, proto_student, 0
    )
    crop_loss = jnp.sum(member * row_loss.reshape(CAP)[:, None], axis=0) * inverse
    grad_in_part, grad_out_part, grad_rows = head_backward(rows, hidden, slope, grad_feats, w_in_all, w_out_all)
    n, m = groups["dp"], groups["tensor"]
    wide = grad_in_part.astype(BF16).reshape(n, -1, grad_in_part.shape[1])
    narrow = grad_out_part.astype(BF16).reshape(n, m, -1, grad_out_part.shape[1])
    wide, narrow = head_totals(wide, narrow, groups, 1)
    grad_in = wide.transpose(1, 0, 2).reshape(wide.shape[1], -1).astype(F32)
    grad_out = narrow.reshape(-1, narrow.shape[2]).astype(F32)
    d_tokens = lax.dot_general(
        place, grad_rows.astype(BF16), (((0,), (0,)), ((), ())), preferred_element_type=F32
    ).astype(BF16)
    return (d_tokens, grad_in, grad_out, grad_proto, crop_loss)


def solution(mesh):
    groups = {"dp": mesh.shape["dp"], "tensor": mesh.shape["tensor"]}
    placed = (
        P("dp", None),
        P("dp", None),
        P("dp", None),
        P("dp", None),
        P("dp", None),
        P(None, ("dp", "tensor")),
        P(None, ("dp", "tensor")),
    )
    return jax.shard_map(
        functools.partial(shards, groups),
        mesh=mesh,
        in_specs=placed,
        out_specs=(P("dp", None), P("dp", None), P("dp", None), P(None, ("dp", "tensor")), P("dp")),
        check_vma=False,
    )
```

```python
import functools

import jax
import jax.numpy as jnp
from jax import lax
from jax.experimental import pallas as pl
from jax.experimental.pallas import tpu as pltpu
from jax.sharding import PartitionSpec as P

ROUNDS = 3
CAP = 256

TEACHER_TEMP = 0.07
STUDENT_TEMP = 0.1
EPS = 1e-06
GRAD_SCALE = 65536.0
LOG2E = 1.4426950408889634
LANES = 128
BLOCK = 1024
ROW_TILE = 64
MESH = pl.DeviceIdType.MESH
F32 = jnp.float32
BF16 = jnp.bfloat16


def gelu_parts(pre):
    cdf = 0.5 * (1.0 + lax.erf(pre * 0.7071067811865476))
    pdf = jnp.exp(-0.5 * pre * pre) * 0.3989422804014327
    return (pre * cdf, cdf + pre * pdf)


def unit_rows(feats):
    inverse = lax.rsqrt(jnp.sum(feats * feats, axis=1, keepdims=True) + EPS)
    return (feats * inverse, inverse)


def unit_columns(protos):
    wide = protos.astype(F32)
    norms = jnp.sqrt(jnp.sum(wide * wide, axis=0, keepdims=True) + EPS)
    return (wide / norms, norms)


def spread(dense, out_ref):
    for c in range(dense.shape[0]):
        row = jnp.broadcast_to(dense[c : c + 1, :], (LANES, LANES))
        out_ref[c * LANES : (c + 1) * LANES, :] = row.T


def gathered(acc_ref, out_ref, base):
    for c in range(acc_ref.shape[0] // LANES):
        turned = acc_ref[c * LANES : (c + 1) * LANES, :].T
        out_ref[base + c : base + c + 1, :] = jnp.sum(turned, axis=0, keepdims=True)


def fold_lanes(values):
    total = values[:, :LANES]
    for start in range(LANES, values.shape[1], LANES):
        total = total + values[:, start : start + LANES]
    return total


def widen(values, cols):
    return jnp.concatenate([values] * (cols // LANES), axis=1)


def two_terms(row):
    high = row.astype(BF16)
    low = (row - high.astype(F32)).astype(BF16)
    return jnp.concatenate([high, low, jnp.zeros((14, row.shape[1]), BF16)], axis=0)


def flatten(dense):
    return jnp.concatenate([dense[c : c + 1, :] for c in range(dense.shape[0])], axis=1)


def row_scale(live, row_sum):
    return live / (row_sum + 1.0 - live)


def greet(groups, many):
    barrier = pltpu.get_barrier_semaphore()
    for axis in ("dp", "tensor"):
        me = lax.axis_index(axis)
        for step in range(1, groups[axis]):
            peer = lax.rem(me + step, groups[axis])
            pl.semaphore_signal(barrier, inc=1, device_id={axis: peer}, device_id_type=MESH)
    pl.semaphore_wait(barrier, many)


def remote(source, target, send, recv, where):
    return pltpu.make_async_remote_copy(
        src_ref=source, dst_ref=target, send_sem=send, recv_sem=recv, device_id=where, device_id_type=MESH
    )


class PairGather:
    def __init__(self, n, own, slot, send, recv):
        self.me = lax.axis_index("dp")
        self.flip = 1 - 2 * lax.rem(self.me, 2)
        self.partner = self.me + self.flip
        self.peers = [lax.rem(self.me + step, n) for step in range(2, n, 2)]
        self.own, self.slot, self.send, self.recv = own, slot, send, recv

    def copy(self, source, slot, sender, peer):
        return remote(source, self.slot(slot), self.send.at[sender], self.recv.at[slot], {"dp": peer})

    def start(self):
        for peer in self.peers + [self.partner]:
            self.copy(self.own, self.me, peer, peer).start()

    def arrive(self, slot):
        self.copy(self.own, slot, slot, slot).wait_recv()

    def forward(self, peer):
        self.copy(self.slot(peer), peer, peer + self.flip, self.partner).start()

    def relay(self):
        for peer in self.peers:
            self.arrive(peer)
            self.forward(peer)

    def finish(self):
        self.arrive(self.partner)
        for peer in self.peers:
            self.arrive(peer + self.flip)

    def drain(self):
        for peer in self.peers:
            self.copy(self.own, self.me, peer, peer).wait_send()
            self.copy(self.slot(peer), peer, peer + self.flip, self.partner).wait_send()
        self.copy(self.own, self.me, self.partner, self.partner).wait_send()


class Exchange:
    def __init__(self, axis, n, source, landing, send, recv):
        self.me = lax.axis_index(axis)
        self.axis, self.source, self.landing, self.send, self.recv = axis, source, landing, send, recv
        self.peers = [lax.rem(self.me + step, n) for step in range(1, n)]

    def copy(self, peer, slot):
        return remote(self.source(peer), self.landing(slot), self.send.at[peer], self.recv.at[slot], {self.axis: peer})

    def start(self):
        for peer in self.peers:
            self.copy(peer, self.me).start()

    def arrive(self):
        for peer in self.peers:
            self.copy(peer, peer).wait_recv()

    def drain(self):
        for peer in self.peers:
            self.copy(peer, self.me).wait_send()


class Total:
    def __init__(self, n, m, value, near, part, far, sems_n, sems_m):
        self.n, self.m = n, m
        self.value, self.near, self.part, self.far = value, near, part, far
        self.first = Exchange("dp", n, lambda peer: value, lambda slot: near.at[slot], *sems_n)
        self.second = Exchange("tensor", m, lambda peer: part, lambda slot: far.at[slot], *sems_m)

    def start(self):
        self.first.start()
        self.near[self.first.me] = self.value[...]

    def turn(self):
        self.first.arrive()
        total = self.near[0]
        for slot in range(1, self.n):
            total = total + self.near[slot]
        self.part[...] = total
        self.second.start()
        self.far[self.second.me] = total

    def finish(self):
        self.second.arrive()
        total = self.far[0]
        for slot in range(1, self.m):
            total = total + self.far[slot]
        return total

    def drain(self):
        self.first.drain()
        self.second.drain()


def plan(groups, rows, columns, width, depth, hidden):
    n, m = groups["dp"], groups["tensor"]
    dense = rows // LANES
    own = CAP // LANES
    part = CAP // m
    block = min(BLOCK, columns)
    vmem = pltpu.VMEM
    shapes = dict(
        expo=vmem((rows, columns), BF16),
        raised=vmem((rows, columns), BF16),
        cols=vmem((width, columns), BF16),
        teach=vmem((n, CAP, width), BF16),
        weight=vmem((n, own, LANES), F32),
        weights=vmem((dense, LANES), F32),
        w_all=vmem((depth, hidden), BF16),
        wo_all=vmem((hidden, width), BF16),
        featp=vmem((CAP, width), F32),
        grad_feats=vmem((CAP, width), BF16),
        near_f=vmem((m, part, width), F32),
        feats=vmem((part, width), F32),
        stud=vmem((n, CAP, width), BF16),
        s_prob=vmem((width, rows), BF16),
        s_target=vmem((width, rows), BF16),
        acc_a=vmem((rows, width), BF16),
        acc_b=vmem((rows, width), BF16),
        g_own=vmem((CAP, width), F32),
        g_near=vmem((n, CAP, width), BF16),
        g_part=vmem((CAP, width), BF16),
        g_far=vmem((m, part, width), BF16),
        c_out=vmem((n, own, LANES), F32),
        c_near=vmem((n, own, LANES), F32),
        c_part=vmem((own, LANES), F32),
        c_far=vmem((m, own, LANES), F32),
        colacc=vmem((8, columns), F32),
        scale=vmem((8, columns), F32),
        inverse=vmem((8, columns), F32),
        u_terms=vmem((16, rows), BF16),
        acc=vmem((CAP, LANES), F32),
        spread_a=vmem((CAP, LANES), F32),
        spread_b=vmem((CAP, LANES), F32),
        probs=vmem((dense, LANES), F32),
        targets=vmem((dense, LANES), F32),
        last=vmem((2 * dense, LANES), F32),
        stage=vmem((2, max(width, CAP), block), F32),
        wide_a=vmem((n // 2, depth // n, hidden // m), BF16),
        wide_b=vmem((n // 2, depth // n, hidden // m), BF16),
        narrow_a=vmem((n, hidden // n // m, width), BF16),
        wide_sems=pltpu.SemaphoreType.DMA((4 * (hidden // m // width), n)),
        pair_send=pltpu.SemaphoreType.DMA((11 + m, n)),
        pair_recv=pltpu.SemaphoreType.DMA((11 + m, n)),
        line_send=pltpu.SemaphoreType.DMA((9 + hidden // m // width, m)),
        line_recv=pltpu.SemaphoreType.DMA((9 + hidden // m // width, m)),
        local=pltpu.SemaphoreType.DMA((8,)),
    )
    for turn in range(ROUNDS):
        size = 2 * dense if turn == ROUNDS - 1 else dense
        shapes[f"value{turn}"] = vmem((size, LANES), F32)
        shapes[f"near{turn}"] = vmem((n, size, LANES), F32)
        shapes[f"part{turn}"] = vmem((size, LANES), F32)
        shapes[f"far{turn}"] = vmem((m, size, LANES), F32)
    return shapes


FOLD_T = LOG2E / TEACHER_TEMP
FOLD_S = LOG2E / STUDENT_TEMP


def balance_kernel(groups, names, *refs):
    n, m = groups["dp"], groups["tensor"]
    teach_own, weight_own, rows_in, w_in, w_out, proto_t, proto_s = refs[:7]
    grad_proto, loss, grad_rows, wide_out, narrow_out = refs[7:12]
    r = dict(zip(names, refs[12:]))
    expo, raised, cols, w_all, wo_all, grad_feats = (
        r["expo"], r["raised"], r["cols"], r["w_all"], r["wo_all"], r["grad_feats"]
    )
    teach, weight, stud, acc, scale = r["teach"], r["weight"], r["stud"], r["acc"], r["scale"]
    acc_a, acc_b, local = r["acc_a"], r["acc_b"], r["local"]
    rows, columns = expo.shape
    width = cols.shape[0]
    dense = rows // LANES
    own = CAP // LANES
    block = r["stage"].shape[2]
    depth = w_in.shape[0]
    slab = w_all.shape[1] // m
    part = CAP // m
    me, z = lax.axis_index("dp"), lax.axis_index("tensor")
    half = n // 2
    flip = 1 - 2 * lax.rem(me, 2)

    def pair(k):
        return r["pair_send"].at[k], r["pair_recv"].at[k]

    def line(k):
        return r["line_send"].at[k], r["line_recv"].at[k]

    def place(step):
        return lax.rem(me + 2 * lax.rem(step, half), n) + flip * (step // half)

    def of_block(j):
        return pl.ds(pl.multiple_of(j * block, block), block)

    def of_slot(slot):
        return pl.ds(pl.multiple_of(slot * CAP, CAP), CAP)

    def each(low, high, body):
        def step(j, carry):
            body(j)
            return carry

        lax.fori_loop(low, high, step, 0)

    teach_g = PairGather(n, teach_own, lambda s: teach.at[s], *pair(0))
    weight_g = PairGather(n, weight_own, lambda s: weight.at[s], *pair(1))

    def of_slab(k):
        return pl.ds(pl.multiple_of(k * slab, slab), slab)

    def of_depth(slot):
        return pl.ds(pl.multiple_of(slot * depth, depth), depth)

    def w_gather(k, index):
        lanes = of_slab(k)
        return PairGather(n, w_all.at[of_depth(me), lanes], lambda s: w_all.at[of_depth(s), lanes], *pair(index))

    w_now = w_gather(z, 2)
    w_later = [w_gather(lax.rem(z + k, m), 10 + k) for k in range(1, m)]
    tall = w_out.shape[0]
    wo_g = PairGather(n, w_out, lambda s: wo_all.at[pl.ds(pl.multiple_of(s * tall, tall), tall), :], *pair(3))
    stud_g = PairGather(n, stud.at[me], lambda s: stud.at[s], *pair(4))
    totals = [
        Total(n, m, r[f"value{k}"], r[f"near{k}"], r[f"part{k}"], r[f"far{k}"], pair(5 + k), line(2 + k))
        for k in range(ROUNDS)
    ]
    grads = Exchange("dp", n, lambda p: acc_a.at[of_slot(p), :], lambda s: r["g_near"].at[s], *pair(8))
    crosses = Exchange("dp", n, lambda p: r["c_out"].at[p], lambda s: r["c_near"].at[s], *pair(9))

    def of_part(k):
        return pl.ds(pl.multiple_of(k * part, part), part)

    feat_x = Exchange("tensor", m, lambda p: r["featp"].at[of_part(p), :], lambda s: r["near_f"].at[s], *line(0))
    stud_x = Exchange(
        "tensor", m, lambda p: stud.at[me, of_part(z), :], lambda s: stud.at[me, of_part(s), :], *line(1)
    )
    grad_x = Exchange("tensor", m, lambda p: r["g_part"].at[of_part(p), :], lambda s: r["g_far"].at[s], *line(5))
    cross_x = Exchange("tensor", m, lambda p: r["c_part"], lambda s: r["c_far"].at[s], *line(6))
    back_x = Exchange(
        "tensor", m, lambda p: grad_feats.at[of_part(z), :], lambda s: grad_feats.at[of_part(s), :], *line(7)
    )

    def unit_cols(factor, keep):
        def one(j):
            here = of_block(j)
            wide = cols[:, here].astype(F32)
            inv = 1.0 / jnp.sqrt(jnp.sum(wide * wide, axis=0, keepdims=True) + EPS)
            if keep is not None:
                keep[:, here] = jnp.broadcast_to(inv, (8, block))
            cols[:, here] = (wide * (inv * factor)).astype(BF16)

        each(0, columns // block, one)

    def teacher_chunk(slot):
        bias = jnp.where(weight[slot] > 0, 0.0, -1e4)
        spread(bias, r["spread_a"])

        def one(j):
            here = of_block(j)
            dots = jnp.dot(teach[slot], cols[:, here], preferred_element_type=F32)
            power = jnp.exp2(dots + widen(r["spread_a"][...], block))
            expo[of_slot(slot), here] = power.astype(BF16)
            total = power[:8, :]
            for start in range(8, CAP, 8):
                total = total + power[start : start + 8, :]
            r["colacc"][:, here] += total

        each(0, columns // block, one)

    def row_pass(store, out):
        def one(k):
            def tile(i):
                here = pl.ds(pl.multiple_of(k * CAP + i * ROW_TILE, ROW_TILE), ROW_TILE)
                total = None
                for start in range(0, columns, LANES):
                    lanes = slice(start, start + LANES)
                    value = expo[here, lanes].astype(F32) * jnp.concatenate([scale[:, lanes]] * (ROW_TILE // 8), axis=0)
                    if store:
                        expo[here, lanes] = value.astype(BF16)
                    total = value if total is None else total + value
                acc[pl.ds(pl.multiple_of(i * ROW_TILE, ROW_TILE), ROW_TILE), :] = total

            each(0, CAP // ROW_TILE, tile)
            gather_rows(out, k * own)

        each(0, n, one)

    def gather_rows(out, base):
        for c in range(own):
            turned = acc[c * LANES : (c + 1) * LANES, :].T
            out[pl.ds(base + c, 1), :] = jnp.sum(turned, axis=0, keepdims=True)

    def column_pass(u):
        r["u_terms"][...] = two_terms(flatten(u))

        def one(j):
            here = of_block(j)
            total = jnp.dot(r["u_terms"][...], expo[:, here], preferred_element_type=F32)
            scale[:, here] = jnp.broadcast_to(1.0 / (total[0:1, :] + total[1:2, :]), (8, block))

        each(0, columns // block, one)

    def student_chunk(slot):
        acc[...] = jnp.zeros_like(acc)

        def one(j):
            here = of_block(j)
            for start in range(0, block, width):
                lanes = pl.ds(pl.multiple_of(j * block + start, width), width)
                power = jnp.exp2(jnp.dot(stud[slot], cols[:, lanes], preferred_element_type=F32))
                raised[of_slot(slot), lanes] = power.astype(BF16)
                acc[...] += fold_lanes(power)

        each(0, columns // block, one)
        gather_rows(r[f"value{ROUNDS - 1}"], dense + slot * own)
        acc_a[of_slot(slot), :] = lax.dot_general(
            raised[of_slot(slot), :], cols[...], (((1,), (1,)), ((), ())), preferred_element_type=F32
        ).astype(BF16)

    def target_chunk(slot):
        term = lax.dot_general(
            expo[of_slot(slot), :], cols[...], (((1,), (1,)), ((), ())), preferred_element_type=F32
        )
        acc_b[of_slot(slot), :] = term.astype(BF16)
        acc[...] = fold_lanes(stud[slot].astype(F32) * term)
        gather_rows(r["c_out"].at[slot], 0)

    load_t = pltpu.make_async_copy(proto_t, cols, local.at[0])
    load_s = pltpu.make_async_copy(proto_s, cols, local.at[1])
    load_w = pltpu.make_async_copy(w_in, w_all.at[of_depth(me), :], local.at[2])
    load_w.start()
    load_t.start()
    greet(groups, n + m - 2)
    teach_g.start()
    weight_g.start()
    load_w.wait()
    w_now.start()
    wo_g.start()
    teach[me] = teach_own[...]
    weight[me] = weight_own[...]
    wo_all[pl.ds(pl.multiple_of(me * tall, tall), tall), :] = w_out[...]
    r["colacc"][...] = jnp.zeros_like(r["colacc"])
    load_t.wait()
    unit_cols(1.0, None)
    teacher_chunk(me)
    teach_g.relay()
    weight_g.relay()
    each(1, half, lambda step: teacher_chunk(place(step)))
    w_now.relay()
    wo_g.relay()

    def teacher_late(step):
        teach_g.arrive(place(step))
        weight_g.arrive(place(step))
        teacher_chunk(place(step))

    each(half, n, teacher_late)
    load_s.start()
    weights = jnp.concatenate([weight[slot] for slot in range(n)], axis=0)
    r["weights"][...] = weights
    live = (weights > 0).astype(F32)
    scale[...] = jnp.broadcast_to(1.0 / jnp.sum(r["colacc"][...], axis=0, keepdims=True), scale.shape)
    row_pass(False, r["value0"])
    totals[0].start()

    load_s.wait()
    unit_cols(FOLD_S, r["inverse"])
    w_now.finish()
    wo_g.finish()
    pre = jnp.dot(rows_in[...], w_all[:, of_slab(z)], preferred_element_type=F32)
    hidden = gelu_parts(pre)[0].astype(BF16)
    r["featp"][...] = jnp.dot(hidden, wo_all[of_slab(z), :], preferred_element_type=F32)
    feat_x.start()
    totals[0].turn()
    feat_x.arrive()
    feats = r["featp"][of_part(z), :]
    for peer in feat_x.peers:
        feats = feats + r["near_f"][peer]
    r["feats"][...] = feats
    stud[me, of_part(z), :] = unit_rows(feats)[0].astype(BF16)
    stud_x.start()
    total = totals[0].finish()
    stud_x.arrive()
    stud_g.start()
    for gather in w_later:
        gather.start()
    for turn in range(1, ROUNDS - 1):
        column_pass(row_scale(live, total))
        if turn == ROUNDS - 2:
            stud_g.relay()
        row_pass(False, r[f"value{turn}"])
        totals[turn].start()
        if turn < ROUNDS - 2:
            totals[turn].turn()
            total = totals[turn].finish()

    student_chunk(me)
    totals[ROUNDS - 2].turn()
    each(1, half, lambda step: student_chunk(place(step)))

    def student_late(step):
        stud_g.arrive(place(step))
        student_chunk(place(step))

    each(half, n, student_late)
    total = totals[ROUNDS - 2].finish()
    column_pass(row_scale(live, total))
    row_pass(True, r[f"value{ROUNDS - 1}"])
    final = totals[ROUNDS - 1]
    final.start()
    for gather in w_later:
        gather.relay()

    def turn_rows(slot):
        r["s_prob"][:, of_slot(slot)] = stud[slot].astype(F32).T.astype(BF16)

    each(0, n, turn_rows)
    each(0, half, target_chunk)
    final.turn()
    each(half, n, target_chunk)
    load_s.start()
    crosses.start()
    sums = final.finish()
    r["last"][...] = sums
    live = (r["weights"][...] > 0).astype(F32)
    factor = r["weights"][...] * (1.0 / STUDENT_TEMP)
    u = row_scale(live, sums[:dense])
    r["probs"][...] = factor / sums[dense:]
    r["targets"][...] = factor * u

    def mix(slot):
        spread(r["probs"][pl.ds(slot * own, own), :], r["spread_a"])
        spread(r["targets"][pl.ds(slot * own, own), :], r["spread_b"])
        return acc_a[of_slot(slot), :].astype(F32) * widen(r["spread_a"][...], width) - acc_b[
            of_slot(slot), :
        ].astype(F32) * widen(r["spread_b"][...], width)

    def send_mix(step):
        peer = lax.rem(me + step, n)
        acc_a[of_slot(peer), :] = mix(peer).astype(BF16)
        grads.copy(peer, me).start()

    each(1, n, send_mix)
    r["g_own"][...] = mix(me)

    def scale_rows(slot):
        here = of_slot(slot)
        turned = r["s_prob"][:, here].astype(F32)
        base = pl.ds(slot * own, own)
        r["s_target"][:, here] = (turned * flatten(r["targets"][base, :])).astype(BF16)
        r["s_prob"][:, here] = (turned * flatten(r["probs"][base, :])).astype(BF16)

    each(0, n, scale_rows)

    def out_copy(j):
        return pltpu.make_async_copy(
            r["stage"].at[lax.rem(j, 2)], grad_proto.at[:, of_block(j)], local.at[4 + lax.rem(j, 2)]
        )

    def column_grad(j):
        @pl.when(j >= 2)
        def _():
            out_copy(j - 2).wait()

        here = of_block(j)
        grad = jnp.dot(r["s_prob"][...], raised[:, here], preferred_element_type=F32) - jnp.dot(
            r["s_target"][...], expo[:, here], preferred_element_type=F32
        )
        inv = r["inverse"][0:1, here]
        unit = cols[:, here].astype(F32) * inv
        r["stage"][lax.rem(j, 2)] = (grad - unit * jnp.sum(unit * grad, axis=0, keepdims=True)) * inv
        out_copy(j).start()

    blocks = columns // block
    load_s.wait()
    each(0, blocks, column_grad)

    for gather in w_later:
        gather.finish()

    for j in range(max(0, blocks - 2), blocks):
        out_copy(j).wait()
    per = block // width
    hidden_blocks = w_all.shape[1] // width
    whole_depth = w_all.shape[0]
    pieces = slab // width

    def of_width(k):
        return pl.ds(pl.multiple_of(k * width, width), width)

    def hidden_block(b):
        pre = jnp.dot(rows_in[...], w_all[:, of_width(b)], preferred_element_type=F32)
        act, slope = gelu_parts(pre)
        raised[of_slot(b), 0:width] = act.astype(BF16)
        r["stage"][b // per, 0:CAP, of_width(lax.rem(b, per))] = slope

    each(0, hidden_blocks, hidden_block)

    def turn_tokens(k):
        expo[of_width(k), width : width + CAP] = rows_in[:, of_width(k)].astype(F32).T.astype(BF16)

    each(0, whole_depth // width, turn_tokens)

    crosses.arrive()
    cross = r["c_out"][me]
    for peer in crosses.peers:
        cross = cross + r["c_near"][peer]
    r["c_part"][...] = cross
    cross_x.start()
    grads.arrive()
    grad = r["g_own"][...]
    for peer in grads.peers:
        grad = grad + r["g_near"][peer].astype(F32)
    r["g_own"][...] = grad
    r["g_part"][...] = grad.astype(BF16)
    grad_x.start()
    cross_x.arrive()
    for peer in cross_x.peers:
        cross = cross + r["c_far"][peer]
    mine = pl.ds(me * own, own)
    u = row_scale((r["weights"][mine, :] > 0).astype(F32), r["last"][mine, :])
    loss[...] = jnp.log(r["last"][pl.ds(dense + me * own, own), :]) - u * cross * (1.0 / LOG2E)
    grad_x.arrive()
    grad = r["g_own"][of_part(z), :]
    for peer in grad_x.peers:
        grad = grad + r["g_far"][peer].astype(F32)
    unit, inv = unit_rows(r["feats"][...])
    grad = grad * (1.0 / FOLD_S)
    inner = jnp.sum(unit * grad, axis=1, keepdims=True)
    grad_feats[of_part(z), :] = (inv * (grad - unit * inner)).astype(BF16)
    back_x.start()

    for gather in [teach_g, weight_g, w_now, wo_g, stud_g] + w_later:
        gather.drain()
    for one in totals + [grads, crosses, feat_x, stud_x, grad_x, cross_x]:
        one.drain()
    back_x.arrive()
    back_x.drain()

    lane_in, lane_mid = width + CAP, 2 * width

    def back_block(b):
        grad_hidden = lax.dot_general(
            grad_feats[...], wo_all[of_width(b), :], (((1,), (1,)), ((), ())), preferred_element_type=F32
        )
        expo[of_slot(b), 0:width] = (grad_hidden * r["stage"][b // per, 0:CAP, of_width(lax.rem(b, per))]).astype(BF16)

    def out_block(b):
        raised[of_width(b), width : 2 * width] = lax.dot_general(
            raised[of_slot(b), 0:width], grad_feats[...], (((0,), (0,)), ((), ())), preferred_element_type=F32
        ).astype(BF16)

    side = lax.rem(me, 2)
    team = me // 2
    teams = [lax.rem(team + step, half) for step in range(1, half)]

    def pair_copy(q, h):
        lanes = slice(h * width, (h + 1) * width)
        return remote(
            expo.at[of_depth(2 * q + 1 - side), lane_in + h * width : lane_in + (h + 1) * width],
            r["wide_a"].at[q, :, lanes],
            r["wide_sems"].at[h, q],
            r["wide_sems"].at[pieces + h, q],
            {"dp": me + flip},
        )

    def team_copy(q, slot, h):
        lanes = slice(h * width, (h + 1) * width)
        return remote(
            raised.at[of_depth(q), lane_mid + h * width : lane_mid + (h + 1) * width],
            r["wide_b"].at[slot, :, lanes],
            r["wide_sems"].at[2 * pieces + h, q],
            r["wide_sems"].at[3 * pieces + h, slot],
            {"dp": 2 * q + side},
        )

    def own_term(q, h):
        lanes = slice(h * width, (h + 1) * width)
        mine = expo[of_depth(2 * q + side), lane_in + h * width : lane_in + (h + 1) * width]
        return mine.astype(F32) + r["wide_a"][q, :, lanes].astype(F32)

    def wide_lanes(s, h):
        return pl.ds(pl.multiple_of(s * slab + h * width, width), width)

    def wide_exchange(h):
        return Exchange(
            "tensor",
            m,
            lambda p: wide_out.at[:, wide_lanes(z, h)],
            lambda s: wide_out.at[:, wide_lanes(s, h)],
            *line(9 + h),
        )

    wide_x = [wide_exchange(h) for h in range(pieces)]
    sub = tall // m
    narrow_n = Exchange(
        "dp",
        n,
        lambda p: raised.at[pl.ds(pl.multiple_of(p * tall + z * sub, sub), sub), width : 2 * width],
        lambda s: r["narrow_a"].at[s],
        *pair(10),
    )

    def of_sub(s):
        return pl.ds(pl.multiple_of(s * sub, sub), sub)

    narrow_x = Exchange("tensor", m, lambda p: narrow_out.at[of_sub(z), :], lambda s: narrow_out.at[of_sub(s), :], *line(8))

    for h in range(pieces):
        mine = z * pieces + h
        back_block(mine)

        def in_block(p):
            expo[of_depth(p), lane_in + h * width : lane_in + (h + 1) * width] = jnp.dot(
                expo[of_depth(p), width : width + CAP], expo[of_slot(mine), 0:width], preferred_element_type=F32
            ).astype(BF16)

        for q in teams + [team]:
            in_block(2 * q + 1 - side)
            pair_copy(q, h).start()
        for q in teams + [team]:
            in_block(2 * q + side)
    each(0, hidden_blocks, out_block)
    narrow_n.start()
    for h in range(pieces):
        for q in teams:
            pair_copy(q, h).wait_recv()
            raised[of_depth(q), lane_mid + h * width : lane_mid + (h + 1) * width] = own_term(q, h).astype(BF16)
            team_copy(q, team, h).start()
        pair_copy(team, h).wait_recv()
    each(0, m * pieces, back_block)
    for h in range(pieces):
        for q in teams:
            team_copy(q, q, h).wait_recv()
        total = own_term(team, h)
        for q in teams:
            total = total + r["wide_b"][q, :, h * width : (h + 1) * width].astype(F32)
        wide_out[:, wide_lanes(z, h)] = total.astype(BF16)
        wide_x[h].start()
    narrow_n.arrive()
    total = raised[pl.ds(pl.multiple_of(me * tall + z * sub, sub), sub), width : 2 * width].astype(F32)
    for peer in narrow_n.peers:
        total = total + r["narrow_a"][peer].astype(F32)
    narrow_out[of_sub(z), :] = total.astype(BF16)
    narrow_x.start()

    def token_block(k):
        total = None
        for b in range(hidden_blocks):
            term = lax.dot_general(
                expo[b * CAP : (b + 1) * CAP, 0:width],
                w_all[of_width(k), b * width : (b + 1) * width],
                (((1,), (1,)), ((), ())),
                preferred_element_type=F32,
            )
            total = term if total is None else total + term
        grad_rows[:, of_width(k)] = total.astype(BF16)

    each(0, whole_depth // width, token_block)
    narrow_x.arrive()
    for one in wide_x:
        one.arrive()
    for one in wide_x + [narrow_n, narrow_x]:
        one.drain()
    for h in range(pieces):
        for q in teams:
            pair_copy(q, h).wait_send()
            team_copy(q, team, h).wait_send()
        pair_copy(team, h).wait_send()


def balance(groups, teach, weight, rows_in, w_in, w_out, proto_t, proto_s, ident):
    n, m = groups["dp"], groups["tensor"]
    rows, width = n * teach.shape[0], teach.shape[1]
    columns = proto_s.shape[1]
    depth, hidden = n * w_in.shape[0], w_in.shape[1]
    shapes = plan(groups, rows, columns, width, depth, hidden)
    vmem, hbm = pl.BlockSpec(memory_space=pltpu.VMEM), pl.BlockSpec(memory_space=pl.ANY)
    return pl.pallas_call(
        functools.partial(balance_kernel, groups, list(shapes)),
        name="balance",
        in_specs=[vmem, vmem, vmem, hbm, vmem, hbm, hbm],
        out_specs=[hbm, vmem, vmem, vmem, vmem],
        out_shape=[
            jax.ShapeDtypeStruct((width, columns), F32),
            jax.ShapeDtypeStruct((CAP // LANES, LANES), F32),
            jax.ShapeDtypeStruct((CAP, depth), BF16),
            jax.ShapeDtypeStruct((depth // n, hidden), BF16),
            jax.ShapeDtypeStruct((hidden // n, width), BF16),
        ],
        scratch_shapes=list(shapes.values()),
        compiler_params=pltpu.CompilerParams(
            collective_id=ident, has_side_effects=True, vmem_limit_bytes=62 * 1024 * 1024
        ),
    )(teach, weight, rows_in, w_in, w_out, proto_t, proto_s)


def selection(masks):
    crops, patches = masks.shape
    size = crops * patches
    flat = masks.reshape(1, size)
    before = (
        lax.broadcasted_iota(jnp.int32, (size, size), 0) < lax.broadcasted_iota(jnp.int32, (size, size), 1)
    ).astype(BF16)
    place = jnp.dot(flat.astype(BF16), before, preferred_element_type=F32).astype(jnp.int32)
    slots = lax.broadcasted_iota(jnp.int32, (CAP, size), 0)
    picked = (place == slots) & (flat > 0)
    dead = slots >= jnp.sum(flat)
    first = lax.broadcasted_iota(jnp.int32, (CAP, size), 1) == 0
    return (picked | (dead & first)).astype(BF16), picked.astype(BF16)


def shards(groups, tokens, teacher_feats, masks, w_in, w_out, proto_student, proto_teacher):
    pick, place = selection(masks)
    counts = jnp.sum(masks, axis=1)
    ends = jnp.sum(
        jnp.where(jnp.arange(counts.shape[0])[:, None] <= jnp.arange(counts.shape[0])[None, :], counts[:, None], 0),
        axis=0,
    )
    slot = jnp.arange(CAP)[:, None]
    member = ((slot >= (ends - counts)[None, :]) & (slot < ends[None, :])).astype(F32)
    inverse = 1.0 / jnp.maximum(counts, 1).astype(F32)
    weight = (GRAD_SCALE * jnp.sum(member * inverse[None, :], axis=1)).astype(BF16)
    teacher_pick = jnp.dot(pick, teacher_feats, preferred_element_type=F32)
    teacher_rows = (unit_rows(teacher_pick)[0] * FOLD_T).astype(BF16)
    rows = jnp.dot(pick, tokens, preferred_element_type=F32).astype(BF16)
    grad_proto, row_loss, grad_rows, wide, narrow = balance(
        groups, teacher_rows, weight.astype(F32).reshape(-1, LANES), rows, w_in, w_out, proto_teacher, proto_student, 0
    )
    crop_loss = jnp.sum(member * row_loss.reshape(CAP)[:, None], axis=0) * inverse
    grad_in = wide.astype(F32)
    grad_out = narrow.astype(F32)
    d_tokens = lax.dot_general(
        place, grad_rows, (((0,), (0,)), ((), ())), preferred_element_type=F32
    ).astype(BF16)
    return (d_tokens, grad_in, grad_out, grad_proto, crop_loss)


def solution(mesh):
    groups = {"dp": mesh.shape["dp"], "tensor": mesh.shape["tensor"]}
    placed = (
        P("dp", None),
        P("dp", None),
        P("dp", None),
        P("dp", None),
        P("dp", None),
        P(None, ("dp", "tensor")),
        P(None, ("dp", "tensor")),
    )
    return jax.shard_map(
        functools.partial(shards, groups),
        mesh=mesh,
        in_specs=placed,
        out_specs=(P("dp", None), P("dp", None), P("dp", None), P(None, ("dp", "tensor")), P("dp")),
        check_vma=False,
    )
```

```python
import functools

import jax
import jax.numpy as jnp
from jax import lax
from jax.experimental import pallas as pl
from jax.experimental.pallas import tpu as pltpu
from jax.sharding import PartitionSpec as P

ROUNDS = 3
CAP = 256

TEACHER_TEMP = 0.07
STUDENT_TEMP = 0.1
EPS = 1e-06
GRAD_SCALE = 65536.0
LOG2E = 1.4426950408889634
LANES = 128
BLOCK = 1024
ROW_TILE = 64
MESH = pl.DeviceIdType.MESH
F32 = jnp.float32
BF16 = jnp.bfloat16


def gelu_parts(pre):
    cdf = 0.5 * (1.0 + lax.erf(pre * 0.7071067811865476))
    pdf = jnp.exp(-0.5 * pre * pre) * 0.3989422804014327
    return (pre * cdf, cdf + pre * pdf)


def unit_rows(feats):
    inverse = lax.rsqrt(jnp.sum(feats * feats, axis=1, keepdims=True) + EPS)
    return (feats * inverse, inverse)


def unit_columns(protos):
    wide = protos.astype(F32)
    norms = jnp.sqrt(jnp.sum(wide * wide, axis=0, keepdims=True) + EPS)
    return (wide / norms, norms)


def spread(dense, out_ref):
    for c in range(dense.shape[0]):
        row = jnp.broadcast_to(dense[c : c + 1, :], (LANES, LANES))
        out_ref[c * LANES : (c + 1) * LANES, :] = row.T


def gathered(acc_ref, out_ref, base):
    for c in range(acc_ref.shape[0] // LANES):
        turned = acc_ref[c * LANES : (c + 1) * LANES, :].T
        out_ref[base + c : base + c + 1, :] = jnp.sum(turned, axis=0, keepdims=True)


def fold_lanes(values):
    total = values[:, :LANES]
    for start in range(LANES, values.shape[1], LANES):
        total = total + values[:, start : start + LANES]
    return total


def widen(values, cols):
    return jnp.concatenate([values] * (cols // LANES), axis=1)


def two_terms(row):
    high = row.astype(BF16)
    low = (row - high.astype(F32)).astype(BF16)
    return jnp.concatenate([high, low, jnp.zeros((14, row.shape[1]), BF16)], axis=0)


def flatten(dense):
    return jnp.concatenate([dense[c : c + 1, :] for c in range(dense.shape[0])], axis=1)


def row_scale(live, row_sum):
    return live / (row_sum + 1.0 - live)


def greet(groups, many):
    barrier = pltpu.get_barrier_semaphore()
    for axis in ("dp", "tensor"):
        me = lax.axis_index(axis)
        for step in range(1, groups[axis]):
            peer = lax.rem(me + step, groups[axis])
            pl.semaphore_signal(barrier, inc=1, device_id={axis: peer}, device_id_type=MESH)
    pl.semaphore_wait(barrier, many)


def remote(source, target, send, recv, where):
    return pltpu.make_async_remote_copy(
        src_ref=source, dst_ref=target, send_sem=send, recv_sem=recv, device_id=where, device_id_type=MESH
    )


class PairGather:
    def __init__(self, n, own, slot, send, recv):
        self.me = lax.axis_index("dp")
        self.flip = 1 - 2 * lax.rem(self.me, 2)
        self.partner = self.me + self.flip
        self.peers = [lax.rem(self.me + step, n) for step in range(2, n, 2)]
        self.own, self.slot, self.send, self.recv = own, slot, send, recv

    def copy(self, source, slot, sender, peer):
        return remote(source, self.slot(slot), self.send.at[sender], self.recv.at[slot], {"dp": peer})

    def start(self):
        for peer in self.peers + [self.partner]:
            self.copy(self.own, self.me, peer, peer).start()

    def arrive(self, slot):
        self.copy(self.own, slot, slot, slot).wait_recv()

    def forward(self, peer):
        self.copy(self.slot(peer), peer, peer + self.flip, self.partner).start()

    def relay(self):
        for peer in self.peers:
            self.arrive(peer)
            self.forward(peer)

    def finish(self):
        self.arrive(self.partner)
        for peer in self.peers:
            self.arrive(peer + self.flip)

    def drain(self):
        for peer in self.peers:
            self.copy(self.own, self.me, peer, peer).wait_send()
            self.copy(self.slot(peer), peer, peer + self.flip, self.partner).wait_send()
        self.copy(self.own, self.me, self.partner, self.partner).wait_send()


class Exchange:
    def __init__(self, axis, n, source, landing, send, recv):
        self.me = lax.axis_index(axis)
        self.axis, self.source, self.landing, self.send, self.recv = axis, source, landing, send, recv
        self.peers = [lax.rem(self.me + step, n) for step in range(1, n)]

    def copy(self, peer, slot):
        return remote(self.source(peer), self.landing(slot), self.send.at[peer], self.recv.at[slot], {self.axis: peer})

    def start(self):
        for peer in self.peers:
            self.copy(peer, self.me).start()

    def arrive(self):
        for peer in self.peers:
            self.copy(peer, peer).wait_recv()

    def drain(self):
        for peer in self.peers:
            self.copy(peer, self.me).wait_send()


class Chain:
    def __init__(self, axis, n, block, send, recv):
        self.me = lax.axis_index(axis)
        self.axis, self.n, self.block, self.send, self.recv = axis, n, block, send, recv

    def copy(self, step, way):
        index = lax.rem(self.me - way * step + self.n, self.n)
        peer = lax.rem(self.me + way + self.n, self.n)
        ref = self.block(index)
        send = self.send.at[self.n if step == 0 and way < 0 else index]
        return remote(ref, ref, send, self.recv.at[index], {self.axis: peer})

    def held(self, step, way):
        index = self.me - way * step
        return (index >= 0) & (index < self.n)

    def each_way(self, step, arrive, send, done):
        for way in (1, -1):
            held = self.held(step, way)
            beyond = self.me + way
            onward = held & (beyond >= 0) & (beyond < self.n)
            if arrive:
                pl.when(held)(lambda way=way: self.copy(step, way).wait_recv())
            if send:
                pl.when(onward)(lambda way=way: self.copy(step, way).start())
            if done:
                pl.when(onward)(lambda way=way: self.copy(step, way).wait_send())

    def start(self):
        self.each_way(0, False, True, False)

    def relay(self, step):
        self.each_way(step, True, step < self.n - 1, False)

    def drain(self):
        for step in range(self.n - 1):
            self.each_way(step, False, False, True)


class Total:
    def __init__(self, n, m, value, near, part, far, sems_n, sems_m):
        self.n, self.m = n, m
        self.value, self.near, self.part, self.far = value, near, part, far
        self.first = Exchange("dp", n, lambda peer: value, lambda slot: near.at[slot], *sems_n)
        self.second = Exchange("tensor", m, lambda peer: part, lambda slot: far.at[slot], *sems_m)

    def start(self):
        self.first.start()
        self.near[self.first.me] = self.value[...]

    def turn(self):
        self.first.arrive()
        total = self.near[0]
        for slot in range(1, self.n):
            total = total + self.near[slot]
        self.part[...] = total
        self.second.start()
        self.far[self.second.me] = total

    def finish(self):
        self.second.arrive()
        total = self.far[0]
        for slot in range(1, self.m):
            total = total + self.far[slot]
        return total

    def drain(self):
        self.first.drain()
        self.second.drain()


def plan(groups, rows, columns, width, depth, hidden):
    n, m = groups["dp"], groups["tensor"]
    dense = rows // LANES
    own = CAP // LANES
    part = CAP // m
    block = min(BLOCK, columns)
    vmem = pltpu.VMEM
    shapes = dict(
        expo=vmem((rows, columns), BF16),
        raised=vmem((rows, columns), BF16),
        cols=vmem((width, columns), BF16),
        teach=vmem((n, CAP, width), BF16),
        weight=vmem((n, own, LANES), F32),
        weights=vmem((dense, LANES), F32),
        w_all=vmem((depth, hidden), BF16),
        wo_all=vmem((hidden, width), BF16),
        featp=vmem((CAP, width), F32),
        grad_feats=vmem((CAP, width), BF16),
        near_f=vmem((m, part, width), F32),
        feats=vmem((part, width), F32),
        stud=vmem((n, CAP, width), BF16),
        s_prob=vmem((width, rows), BF16),
        s_target=vmem((width, rows), BF16),
        acc_a=vmem((rows, width), BF16),
        acc_b=vmem((rows, width), BF16),
        g_own=vmem((CAP, width), F32),
        g_near=vmem((n, CAP, width), BF16),
        g_part=vmem((CAP, width), BF16),
        g_far=vmem((m, part, width), BF16),
        c_out=vmem((n, own, LANES), F32),
        c_near=vmem((n, own, LANES), F32),
        c_part=vmem((own, LANES), F32),
        c_far=vmem((m, own, LANES), F32),
        colacc=vmem((8, columns), F32),
        scale=vmem((8, columns), F32),
        inverse=vmem((8, columns), F32),
        u_terms=vmem((16, rows), BF16),
        acc=vmem((CAP, LANES), F32),
        spread_a=vmem((CAP, LANES), F32),
        spread_b=vmem((CAP, LANES), F32),
        probs=vmem((dense, LANES), F32),
        targets=vmem((dense, LANES), F32),
        last=vmem((2 * dense, LANES), F32),
        stage=vmem((2, max(width, CAP), block), F32),
        wide_a=vmem((n // 2, depth // n, hidden // m), BF16),
        wide_b=vmem((n // 2, depth // n, hidden // m), BF16),
        narrow_a=vmem((n, hidden // n // m, width), BF16),
        wide_sems=pltpu.SemaphoreType.DMA((4 * (hidden // m // width), n)),
        pair_send=pltpu.SemaphoreType.DMA((11 + m, n)),
        pair_recv=pltpu.SemaphoreType.DMA((11 + m, n)),
        line_send=pltpu.SemaphoreType.DMA((9 + hidden // m // width, m + 1)),
        line_recv=pltpu.SemaphoreType.DMA((9 + hidden // m // width, m + 1)),
        local=pltpu.SemaphoreType.DMA((8,)),
    )
    for turn in range(ROUNDS):
        size = 2 * dense if turn == ROUNDS - 1 else dense
        shapes[f"value{turn}"] = vmem((size, LANES), F32)
        shapes[f"near{turn}"] = vmem((n, size, LANES), F32)
        shapes[f"part{turn}"] = vmem((size, LANES), F32)
        shapes[f"far{turn}"] = vmem((m, size, LANES), F32)
    return shapes


FOLD_T = LOG2E / TEACHER_TEMP
FOLD_S = LOG2E / STUDENT_TEMP


def balance_kernel(groups, names, *refs):
    n, m = groups["dp"], groups["tensor"]
    teach_own, weight_own, rows_in, w_in, w_out, proto_t, proto_s = refs[:7]
    grad_proto, loss, grad_rows, wide_out, narrow_out = refs[7:12]
    r = dict(zip(names, refs[12:]))
    expo, raised, cols, w_all, wo_all, grad_feats = (
        r["expo"], r["raised"], r["cols"], r["w_all"], r["wo_all"], r["grad_feats"]
    )
    teach, weight, stud, acc, scale = r["teach"], r["weight"], r["stud"], r["acc"], r["scale"]
    acc_a, acc_b, local = r["acc_a"], r["acc_b"], r["local"]
    rows, columns = expo.shape
    width = cols.shape[0]
    dense = rows // LANES
    own = CAP // LANES
    block = r["stage"].shape[2]
    depth = w_in.shape[0]
    slab = w_all.shape[1] // m
    part = CAP // m
    me, z = lax.axis_index("dp"), lax.axis_index("tensor")
    half = n // 2
    flip = 1 - 2 * lax.rem(me, 2)

    def pair(k):
        return r["pair_send"].at[k], r["pair_recv"].at[k]

    def line(k):
        return r["line_send"].at[k], r["line_recv"].at[k]

    def place(step):
        return lax.rem(me + 2 * lax.rem(step, half), n) + flip * (step // half)

    def of_block(j):
        if isinstance(j, int):
            return slice(j * block, (j + 1) * block)
        return pl.ds(pl.multiple_of(j * block, block), block)

    def of_slot(slot):
        return pl.ds(pl.multiple_of(slot * CAP, CAP), CAP)

    def each(low, high, body):
        def step(j, carry):
            body(j)
            return carry

        lax.fori_loop(low, high, step, 0)

    teach_g = PairGather(n, teach_own, lambda s: teach.at[s], *pair(0))
    weight_g = PairGather(n, weight_own, lambda s: weight.at[s], *pair(1))

    def of_slab(k):
        return pl.ds(pl.multiple_of(k * slab, slab), slab)

    def of_depth(slot):
        return pl.ds(pl.multiple_of(slot * depth, depth), depth)

    def w_gather(k, index):
        lanes = of_slab(k)
        return PairGather(n, w_all.at[of_depth(me), lanes], lambda s: w_all.at[of_depth(s), lanes], *pair(index))

    w_now = w_gather(z, 2)
    w_later = [w_gather(lax.rem(z + k, m), 10 + k) for k in range(1, m)]
    tall = w_out.shape[0]
    wo_g = PairGather(n, w_out, lambda s: wo_all.at[pl.ds(pl.multiple_of(s * tall, tall), tall), :], *pair(3))
    stud_g = PairGather(n, stud.at[me], lambda s: stud.at[s], *pair(4))
    totals = [
        Total(n, m, r[f"value{k}"], r[f"near{k}"], r[f"part{k}"], r[f"far{k}"], pair(5 + k), line(2 + k))
        for k in range(ROUNDS)
    ]
    grads = Exchange("dp", n, lambda p: acc_a.at[of_slot(p), :], lambda s: r["g_near"].at[s], *pair(8))
    crosses = Exchange("dp", n, lambda p: r["c_out"].at[p], lambda s: r["c_near"].at[s], *pair(9))

    def of_part(k):
        return pl.ds(pl.multiple_of(k * part, part), part)

    feat_x = Exchange("tensor", m, lambda p: r["featp"].at[of_part(p), :], lambda s: r["near_f"].at[s], *line(0))
    stud_x = Exchange(
        "tensor", m, lambda p: stud.at[me, of_part(z), :], lambda s: stud.at[me, of_part(s), :], *line(1)
    )
    grad_x = Exchange("tensor", m, lambda p: r["g_part"].at[of_part(p), :], lambda s: r["g_far"].at[s], *line(5))
    cross_x = Exchange("tensor", m, lambda p: r["c_part"], lambda s: r["c_far"].at[s], *line(6))
    back_x = Exchange(
        "tensor", m, lambda p: grad_feats.at[of_part(z), :], lambda s: grad_feats.at[of_part(s), :], *line(7)
    )

    def unit_cols(factor, keep):
        def one(j):
            here = of_block(j)
            wide = cols[:, here].astype(F32)
            inv = 1.0 / jnp.sqrt(jnp.sum(wide * wide, axis=0, keepdims=True) + EPS)
            if keep is not None:
                keep[:, here] = jnp.broadcast_to(inv, (8, block))
            cols[:, here] = (wide * (inv * factor)).astype(BF16)

        each(0, columns // block, one)

    def teacher_chunk(slot):
        bias = jnp.where(weight[slot] > 0, 0.0, -1e4)
        spread(bias, r["spread_a"])

        def one(j):
            here = of_block(j)
            dots = jnp.dot(teach[slot], cols[:, here], preferred_element_type=F32)
            power = jnp.exp2(dots + widen(r["spread_a"][...], block))
            expo[of_slot(slot), here] = power.astype(BF16)
            total = power[:8, :]
            for start in range(8, CAP, 8):
                total = total + power[start : start + 8, :]
            r["colacc"][:, here] += total

        for j in range(columns // block):
            one(j)

    def row_pass(store, out):
        def one(k):
            def tile(i):
                here = pl.ds(pl.multiple_of(k * CAP + i * ROW_TILE, ROW_TILE), ROW_TILE)
                total = None
                for start in range(0, columns, LANES):
                    lanes = slice(start, start + LANES)
                    value = expo[here, lanes].astype(F32) * jnp.concatenate([scale[:, lanes]] * (ROW_TILE // 8), axis=0)
                    if store:
                        expo[here, lanes] = value.astype(BF16)
                    total = value if total is None else total + value
                acc[pl.ds(pl.multiple_of(i * ROW_TILE, ROW_TILE), ROW_TILE), :] = total

            each(0, CAP // ROW_TILE, tile)
            gather_rows(out, k * own)

        each(0, n, one)

    def gather_rows(out, base):
        for c in range(own):
            turned = acc[c * LANES : (c + 1) * LANES, :].T
            out[pl.ds(base + c, 1), :] = jnp.sum(turned, axis=0, keepdims=True)

    def column_pass(u):
        r["u_terms"][...] = two_terms(flatten(u))

        def one(j):
            here = of_block(j)
            total = jnp.dot(r["u_terms"][...], expo[:, here], preferred_element_type=F32)
            scale[:, here] = jnp.broadcast_to(1.0 / (total[0:1, :] + total[1:2, :]), (8, block))

        for j in range(columns // block):
            one(j)

    def student_chunk(slot):
        acc[...] = jnp.zeros_like(acc)

        def one(j):
            here = of_block(j)
            for start in range(0, block, width):
                lanes = slice(j * block + start, j * block + start + width)
                power = jnp.exp2(jnp.dot(stud[slot], cols[:, lanes], preferred_element_type=F32))
                raised[of_slot(slot), lanes] = power.astype(BF16)
                acc[...] += fold_lanes(power)

        for j in range(columns // block):
            one(j)
        gather_rows(r[f"value{ROUNDS - 1}"], dense + slot * own)
        acc_a[of_slot(slot), :] = lax.dot_general(
            raised[of_slot(slot), :], cols[...], (((1,), (1,)), ((), ())), preferred_element_type=F32
        ).astype(BF16)

    def target_chunk(slot):
        term = lax.dot_general(
            expo[of_slot(slot), :], cols[...], (((1,), (1,)), ((), ())), preferred_element_type=F32
        )
        acc_b[of_slot(slot), :] = term.astype(BF16)
        acc[...] = fold_lanes(stud[slot].astype(F32) * term)
        gather_rows(r["c_out"].at[slot], 0)

    load_t = pltpu.make_async_copy(proto_t, cols, local.at[0])
    load_s = pltpu.make_async_copy(proto_s, cols, local.at[1])
    load_w = pltpu.make_async_copy(w_in, w_all.at[of_depth(me), :], local.at[2])
    load_w.start()
    load_t.start()
    greet(groups, n + m - 2)
    teach_g.start()
    weight_g.start()
    load_w.wait()
    w_now.start()
    wo_g.start()
    teach[me] = teach_own[...]
    weight[me] = weight_own[...]
    wo_all[pl.ds(pl.multiple_of(me * tall, tall), tall), :] = w_out[...]
    r["colacc"][...] = jnp.zeros_like(r["colacc"])
    load_t.wait()
    unit_cols(1.0, None)
    teacher_chunk(me)
    teach_g.relay()
    weight_g.relay()
    each(1, half, lambda step: teacher_chunk(place(step)))
    w_now.relay()
    wo_g.relay()

    def teacher_late(step):
        teach_g.arrive(place(step))
        weight_g.arrive(place(step))
        teacher_chunk(place(step))

    each(half, n, teacher_late)
    load_s.start()
    weights = jnp.concatenate([weight[slot] for slot in range(n)], axis=0)
    r["weights"][...] = weights
    live = (weights > 0).astype(F32)
    scale[...] = jnp.broadcast_to(1.0 / jnp.sum(r["colacc"][...], axis=0, keepdims=True), scale.shape)
    row_pass(False, r["value0"])
    totals[0].start()

    load_s.wait()
    unit_cols(FOLD_S, r["inverse"])
    w_now.finish()
    wo_g.finish()
    pre = jnp.dot(rows_in[...], w_all[:, of_slab(z)], preferred_element_type=F32)
    hidden = gelu_parts(pre)[0].astype(BF16)
    r["featp"][...] = jnp.dot(hidden, wo_all[of_slab(z), :], preferred_element_type=F32)
    feat_x.start()
    totals[0].turn()
    feat_x.arrive()
    feats = r["featp"][of_part(z), :]
    for peer in feat_x.peers:
        feats = feats + r["near_f"][peer]
    r["feats"][...] = feats
    stud[me, of_part(z), :] = unit_rows(feats)[0].astype(BF16)
    stud_x.start()
    total = totals[0].finish()
    stud_x.arrive()
    stud_g.start()
    for turn in range(1, ROUNDS - 1):
        column_pass(row_scale(live, total))
        if turn == ROUNDS - 2:
            stud_g.relay()
        row_pass(False, r[f"value{turn}"])
        totals[turn].start()
        if turn < ROUNDS - 2:
            totals[turn].turn()
            total = totals[turn].finish()

    student_chunk(me)
    totals[ROUNDS - 2].turn()
    stud_g.finish()
    for gather in w_later:
        gather.start()
    each(1, n, lambda step: student_chunk(place(step)))

    total = totals[ROUNDS - 2].finish()
    column_pass(row_scale(live, total))
    row_pass(True, r[f"value{ROUNDS - 1}"])
    final = totals[ROUNDS - 1]
    final.start()
    for gather in w_later:
        gather.relay()

    def turn_rows(slot):
        r["s_prob"][:, of_slot(slot)] = stud[slot].astype(F32).T.astype(BF16)

    each(0, n, turn_rows)
    each(0, half, target_chunk)
    final.turn()
    each(half, n, target_chunk)
    load_s.start()
    crosses.start()
    sums = final.finish()
    r["last"][...] = sums
    live = (r["weights"][...] > 0).astype(F32)
    factor = r["weights"][...] * (1.0 / STUDENT_TEMP)
    u = row_scale(live, sums[:dense])
    r["probs"][...] = factor / sums[dense:]
    r["targets"][...] = factor * u

    def mix(slot):
        spread(r["probs"][pl.ds(slot * own, own), :], r["spread_a"])
        spread(r["targets"][pl.ds(slot * own, own), :], r["spread_b"])
        return acc_a[of_slot(slot), :].astype(F32) * widen(r["spread_a"][...], width) - acc_b[
            of_slot(slot), :
        ].astype(F32) * widen(r["spread_b"][...], width)

    def send_mix(step):
        peer = lax.rem(me + step, n)
        acc_a[of_slot(peer), :] = mix(peer).astype(BF16)
        grads.copy(peer, me).start()

    each(1, n, send_mix)
    r["g_own"][...] = mix(me)

    def scale_rows(slot):
        here = of_slot(slot)
        turned = r["s_prob"][:, here].astype(F32)
        base = pl.ds(slot * own, own)
        r["s_target"][:, here] = (turned * flatten(r["targets"][base, :])).astype(BF16)
        r["s_prob"][:, here] = (turned * flatten(r["probs"][base, :])).astype(BF16)

    each(0, n, scale_rows)

    def out_copy(j):
        return pltpu.make_async_copy(
            r["stage"].at[lax.rem(j, 2)], grad_proto.at[:, of_block(j)], local.at[4 + lax.rem(j, 2)]
        )

    def column_grad(j):
        @pl.when(j >= 2)
        def _():
            out_copy(j - 2).wait()

        here = of_block(j)
        grad = jnp.dot(r["s_prob"][...], raised[:, here], preferred_element_type=F32) - jnp.dot(
            r["s_target"][...], expo[:, here], preferred_element_type=F32
        )
        inv = r["inverse"][0:1, here]
        unit = cols[:, here].astype(F32) * inv
        r["stage"][lax.rem(j, 2)] = (grad - unit * jnp.sum(unit * grad, axis=0, keepdims=True)) * inv
        out_copy(j).start()

    blocks = columns // block
    load_s.wait()
    each(0, blocks, column_grad)

    for gather in w_later:
        gather.finish()

    for j in range(max(0, blocks - 2), blocks):
        out_copy(j).wait()
    per = block // width
    hidden_blocks = w_all.shape[1] // width
    whole_depth = w_all.shape[0]
    pieces = slab // width

    def of_width(k):
        return pl.ds(pl.multiple_of(k * width, width), width)

    def hidden_block(b):
        pre = jnp.dot(rows_in[...], w_all[:, of_width(b)], preferred_element_type=F32)
        act, slope = gelu_parts(pre)
        raised[of_slot(b), 0:width] = act.astype(BF16)
        r["stage"][b // per, 0:CAP, of_width(lax.rem(b, per))] = slope

    each(0, hidden_blocks, hidden_block)

    def turn_tokens(k):
        expo[of_width(k), width : width + CAP] = rows_in[:, of_width(k)].astype(F32).T.astype(BF16)

    each(0, whole_depth // width, turn_tokens)

    crosses.arrive()
    cross = r["c_out"][me]
    for peer in crosses.peers:
        cross = cross + r["c_near"][peer]
    r["c_part"][...] = cross
    cross_x.start()
    grads.arrive()
    grad = r["g_own"][...]
    for peer in grads.peers:
        grad = grad + r["g_near"][peer].astype(F32)
    r["g_own"][...] = grad
    r["g_part"][...] = grad.astype(BF16)
    grad_x.start()
    cross_x.arrive()
    for peer in cross_x.peers:
        cross = cross + r["c_far"][peer]
    mine = pl.ds(me * own, own)
    u = row_scale((r["weights"][mine, :] > 0).astype(F32), r["last"][mine, :])
    loss[...] = jnp.log(r["last"][pl.ds(dense + me * own, own), :]) - u * cross * (1.0 / LOG2E)
    grad_x.arrive()
    grad = r["g_own"][of_part(z), :]
    for peer in grad_x.peers:
        grad = grad + r["g_far"][peer].astype(F32)
    unit, inv = unit_rows(r["feats"][...])
    grad = grad * (1.0 / FOLD_S)
    inner = jnp.sum(unit * grad, axis=1, keepdims=True)
    grad_feats[of_part(z), :] = (inv * (grad - unit * inner)).astype(BF16)
    back_x.start()

    for gather in [teach_g, weight_g, w_now, wo_g, stud_g] + w_later:
        gather.drain()
    for one in totals + [grads, crosses, feat_x, stud_x, grad_x, cross_x]:
        one.drain()
    back_x.arrive()
    back_x.drain()

    lane_in, lane_mid = width + CAP, 2 * width

    def back_block(b):
        grad_hidden = lax.dot_general(
            grad_feats[...], wo_all[of_width(b), :], (((1,), (1,)), ((), ())), preferred_element_type=F32
        )
        expo[of_slot(b), 0:width] = (grad_hidden * r["stage"][b // per, 0:CAP, of_width(lax.rem(b, per))]).astype(BF16)

    def out_block(b):
        raised[of_width(b), width : 2 * width] = lax.dot_general(
            raised[of_slot(b), 0:width], grad_feats[...], (((0,), (0,)), ((), ())), preferred_element_type=F32
        ).astype(BF16)

    side = lax.rem(me, 2)
    team = me // 2
    teams = [lax.rem(team + step, half) for step in range(1, half)]

    def pair_copy(q, h):
        lanes = slice(h * width, (h + 1) * width)
        return remote(
            expo.at[of_depth(2 * q + 1 - side), lane_in + h * width : lane_in + (h + 1) * width],
            r["wide_a"].at[q, :, lanes],
            r["wide_sems"].at[h, q],
            r["wide_sems"].at[pieces + h, q],
            {"dp": me + flip},
        )

    def team_copy(q, slot, h):
        lanes = slice(h * width, (h + 1) * width)
        return remote(
            raised.at[of_depth(q), lane_mid + h * width : lane_mid + (h + 1) * width],
            r["wide_b"].at[slot, :, lanes],
            r["wide_sems"].at[2 * pieces + h, q],
            r["wide_sems"].at[3 * pieces + h, slot],
            {"dp": 2 * q + side},
        )

    def own_term(q, h):
        lanes = slice(h * width, (h + 1) * width)
        mine = expo[of_depth(2 * q + side), lane_in + h * width : lane_in + (h + 1) * width]
        return mine.astype(F32) + r["wide_a"][q, :, lanes].astype(F32)

    def wide_lanes(s, h):
        return pl.ds(pl.multiple_of(s * slab + h * width, width), width)

    def wide_exchange(h):
        return Chain("tensor", m, lambda s: wide_out.at[:, wide_lanes(s, h)], *line(9 + h))

    wide_x = [wide_exchange(h) for h in range(pieces)]
    sub = tall // m
    narrow_n = Exchange(
        "dp",
        n,
        lambda p: raised.at[pl.ds(pl.multiple_of(p * tall + z * sub, sub), sub), width : 2 * width],
        lambda s: r["narrow_a"].at[s],
        *pair(10),
    )

    def of_sub(s):
        return pl.ds(pl.multiple_of(s * sub, sub), sub)

    narrow_x = Exchange("tensor", m, lambda p: narrow_out.at[of_sub(z), :], lambda s: narrow_out.at[of_sub(s), :], *line(8))

    for h in range(pieces):
        mine = z * pieces + h
        back_block(mine)

        def in_block(p):
            expo[of_depth(p), lane_in + h * width : lane_in + (h + 1) * width] = jnp.dot(
                expo[of_depth(p), width : width + CAP], expo[of_slot(mine), 0:width], preferred_element_type=F32
            ).astype(BF16)

        for q in teams + [team]:
            in_block(2 * q + 1 - side)
            pair_copy(q, h).start()
        for q in teams + [team]:
            in_block(2 * q + side)
    each(0, hidden_blocks, out_block)
    narrow_n.start()
    for h in range(pieces):
        for q in teams:
            pair_copy(q, h).wait_recv()
            raised[of_depth(q), lane_mid + h * width : lane_mid + (h + 1) * width] = own_term(q, h).astype(BF16)
            team_copy(q, team, h).start()
        pair_copy(team, h).wait_recv()
    each(0, m * pieces, back_block)
    for h in range(pieces):
        for q in teams:
            team_copy(q, q, h).wait_recv()
        total = own_term(team, h)
        for q in teams:
            total = total + r["wide_b"][q, :, h * width : (h + 1) * width].astype(F32)
        wide_out[:, wide_lanes(z, h)] = total.astype(BF16)
        wide_x[h].start()
    narrow_n.arrive()
    total = raised[pl.ds(pl.multiple_of(me * tall + z * sub, sub), sub), width : 2 * width].astype(F32)
    for peer in narrow_n.peers:
        total = total + r["narrow_a"][peer].astype(F32)
    narrow_out[of_sub(z), :] = total.astype(BF16)
    narrow_x.start()

    def token_block(k):
        total = None
        for b in range(hidden_blocks):
            term = lax.dot_general(
                expo[b * CAP : (b + 1) * CAP, 0:width],
                w_all[of_width(k), b * width : (b + 1) * width],
                (((1,), (1,)), ((), ())),
                preferred_element_type=F32,
            )
            total = term if total is None else total + term
        grad_rows[:, of_width(k)] = total.astype(BF16)

    token_blocks = whole_depth // width
    for step in range(1, m):
        each(token_blocks * (step - 1) // (m - 1), token_blocks * step // (m - 1), token_block)
        for one in wide_x:
            one.relay(step)
    narrow_x.arrive()
    for one in wide_x + [narrow_n, narrow_x]:
        one.drain()
    for h in range(pieces):
        for q in teams:
            pair_copy(q, h).wait_send()
            team_copy(q, team, h).wait_send()
        pair_copy(team, h).wait_send()


def balance(groups, teach, weight, rows_in, w_in, w_out, proto_t, proto_s, ident):
    n, m = groups["dp"], groups["tensor"]
    rows, width = n * teach.shape[0], teach.shape[1]
    columns = proto_s.shape[1]
    depth, hidden = n * w_in.shape[0], w_in.shape[1]
    shapes = plan(groups, rows, columns, width, depth, hidden)
    vmem, hbm = pl.BlockSpec(memory_space=pltpu.VMEM), pl.BlockSpec(memory_space=pl.ANY)
    return pl.pallas_call(
        functools.partial(balance_kernel, groups, list(shapes)),
        name="balance",
        in_specs=[vmem, vmem, vmem, hbm, vmem, hbm, hbm],
        out_specs=[hbm, vmem, vmem, vmem, vmem],
        out_shape=[
            jax.ShapeDtypeStruct((width, columns), F32),
            jax.ShapeDtypeStruct((CAP // LANES, LANES), F32),
            jax.ShapeDtypeStruct((CAP, depth), BF16),
            jax.ShapeDtypeStruct((depth // n, hidden), BF16),
            jax.ShapeDtypeStruct((hidden // n, width), BF16),
        ],
        scratch_shapes=list(shapes.values()),
        compiler_params=pltpu.CompilerParams(
            collective_id=ident, has_side_effects=True, vmem_limit_bytes=62 * 1024 * 1024
        ),
    )(teach, weight, rows_in, w_in, w_out, proto_t, proto_s)


def selection(masks):
    crops, patches = masks.shape
    size = crops * patches
    flat = masks.reshape(1, size)
    before = (
        lax.broadcasted_iota(jnp.int32, (size, size), 0) < lax.broadcasted_iota(jnp.int32, (size, size), 1)
    ).astype(BF16)
    place = jnp.dot(flat.astype(BF16), before, preferred_element_type=F32).astype(jnp.int32)
    slots = lax.broadcasted_iota(jnp.int32, (CAP, size), 0)
    picked = (place == slots) & (flat > 0)
    dead = slots >= jnp.sum(flat)
    first = lax.broadcasted_iota(jnp.int32, (CAP, size), 1) == 0
    return (picked | (dead & first)).astype(BF16), picked.astype(BF16)


def shards(groups, tokens, teacher_feats, masks, w_in, w_out, proto_student, proto_teacher):
    pick, place = selection(masks)
    counts = jnp.sum(masks, axis=1)
    ends = jnp.sum(
        jnp.where(jnp.arange(counts.shape[0])[:, None] <= jnp.arange(counts.shape[0])[None, :], counts[:, None], 0),
        axis=0,
    )
    slot = jnp.arange(CAP)[:, None]
    member = ((slot >= (ends - counts)[None, :]) & (slot < ends[None, :])).astype(F32)
    inverse = 1.0 / jnp.maximum(counts, 1).astype(F32)
    weight = (GRAD_SCALE * jnp.sum(member * inverse[None, :], axis=1)).astype(BF16)
    teacher_pick = jnp.dot(pick, teacher_feats, preferred_element_type=F32)
    teacher_rows = (unit_rows(teacher_pick)[0] * FOLD_T).astype(BF16)
    rows = jnp.dot(pick, tokens, preferred_element_type=F32).astype(BF16)
    grad_proto, row_loss, grad_rows, wide, narrow = balance(
        groups, teacher_rows, weight.astype(F32).reshape(-1, LANES), rows, w_in, w_out, proto_teacher, proto_student, 0
    )
    crop_loss = jnp.sum(member * row_loss.reshape(CAP)[:, None], axis=0) * inverse
    grad_in = wide.astype(F32)
    grad_out = narrow.astype(F32)
    d_tokens = lax.dot_general(
        place, grad_rows, (((0,), (0,)), ((), ())), preferred_element_type=F32
    ).astype(BF16)
    return (d_tokens, grad_in, grad_out, grad_proto, crop_loss)


def solution(mesh):
    groups = {"dp": mesh.shape["dp"], "tensor": mesh.shape["tensor"]}
    placed = (
        P("dp", None),
        P("dp", None),
        P("dp", None),
        P("dp", None),
        P("dp", None),
        P(None, ("dp", "tensor")),
        P(None, ("dp", "tensor")),
    )
    return jax.shard_map(
        functools.partial(shards, groups),
        mesh=mesh,
        in_specs=placed,
        out_specs=(P("dp", None), P("dp", None), P("dp", None), P(None, ("dp", "tensor")), P("dp")),
        check_vma=False,
    )
```

```python
import functools

import jax
import jax.numpy as jnp
from jax import lax
from jax.experimental import pallas as pl
from jax.experimental.pallas import tpu as pltpu
from jax.sharding import PartitionSpec as P

ROUNDS = 3
CAP = 256

TEACHER_TEMP = 0.07
STUDENT_TEMP = 0.1
EPS = 1e-06
GRAD_SCALE = 65536.0
LOG2E = 1.4426950408889634
LANES = 128
BLOCK = 1024
ROW_TILE = 64
MESH = pl.DeviceIdType.MESH
F32 = jnp.float32
BF16 = jnp.bfloat16


def gelu_parts(pre):
    cdf = 0.5 * (1.0 + lax.erf(pre * 0.7071067811865476))
    pdf = jnp.exp(-0.5 * pre * pre) * 0.3989422804014327
    return (pre * cdf, cdf + pre * pdf)


def unit_rows(feats):
    inverse = lax.rsqrt(jnp.sum(feats * feats, axis=1, keepdims=True) + EPS)
    return (feats * inverse, inverse)


def unit_columns(protos):
    wide = protos.astype(F32)
    norms = jnp.sqrt(jnp.sum(wide * wide, axis=0, keepdims=True) + EPS)
    return (wide / norms, norms)


def spread(dense, out_ref):
    for c in range(dense.shape[0]):
        row = jnp.broadcast_to(dense[c : c + 1, :], (LANES, LANES))
        out_ref[c * LANES : (c + 1) * LANES, :] = row.T


def gathered(acc_ref, out_ref, base):
    for c in range(acc_ref.shape[0] // LANES):
        turned = acc_ref[c * LANES : (c + 1) * LANES, :].T
        out_ref[base + c : base + c + 1, :] = jnp.sum(turned, axis=0, keepdims=True)


def fold_lanes(values):
    total = values[:, :LANES]
    for start in range(LANES, values.shape[1], LANES):
        total = total + values[:, start : start + LANES]
    return total


def widen(values, cols):
    return jnp.concatenate([values] * (cols // LANES), axis=1)


def two_terms(row):
    high = row.astype(BF16)
    low = (row - high.astype(F32)).astype(BF16)
    return jnp.concatenate([high, low, jnp.zeros((14, row.shape[1]), BF16)], axis=0)


def flatten(dense):
    return jnp.concatenate([dense[c : c + 1, :] for c in range(dense.shape[0])], axis=1)


def row_scale(live, row_sum):
    return live / (row_sum + 1.0 - live)


def greet(groups, many):
    barrier = pltpu.get_barrier_semaphore()
    for axis in ("dp", "tensor"):
        me = lax.axis_index(axis)
        for step in range(1, groups[axis]):
            peer = lax.rem(me + step, groups[axis])
            pl.semaphore_signal(barrier, inc=1, device_id={axis: peer}, device_id_type=MESH)
    pl.semaphore_wait(barrier, many)


def remote(source, target, send, recv, where):
    return pltpu.make_async_remote_copy(
        src_ref=source, dst_ref=target, send_sem=send, recv_sem=recv, device_id=where, device_id_type=MESH
    )


class PairGather:
    def __init__(self, n, own, slot, send, recv):
        self.me = lax.axis_index("dp")
        self.flip = 1 - 2 * lax.rem(self.me, 2)
        self.partner = self.me + self.flip
        self.peers = [lax.rem(self.me + step, n) for step in range(2, n, 2)]
        self.own, self.slot, self.send, self.recv = own, slot, send, recv

    def copy(self, source, slot, sender, peer):
        return remote(source, self.slot(slot), self.send.at[sender], self.recv.at[slot], {"dp": peer})

    def start(self):
        for peer in self.peers + [self.partner]:
            self.copy(self.own, self.me, peer, peer).start()

    def arrive(self, slot):
        self.copy(self.own, slot, slot, slot).wait_recv()

    def forward(self, peer):
        self.copy(self.slot(peer), peer, peer + self.flip, self.partner).start()

    def relay(self):
        for peer in self.peers:
            self.arrive(peer)
            self.forward(peer)

    def finish(self):
        self.arrive(self.partner)
        for peer in self.peers:
            self.arrive(peer + self.flip)

    def drain(self):
        for peer in self.peers:
            self.copy(self.own, self.me, peer, peer).wait_send()
            self.copy(self.slot(peer), peer, peer + self.flip, self.partner).wait_send()
        self.copy(self.own, self.me, self.partner, self.partner).wait_send()


class Exchange:
    def __init__(self, axis, n, source, landing, send, recv):
        self.me = lax.axis_index(axis)
        self.axis, self.source, self.landing, self.send, self.recv = axis, source, landing, send, recv
        self.peers = [lax.rem(self.me + step, n) for step in range(1, n)]

    def copy(self, peer, slot):
        return remote(self.source(peer), self.landing(slot), self.send.at[peer], self.recv.at[slot], {self.axis: peer})

    def start(self):
        for peer in self.peers:
            self.copy(peer, self.me).start()

    def arrive(self):
        for peer in self.peers:
            self.copy(peer, peer).wait_recv()

    def drain(self):
        for peer in self.peers:
            self.copy(peer, self.me).wait_send()


class Chain:
    def __init__(self, axis, n, block, send, recv):
        self.me = lax.axis_index(axis)
        self.axis, self.n, self.block, self.send, self.recv = axis, n, block, send, recv

    def copy(self, step, way):
        index = lax.rem(self.me - way * step + self.n, self.n)
        peer = lax.rem(self.me + way + self.n, self.n)
        ref = self.block(index)
        send = self.send.at[self.n if step == 0 and way < 0 else index]
        return remote(ref, ref, send, self.recv.at[index], {self.axis: peer})

    def held(self, step, way):
        index = self.me - way * step
        return (index >= 0) & (index < self.n)

    def each_way(self, step, arrive, send, done):
        for way in (1, -1):
            held = self.held(step, way)
            beyond = self.me + way
            onward = held & (beyond >= 0) & (beyond < self.n)
            if arrive:
                pl.when(held)(lambda way=way: self.copy(step, way).wait_recv())
            if send:
                pl.when(onward)(lambda way=way: self.copy(step, way).start())
            if done:
                pl.when(onward)(lambda way=way: self.copy(step, way).wait_send())

    def start(self):
        self.each_way(0, False, True, False)

    def relay(self, step):
        self.each_way(step, True, step < self.n - 1, False)

    def drain(self):
        for step in range(self.n - 1):
            self.each_way(step, False, False, True)


class Total:
    def __init__(self, n, m, value, near, part, far, sems_n, sems_m):
        self.n, self.m = n, m
        self.value, self.near, self.part, self.far = value, near, part, far
        self.first = Exchange("dp", n, lambda peer: value, lambda slot: near.at[slot], *sems_n)
        self.second = Exchange("tensor", m, lambda peer: part, lambda slot: far.at[slot], *sems_m)

    def start(self):
        self.first.start()
        self.near[self.first.me] = self.value[...]

    def turn(self):
        self.first.arrive()
        total = self.near[0]
        for slot in range(1, self.n):
            total = total + self.near[slot]
        self.part[...] = total
        self.second.start()
        self.far[self.second.me] = total

    def finish(self):
        self.second.arrive()
        total = self.far[0]
        for slot in range(1, self.m):
            total = total + self.far[slot]
        return total

    def drain(self):
        self.first.drain()
        self.second.drain()


def plan(groups, rows, columns, width, depth, hidden):
    n, m = groups["dp"], groups["tensor"]
    dense = rows // LANES
    own = CAP // LANES
    part = CAP // m
    block = min(BLOCK, columns)
    vmem = pltpu.VMEM
    shapes = dict(
        expo=vmem((rows, columns), BF16),
        raised=vmem((rows, columns), BF16),
        cols=vmem((width, columns), BF16),
        teach=vmem((n, CAP, width), BF16),
        weight=vmem((n, own, LANES), F32),
        weights=vmem((dense, LANES), F32),
        rows_in=vmem((CAP, depth), BF16),
        w_all=vmem((depth, hidden), BF16),
        wo_all=vmem((hidden, width), BF16),
        featp=vmem((CAP, width), F32),
        grad_feats=vmem((CAP, width), BF16),
        near_f=vmem((m, part, width), F32),
        feats=vmem((part, width), F32),
        stud=vmem((n, CAP, width), BF16),
        s_prob=vmem((width, rows), BF16),
        s_target=vmem((width, rows), BF16),
        acc_a=vmem((rows, width), BF16),
        acc_b=vmem((rows, width), BF16),
        g_own=vmem((CAP, width), F32),
        g_near=vmem((n, CAP, width), BF16),
        g_part=vmem((CAP, width), BF16),
        g_far=vmem((m, part, width), BF16),
        c_out=vmem((n, own, LANES), F32),
        c_near=vmem((n, own, LANES), F32),
        c_part=vmem((own, LANES), F32),
        c_far=vmem((m, own, LANES), F32),
        colacc=vmem((8, columns), F32),
        scale=vmem((8, columns), F32),
        inverse=vmem((8, columns), F32),
        u_terms=vmem((16, rows), BF16),
        acc=vmem((CAP, LANES), F32),
        spread_a=vmem((CAP, LANES), F32),
        spread_b=vmem((CAP, LANES), F32),
        probs=vmem((dense, LANES), F32),
        targets=vmem((dense, LANES), F32),
        last=vmem((2 * dense, LANES), F32),
        stage=vmem((2, max(width, CAP), block), F32),
        wide_a=vmem((n // 2, depth // n, hidden // m), BF16),
        wide_b=vmem((n // 2, depth // n, hidden // m), BF16),
        narrow_a=vmem((n, hidden // n // m, width), BF16),
        wide_sems=pltpu.SemaphoreType.DMA((4 * (hidden // m // LANES), n)),
        pair_send=pltpu.SemaphoreType.DMA((11 + m, n)),
        pair_recv=pltpu.SemaphoreType.DMA((11 + m, n)),
        line_send=pltpu.SemaphoreType.DMA((9 + hidden // m // LANES, m + 1)),
        line_recv=pltpu.SemaphoreType.DMA((9 + hidden // m // LANES, m + 1)),
        local=pltpu.SemaphoreType.DMA((8 + depth // width,)),
    )
    for turn in range(ROUNDS):
        size = 2 * dense if turn == ROUNDS - 1 else dense
        shapes[f"value{turn}"] = vmem((size, LANES), F32)
        shapes[f"near{turn}"] = vmem((n, size, LANES), F32)
        shapes[f"part{turn}"] = vmem((size, LANES), F32)
        shapes[f"far{turn}"] = vmem((m, size, LANES), F32)
    return shapes


FOLD_T = LOG2E / TEACHER_TEMP
FOLD_S = LOG2E / STUDENT_TEMP


def balance_kernel(groups, names, *refs):
    n, m = groups["dp"], groups["tensor"]
    teach_own, weight_own, pick, tokens, w_in, w_out, proto_t, proto_s = refs[:8]
    grad_proto, loss, d_tokens, wide_out, narrow_out = refs[8:13]
    r = dict(zip(names, refs[13:]))
    rows_in = r["rows_in"]
    expo, raised, cols, w_all, wo_all, grad_feats = (
        r["expo"], r["raised"], r["cols"], r["w_all"], r["wo_all"], r["grad_feats"]
    )
    teach, weight, stud, acc, scale = r["teach"], r["weight"], r["stud"], r["acc"], r["scale"]
    acc_a, acc_b, local = r["acc_a"], r["acc_b"], r["local"]
    rows, columns = expo.shape
    width = cols.shape[0]
    dense = rows // LANES
    own = CAP // LANES
    block = r["stage"].shape[2]
    depth = w_in.shape[0]
    slab = w_all.shape[1] // m
    part = CAP // m
    me, z = lax.axis_index("dp"), lax.axis_index("tensor")
    half = n // 2
    flip = 1 - 2 * lax.rem(me, 2)

    def pair(k):
        return r["pair_send"].at[k], r["pair_recv"].at[k]

    def line(k):
        return r["line_send"].at[k], r["line_recv"].at[k]

    def place(step):
        return lax.rem(me + 2 * lax.rem(step, half), n) + flip * (step // half)

    def of_block(j):
        if isinstance(j, int):
            return slice(j * block, (j + 1) * block)
        return pl.ds(pl.multiple_of(j * block, block), block)

    def of_slot(slot):
        return pl.ds(pl.multiple_of(slot * CAP, CAP), CAP)

    def each(low, high, body):
        def step(j, carry):
            body(j)
            return carry

        lax.fori_loop(low, high, step, 0)

    teach_g = PairGather(n, teach_own, lambda s: teach.at[s], *pair(0))
    weight_g = PairGather(n, weight_own, lambda s: weight.at[s], *pair(1))

    def of_slab(k):
        return pl.ds(pl.multiple_of(k * slab, slab), slab)

    def of_depth(slot):
        return pl.ds(pl.multiple_of(slot * depth, depth), depth)

    def w_gather(k, index):
        lanes = of_slab(k)
        return PairGather(n, w_all.at[of_depth(me), lanes], lambda s: w_all.at[of_depth(s), lanes], *pair(index))

    w_now = w_gather(z, 2)
    w_later = [w_gather(lax.rem(z + k, m), 10 + k) for k in range(1, m)]
    tall = w_out.shape[0]
    wo_g = PairGather(n, w_out, lambda s: wo_all.at[pl.ds(pl.multiple_of(s * tall, tall), tall), :], *pair(3))
    stud_g = PairGather(n, stud.at[me], lambda s: stud.at[s], *pair(4))
    totals = [
        Total(n, m, r[f"value{k}"], r[f"near{k}"], r[f"part{k}"], r[f"far{k}"], pair(5 + k), line(2 + k))
        for k in range(ROUNDS)
    ]
    grads = Exchange("dp", n, lambda p: acc_a.at[of_slot(p), :], lambda s: r["g_near"].at[s], *pair(8))
    crosses = Exchange("dp", n, lambda p: r["c_out"].at[p], lambda s: r["c_near"].at[s], *pair(9))

    def of_part(k):
        return pl.ds(pl.multiple_of(k * part, part), part)

    feat_x = Exchange("tensor", m, lambda p: r["featp"].at[of_part(p), :], lambda s: r["near_f"].at[s], *line(0))
    stud_x = Exchange(
        "tensor", m, lambda p: stud.at[me, of_part(z), :], lambda s: stud.at[me, of_part(s), :], *line(1)
    )
    grad_x = Exchange("tensor", m, lambda p: r["g_part"].at[of_part(p), :], lambda s: r["g_far"].at[s], *line(5))
    cross_x = Exchange("tensor", m, lambda p: r["c_part"], lambda s: r["c_far"].at[s], *line(6))
    back_x = Exchange(
        "tensor", m, lambda p: grad_feats.at[of_part(z), :], lambda s: grad_feats.at[of_part(s), :], *line(7)
    )

    def unit_cols(factor, keep):
        def one(j):
            here = of_block(j)
            wide = cols[:, here].astype(F32)
            inv = 1.0 / jnp.sqrt(jnp.sum(wide * wide, axis=0, keepdims=True) + EPS)
            if keep is not None:
                keep[:, here] = jnp.broadcast_to(inv, (8, block))
            cols[:, here] = (wide * (inv * factor)).astype(BF16)

        each(0, columns // block, one)

    def teacher_chunk(slot):
        bias = jnp.where(weight[slot] > 0, 0.0, -1e4)
        spread(bias, r["spread_a"])

        def one(j):
            here = of_block(j)
            dots = jnp.dot(teach[slot], cols[:, here], preferred_element_type=F32)
            power = jnp.exp2(dots + widen(r["spread_a"][...], block))
            expo[of_slot(slot), here] = power.astype(BF16)
            total = power[:8, :]
            for start in range(8, CAP, 8):
                total = total + power[start : start + 8, :]
            r["colacc"][:, here] += total

        for j in range(columns // block):
            one(j)

    def row_pass(store, out):
        def one(k):
            def tile(i):
                here = pl.ds(pl.multiple_of(k * CAP + i * ROW_TILE, ROW_TILE), ROW_TILE)
                total = None
                for start in range(0, columns, LANES):
                    lanes = slice(start, start + LANES)
                    value = expo[here, lanes].astype(F32) * jnp.concatenate([scale[:, lanes]] * (ROW_TILE // 8), axis=0)
                    if store:
                        expo[here, lanes] = value.astype(BF16)
                    total = value if total is None else total + value
                acc[pl.ds(pl.multiple_of(i * ROW_TILE, ROW_TILE), ROW_TILE), :] = total

            each(0, CAP // ROW_TILE, tile)
            gather_rows(out, k * own)

        each(0, n, one)

    def gather_rows(out, base):
        for c in range(own):
            turned = acc[c * LANES : (c + 1) * LANES, :].T
            out[pl.ds(base + c, 1), :] = jnp.sum(turned, axis=0, keepdims=True)

    def column_pass(u):
        r["u_terms"][...] = two_terms(flatten(u))

        def one(j):
            here = of_block(j)
            total = jnp.dot(r["u_terms"][...], expo[:, here], preferred_element_type=F32)
            scale[:, here] = jnp.broadcast_to(1.0 / (total[0:1, :] + total[1:2, :]), (8, block))

        for j in range(columns // block):
            one(j)

    def student_chunk(slot):
        acc[...] = jnp.zeros_like(acc)

        def one(j):
            here = of_block(j)
            for start in range(0, block, width):
                lanes = slice(j * block + start, j * block + start + width)
                power = jnp.exp2(jnp.dot(stud[slot], cols[:, lanes], preferred_element_type=F32))
                raised[of_slot(slot), lanes] = power.astype(BF16)
                acc[...] += fold_lanes(power)

        for j in range(columns // block):
            one(j)
        gather_rows(r[f"value{ROUNDS - 1}"], dense + slot * own)
        acc_a[of_slot(slot), :] = lax.dot_general(
            raised[of_slot(slot), :], cols[...], (((1,), (1,)), ((), ())), preferred_element_type=F32
        ).astype(BF16)

    def student_own():
        feat_x.arrive()
        feats = r["featp"][of_part(z), :]
        for peer in feat_x.peers:
            feats = feats + r["near_f"][peer]
        r["feats"][...] = feats
        stud[me, of_part(z), :] = unit_rows(feats)[0].astype(BF16)
        stud_x.start()

    def target_chunk(slot):
        term = lax.dot_general(
            expo[of_slot(slot), :], cols[...], (((1,), (1,)), ((), ())), preferred_element_type=F32
        )
        acc_b[of_slot(slot), :] = term.astype(BF16)
        acc[...] = fold_lanes(stud[slot].astype(F32) * term)
        gather_rows(r["c_out"].at[slot], 0)

    load_t = pltpu.make_async_copy(proto_t, cols, local.at[0])
    load_s = pltpu.make_async_copy(proto_s, cols, local.at[1])
    load_w = pltpu.make_async_copy(w_in, w_all.at[of_depth(me), :], local.at[2])
    load_w.start()
    load_t.start()
    patches = tokens.shape[0]
    in_row = block // width

    def of_width(k):
        if isinstance(k, int):
            return slice(k * width, (k + 1) * width)
        return pl.ds(pl.multiple_of(k * width, width), width)

    def token_home(k):
        return slice(k // in_row * patches, (k // in_row + 1) * patches), of_width(k % in_row)

    token_loads = [
        pltpu.make_async_copy(tokens.at[:, of_width(k)], raised.at[token_home(k)], local.at[8 + k])
        for k in range(w_all.shape[0] // width)
    ]
    for load in token_loads:
        load.start()
    greet(groups, n + m - 2)
    teach_g.start()
    weight_g.start()
    teach[me] = teach_own[...]
    weight[me] = weight_own[...]
    wo_all[pl.ds(pl.multiple_of(me * tall, tall), tall), :] = w_out[...]
    r["colacc"][...] = jnp.zeros_like(r["colacc"])
    load_t.wait()
    unit_cols(1.0, None)
    teacher_chunk(me)
    for k, load in enumerate(token_loads):
        load.wait()
        rows_in[:, of_width(k)] = jnp.dot(pick[...], raised[token_home(k)], preferred_element_type=F32).astype(BF16)
    teach_g.relay()
    weight_g.relay()
    load_w.wait()
    w_now.start()
    wo_g.start()
    each(1, half, lambda step: teacher_chunk(place(step)))

    def teacher_late(step):
        teach_g.arrive(place(step))
        weight_g.arrive(place(step))
        teacher_chunk(place(step))

    each(half, n, teacher_late)
    load_s.start()
    weights = jnp.concatenate([weight[slot] for slot in range(n)], axis=0)
    r["weights"][...] = weights
    live = (weights > 0).astype(F32)
    scale[...] = jnp.broadcast_to(1.0 / jnp.sum(r["colacc"][...], axis=0, keepdims=True), scale.shape)
    row_pass(False, r["value0"])
    totals[0].start()

    load_s.wait()
    unit_cols(FOLD_S, r["inverse"])
    w_now.relay()
    wo_g.relay()
    totals[0].turn()
    w_now.finish()
    wo_g.finish()
    pre = jnp.dot(rows_in[...], w_all[:, of_slab(z)], preferred_element_type=F32)
    hidden = gelu_parts(pre)[0].astype(BF16)
    r["featp"][...] = jnp.dot(hidden, wo_all[of_slab(z), :], preferred_element_type=F32)
    feat_x.start()
    total = totals[0].finish()
    for turn in range(1, ROUNDS - 1):
        column_pass(row_scale(live, total))
        if turn == ROUNDS - 2:
            student_own()
        row_pass(False, r[f"value{turn}"])
        totals[turn].start()
        if turn < ROUNDS - 2:
            totals[turn].turn()
            total = totals[turn].finish()
    stud_x.arrive()
    stud_g.start()
    student_chunk(me)
    stud_g.relay()
    totals[ROUNDS - 2].turn()
    each(1, half, lambda step: student_chunk(place(step)))
    stud_g.finish()
    for gather in w_later:
        gather.start()
    each(half, n, lambda step: student_chunk(place(step)))
    total = totals[ROUNDS - 2].finish()
    column_pass(row_scale(live, total))
    row_pass(True, r[f"value{ROUNDS - 1}"])
    final = totals[ROUNDS - 1]
    final.start()

    def turn_rows(slot):
        r["s_prob"][:, of_slot(slot)] = stud[slot].astype(F32).T.astype(BF16)

    each(0, n, turn_rows)
    each(0, half, target_chunk)
    final.turn()
    each(half, n, target_chunk)
    load_s.start()
    crosses.start()
    sums = final.finish()
    r["last"][...] = sums
    live = (r["weights"][...] > 0).astype(F32)
    factor = r["weights"][...] * (1.0 / STUDENT_TEMP)
    u = row_scale(live, sums[:dense])
    r["probs"][...] = factor / sums[dense:]
    r["targets"][...] = factor * u

    def mix(slot):
        spread(r["probs"][pl.ds(slot * own, own), :], r["spread_a"])
        spread(r["targets"][pl.ds(slot * own, own), :], r["spread_b"])
        return acc_a[of_slot(slot), :].astype(F32) * widen(r["spread_a"][...], width) - acc_b[
            of_slot(slot), :
        ].astype(F32) * widen(r["spread_b"][...], width)

    def send_mix(step):
        peer = lax.rem(me + step, n)
        acc_a[of_slot(peer), :] = mix(peer).astype(BF16)
        grads.copy(peer, me).start()

    each(1, n, send_mix)
    r["g_own"][...] = mix(me)

    def scale_rows(slot):
        here = of_slot(slot)
        turned = r["s_prob"][:, here].astype(F32)
        base = pl.ds(slot * own, own)
        r["s_target"][:, here] = (turned * flatten(r["targets"][base, :])).astype(BF16)
        r["s_prob"][:, here] = (turned * flatten(r["probs"][base, :])).astype(BF16)

    each(0, n, scale_rows)

    def owner_sums():
        crosses.arrive()
        cross = r["c_out"][me]
        for peer in crosses.peers:
            cross = cross + r["c_near"][peer]
        r["c_part"][...] = cross
        cross_x.start()
        grads.arrive()
        grad = r["g_own"][...]
        for peer in grads.peers:
            grad = grad + r["g_near"][peer].astype(F32)
        r["g_own"][...] = grad
        r["g_part"][...] = grad.astype(BF16)
        grad_x.start()

    def owner_grads():
        cross_x.arrive()
        cross = r["c_part"][...]
        for peer in cross_x.peers:
            cross = cross + r["c_far"][peer]
        mine = pl.ds(me * own, own)
        u = row_scale((r["weights"][mine, :] > 0).astype(F32), r["last"][mine, :])
        loss[...] = jnp.log(r["last"][pl.ds(dense + me * own, own), :]) - u * cross * (1.0 / LOG2E)
        grad_x.arrive()
        grad = r["g_own"][of_part(z), :]
        for peer in grad_x.peers:
            grad = grad + r["g_far"][peer].astype(F32)
        unit, inv = unit_rows(r["feats"][...])
        grad = grad * (1.0 / FOLD_S)
        inner = jnp.sum(unit * grad, axis=1, keepdims=True)
        grad_feats[of_part(z), :] = (inv * (grad - unit * inner)).astype(BF16)
        back_x.start()


    def out_copy(j):
        return pltpu.make_async_copy(
            r["stage"].at[lax.rem(j, 2)], grad_proto.at[:, of_block(j)], local.at[4 + lax.rem(j, 2)]
        )

    def column_grad(j):
        @pl.when(j >= 2)
        def _():
            out_copy(j - 2).wait()

        here = of_block(j)
        grad = jnp.dot(r["s_prob"][...], raised[:, here], preferred_element_type=F32) - jnp.dot(
            r["s_target"][...], expo[:, here], preferred_element_type=F32
        )
        inv = r["inverse"][0:1, here]
        unit = cols[:, here].astype(F32) * inv
        r["stage"][lax.rem(j, 2)] = (grad - unit * jnp.sum(unit * grad, axis=0, keepdims=True)) * inv
        out_copy(j).start()

    blocks = columns // block
    load_s.wait()
    each(0, blocks // 2, column_grad)
    owner_sums()
    for gather in w_later:
        gather.relay()
    each(blocks // 2, blocks, column_grad)
    owner_grads()

    for gather in w_later:
        gather.finish()

    for j in range(max(0, blocks - 2), blocks):
        out_copy(j).wait()
    per = block // width
    hidden_blocks = w_all.shape[1] // width
    whole_depth = w_all.shape[0]
    pieces = slab // LANES

    def hidden_block(b):
        pre = jnp.dot(rows_in[...], w_all[:, of_width(b)], preferred_element_type=F32)
        act, slope = gelu_parts(pre)
        raised[of_slot(b), 0:width] = act.astype(BF16)
        r["stage"][b // per, 0:CAP, of_width(lax.rem(b, per))] = slope

    each(0, hidden_blocks, hidden_block)

    def turn_tokens(k):
        expo[of_width(k), width : width + CAP] = rows_in[:, of_width(k)].astype(F32).T.astype(BF16)

    each(0, whole_depth // width, turn_tokens)
    own_live = (r["weights"][pl.ds(me * own, own), :] > 0).astype(F32)
    for start in range(0, patches, CAP):
        turned = pick[:, start : start + CAP].astype(F32).T
        acc_b[start : start + CAP, :] = (turned * flatten(own_live)).astype(BF16)

    for gather in [teach_g, weight_g, w_now, wo_g, stud_g] + w_later:
        gather.drain()
    for one in totals + [grads, crosses, feat_x, stud_x, grad_x, cross_x]:
        one.drain()
    back_x.arrive()
    back_x.drain()

    lane_in, lane_mid = width + CAP, 2 * width

    def back_block(b):
        grad_hidden = lax.dot_general(
            grad_feats[...], wo_all[of_width(b), :], (((1,), (1,)), ((), ())), preferred_element_type=F32
        )
        expo[of_slot(b), 0:width] = (grad_hidden * r["stage"][b // per, 0:CAP, of_width(lax.rem(b, per))]).astype(BF16)

    def out_block(b):
        raised[of_width(b), width : 2 * width] = lax.dot_general(
            raised[of_slot(b), 0:width], grad_feats[...], (((0,), (0,)), ((), ())), preferred_element_type=F32
        ).astype(BF16)

    side = lax.rem(me, 2)
    team = me // 2
    teams = [lax.rem(team + step, half) for step in range(1, half)]

    def pair_copy(q, h):
        lanes = slice(h * LANES, (h + 1) * LANES)
        return remote(
            expo.at[of_depth(2 * q + 1 - side), lane_in + h * LANES : lane_in + (h + 1) * LANES],
            r["wide_a"].at[q, :, lanes],
            r["wide_sems"].at[h, q],
            r["wide_sems"].at[pieces + h, q],
            {"dp": me + flip},
        )

    def team_copy(q, slot, h):
        lanes = slice(h * LANES, (h + 1) * LANES)
        return remote(
            raised.at[of_depth(q), lane_mid + h * LANES : lane_mid + (h + 1) * LANES],
            r["wide_b"].at[slot, :, lanes],
            r["wide_sems"].at[2 * pieces + h, q],
            r["wide_sems"].at[3 * pieces + h, slot],
            {"dp": 2 * q + side},
        )

    def own_term(q, h):
        lanes = slice(h * LANES, (h + 1) * LANES)
        mine = expo[of_depth(2 * q + side), lane_in + h * LANES : lane_in + (h + 1) * LANES]
        return mine.astype(F32) + r["wide_a"][q, :, lanes].astype(F32)

    def wide_lanes(s, h):
        return pl.ds(pl.multiple_of(s * slab + h * LANES, LANES), LANES)

    def wide_exchange(h):
        return Chain("tensor", m, lambda s: wide_out.at[:, wide_lanes(s, h)], *line(9 + h))

    wide_x = [wide_exchange(h) for h in range(pieces)]
    sub = tall // m
    narrow_n = Exchange(
        "dp",
        n,
        lambda p: raised.at[pl.ds(pl.multiple_of(p * tall + z * sub, sub), sub), width : 2 * width],
        lambda s: r["narrow_a"].at[s],
        *pair(10),
    )

    def of_sub(s):
        return pl.ds(pl.multiple_of(s * sub, sub), sub)

    narrow_x = Exchange("tensor", m, lambda p: narrow_out.at[of_sub(z), :], lambda s: narrow_out.at[of_sub(s), :], *line(8))

    for b in range(slab // width):
        mine = z * (slab // width) + b
        back_block(mine)

        def in_block(p):
            expo[of_depth(p), lane_in + b * width : lane_in + (b + 1) * width] = jnp.dot(
                expo[of_depth(p), width : width + CAP], expo[of_slot(mine), 0:width], preferred_element_type=F32
            ).astype(BF16)

        for q in teams + [team]:
            in_block(2 * q + 1 - side)
        for h in range(b * width // LANES, (b + 1) * width // LANES):
            for q in teams + [team]:
                pair_copy(q, h).start()
        for q in teams + [team]:
            in_block(2 * q + side)
    each(0, hidden_blocks, out_block)
    narrow_n.start()
    for h in range(pieces):
        for q in teams:
            pair_copy(q, h).wait_recv()
            raised[of_depth(q), lane_mid + h * LANES : lane_mid + (h + 1) * LANES] = own_term(q, h).astype(BF16)
            team_copy(q, team, h).start()
        pair_copy(team, h).wait_recv()
    each(0, hidden_blocks, back_block)
    for h in range(pieces):
        for q in teams:
            team_copy(q, q, h).wait_recv()
        total = own_term(team, h)
        for q in teams:
            total = total + r["wide_b"][q, :, h * LANES : (h + 1) * LANES].astype(F32)
        wide_out[:, wide_lanes(z, h)] = total.astype(BF16)
        wide_x[h].start()
    narrow_n.arrive()
    total = raised[pl.ds(pl.multiple_of(me * tall + z * sub, sub), sub), width : 2 * width].astype(F32)
    for peer in narrow_n.peers:
        total = total + r["narrow_a"][peer].astype(F32)
    narrow_out[of_sub(z), :] = total.astype(BF16)
    narrow_x.start()

    def token_slot(k):
        return pl.ds(pl.multiple_of(lax.rem(k, 2) * patches, patches), patches)

    def token_copy(k):
        return pltpu.make_async_copy(
            acc_a.at[token_slot(k), :], d_tokens.at[:, of_width(k)], local.at[6 + lax.rem(k, 2)]
        )

    def token_block(k):
        total = None
        for b in range(hidden_blocks):
            term = lax.dot_general(
                expo[b * CAP : (b + 1) * CAP, 0:width],
                w_all[of_width(k), b * width : (b + 1) * width],
                (((1,), (1,)), ((), ())),
                preferred_element_type=F32,
            )
            total = term if total is None else total + term
        @pl.when(k >= 2)
        def _():
            token_copy(k - 2).wait()

        acc_a[token_slot(k), :] = jnp.dot(
            acc_b[0:patches, :], total.astype(BF16), preferred_element_type=F32
        ).astype(BF16)
        token_copy(k).start()

    token_blocks = whole_depth // width
    for step in range(1, m):
        each(token_blocks * (step - 1) // (m - 1), token_blocks * step // (m - 1), token_block)
        for one in wide_x:
            one.relay(step)
    narrow_x.arrive()
    for one in wide_x + [narrow_n, narrow_x]:
        one.drain()
    for h in range(pieces):
        for q in teams:
            pair_copy(q, h).wait_send()
            team_copy(q, team, h).wait_send()
        pair_copy(team, h).wait_send()
    for k in range(max(0, token_blocks - 2), token_blocks):
        token_copy(k).wait()


def balance(groups, teach, weight, pick, tokens, w_in, w_out, proto_t, proto_s, ident):
    n, m = groups["dp"], groups["tensor"]
    rows, width = n * teach.shape[0], teach.shape[1]
    columns = proto_s.shape[1]
    depth, hidden = n * w_in.shape[0], w_in.shape[1]
    shapes = plan(groups, rows, columns, width, depth, hidden)
    vmem, hbm = pl.BlockSpec(memory_space=pltpu.VMEM), pl.BlockSpec(memory_space=pl.ANY)
    return pl.pallas_call(
        functools.partial(balance_kernel, groups, list(shapes)),
        name="balance",
        in_specs=[vmem, vmem, vmem, hbm, hbm, vmem, hbm, hbm],
        out_specs=[hbm, vmem, hbm, vmem, vmem],
        out_shape=[
            jax.ShapeDtypeStruct((width, columns), F32),
            jax.ShapeDtypeStruct((CAP // LANES, LANES), F32),
            jax.ShapeDtypeStruct(tokens.shape, BF16),
            jax.ShapeDtypeStruct((depth // n, hidden), BF16),
            jax.ShapeDtypeStruct((hidden // n, width), BF16),
        ],
        scratch_shapes=list(shapes.values()),
        compiler_params=pltpu.CompilerParams(
            collective_id=ident, has_side_effects=True, vmem_limit_bytes=62 * 1024 * 1024
        ),
    )(teach, weight, pick, tokens, w_in, w_out, proto_t, proto_s)


def selection(masks):
    crops, patches = masks.shape
    size = crops * patches
    flat = masks.reshape(1, size)
    before = (
        lax.broadcasted_iota(jnp.int32, (size, size), 0) < lax.broadcasted_iota(jnp.int32, (size, size), 1)
    ).astype(BF16)
    place = jnp.dot(flat.astype(BF16), before, preferred_element_type=F32).astype(jnp.int32)
    slots = lax.broadcasted_iota(jnp.int32, (CAP, size), 0)
    picked = (place == slots) & (flat > 0)
    dead = slots >= jnp.sum(flat)
    first = lax.broadcasted_iota(jnp.int32, (CAP, size), 1) == 0
    return (picked | (dead & first)).astype(BF16)


def shards(groups, tokens, teacher_feats, masks, w_in, w_out, proto_student, proto_teacher):
    pick = selection(masks)
    counts = jnp.sum(masks, axis=1)
    ends = jnp.sum(
        jnp.where(jnp.arange(counts.shape[0])[:, None] <= jnp.arange(counts.shape[0])[None, :], counts[:, None], 0),
        axis=0,
    )
    slot = jnp.arange(CAP)[:, None]
    member = ((slot >= (ends - counts)[None, :]) & (slot < ends[None, :])).astype(F32)
    inverse = 1.0 / jnp.maximum(counts, 1).astype(F32)
    weight = (GRAD_SCALE * jnp.sum(member * inverse[None, :], axis=1)).astype(BF16)
    teacher_pick = jnp.dot(pick, teacher_feats, preferred_element_type=F32)
    teacher_rows = (unit_rows(teacher_pick)[0] * FOLD_T).astype(BF16)
    grad_proto, row_loss, d_tokens, wide, narrow = balance(
        groups, teacher_rows, weight.astype(F32).reshape(-1, LANES), pick, tokens, w_in, w_out, proto_teacher, proto_student, 0
    )
    crop_loss = jnp.sum(member * row_loss.reshape(CAP)[:, None], axis=0) * inverse
    grad_in = wide.astype(F32)
    grad_out = narrow.astype(F32)
    return (d_tokens, grad_in, grad_out, grad_proto, crop_loss)


def solution(mesh):
    groups = {"dp": mesh.shape["dp"], "tensor": mesh.shape["tensor"]}
    placed = (
        P("dp", None),
        P("dp", None),
        P("dp", None),
        P("dp", None),
        P("dp", None),
        P(None, ("dp", "tensor")),
        P(None, ("dp", "tensor")),
    )
    return jax.shard_map(
        functools.partial(shards, groups),
        mesh=mesh,
        in_specs=placed,
        out_specs=(P("dp", None), P("dp", None), P("dp", None), P(None, ("dp", "tensor")), P("dp")),
        check_vma=False,
    )
```

```python
import functools

import jax
import jax.numpy as jnp
from jax import lax
from jax.experimental import pallas as pl
from jax.experimental.pallas import tpu as pltpu
from jax.sharding import PartitionSpec as P

ROUNDS = 3
CAP = 256

TEACHER_TEMP = 0.07
STUDENT_TEMP = 0.1
EPS = 1e-06
GRAD_SCALE = 65536.0
LOG2E = 1.4426950408889634
LANES = 128
BLOCK = 1024
ROW_TILE = 64
MESH = pl.DeviceIdType.MESH
F32 = jnp.float32
BF16 = jnp.bfloat16


def gelu_parts(pre):
    cdf = 0.5 * (1.0 + lax.erf(pre * 0.7071067811865476))
    pdf = jnp.exp(-0.5 * pre * pre) * 0.3989422804014327
    return (pre * cdf, cdf + pre * pdf)


def unit_rows(feats):
    inverse = lax.rsqrt(jnp.sum(feats * feats, axis=1, keepdims=True) + EPS)
    return (feats * inverse, inverse)


def unit_columns(protos):
    wide = protos.astype(F32)
    norms = jnp.sqrt(jnp.sum(wide * wide, axis=0, keepdims=True) + EPS)
    return (wide / norms, norms)


def spread(dense, out_ref):
    for c in range(dense.shape[0]):
        row = jnp.broadcast_to(dense[c : c + 1, :], (LANES, LANES))
        out_ref[c * LANES : (c + 1) * LANES, :] = row.T


def gathered(acc_ref, out_ref, base):
    for c in range(acc_ref.shape[0] // LANES):
        turned = acc_ref[c * LANES : (c + 1) * LANES, :].T
        out_ref[base + c : base + c + 1, :] = jnp.sum(turned, axis=0, keepdims=True)


def fold_lanes(values):
    total = values[:, :LANES]
    for start in range(LANES, values.shape[1], LANES):
        total = total + values[:, start : start + LANES]
    return total


def widen(values, cols):
    return jnp.concatenate([values] * (cols // LANES), axis=1)


def two_terms(row):
    high = row.astype(BF16)
    low = (row - high.astype(F32)).astype(BF16)
    return jnp.concatenate([high, low, jnp.zeros((14, row.shape[1]), BF16)], axis=0)


def flatten(dense):
    return jnp.concatenate([dense[c : c + 1, :] for c in range(dense.shape[0])], axis=1)


def row_scale(live, row_sum):
    return live / (row_sum + 1.0 - live)


def greet(groups, many):
    barrier = pltpu.get_barrier_semaphore()
    for axis in ("dp", "tensor"):
        me = lax.axis_index(axis)
        for step in range(1, groups[axis]):
            peer = lax.rem(me + step, groups[axis])
            pl.semaphore_signal(barrier, inc=1, device_id={axis: peer}, device_id_type=MESH)
    pl.semaphore_wait(barrier, many)


def remote(source, target, send, recv, where):
    return pltpu.make_async_remote_copy(
        src_ref=source, dst_ref=target, send_sem=send, recv_sem=recv, device_id=where, device_id_type=MESH
    )


class PairGather:
    def __init__(self, n, own, slot, send, recv):
        self.me = lax.axis_index("dp")
        self.flip = 1 - 2 * lax.rem(self.me, 2)
        self.partner = self.me + self.flip
        self.peers = [lax.rem(self.me + step, n) for step in range(2, n, 2)]
        self.own, self.slot, self.send, self.recv = own, slot, send, recv

    def copy(self, source, slot, sender, peer):
        return remote(source, self.slot(slot), self.send.at[sender], self.recv.at[slot], {"dp": peer})

    def start(self):
        for peer in self.peers + [self.partner]:
            self.copy(self.own, self.me, peer, peer).start()

    def arrive(self, slot):
        self.copy(self.own, slot, slot, slot).wait_recv()

    def forward(self, peer):
        self.copy(self.slot(peer), peer, peer + self.flip, self.partner).start()

    def relay(self):
        for peer in self.peers:
            self.arrive(peer)
            self.forward(peer)

    def finish(self):
        self.arrive(self.partner)
        for peer in self.peers:
            self.arrive(peer + self.flip)

    def drain(self):
        for peer in self.peers:
            self.copy(self.own, self.me, peer, peer).wait_send()
            self.copy(self.slot(peer), peer, peer + self.flip, self.partner).wait_send()
        self.copy(self.own, self.me, self.partner, self.partner).wait_send()


class Exchange:
    def __init__(self, axis, n, source, landing, send, recv):
        self.me = lax.axis_index(axis)
        self.axis, self.source, self.landing, self.send, self.recv = axis, source, landing, send, recv
        self.peers = [lax.rem(self.me + step, n) for step in range(1, n)]

    def copy(self, peer, slot):
        return remote(self.source(peer), self.landing(slot), self.send.at[peer], self.recv.at[slot], {self.axis: peer})

    def start(self):
        for peer in self.peers:
            self.copy(peer, self.me).start()

    def arrive(self):
        for peer in self.peers:
            self.copy(peer, peer).wait_recv()

    def drain(self):
        for peer in self.peers:
            self.copy(peer, self.me).wait_send()


class Chain:
    def __init__(self, axis, n, block, send, recv):
        self.me = lax.axis_index(axis)
        self.axis, self.n, self.block, self.send, self.recv = axis, n, block, send, recv

    def copy(self, step, way):
        index = lax.rem(self.me - way * step + self.n, self.n)
        peer = lax.rem(self.me + way + self.n, self.n)
        ref = self.block(index)
        send = self.send.at[self.n if step == 0 and way < 0 else index]
        return remote(ref, ref, send, self.recv.at[index], {self.axis: peer})

    def held(self, step, way):
        index = self.me - way * step
        return (index >= 0) & (index < self.n)

    def each_way(self, step, arrive, send, done):
        for way in (1, -1):
            held = self.held(step, way)
            beyond = self.me + way
            onward = held & (beyond >= 0) & (beyond < self.n)
            if arrive:
                pl.when(held)(lambda way=way: self.copy(step, way).wait_recv())
            if send:
                pl.when(onward)(lambda way=way: self.copy(step, way).start())
            if done:
                pl.when(onward)(lambda way=way: self.copy(step, way).wait_send())

    def start(self):
        self.each_way(0, False, True, False)

    def relay(self, step):
        self.each_way(step, True, step < self.n - 1, False)

    def drain(self):
        for step in range(self.n - 1):
            self.each_way(step, False, False, True)


class Total:
    def __init__(self, n, m, value, near, part, far, sems_n, sems_m):
        self.n, self.m = n, m
        self.value, self.near, self.part, self.far = value, near, part, far
        self.first = Exchange("dp", n, lambda peer: value, lambda slot: near.at[slot], *sems_n)
        self.second = Exchange("tensor", m, lambda peer: part, lambda slot: far.at[slot], *sems_m)

    def start(self):
        self.first.start()
        self.near[self.first.me] = self.value[...]

    def turn(self):
        self.first.arrive()
        total = self.near[0]
        for slot in range(1, self.n):
            total = total + self.near[slot]
        self.part[...] = total
        self.second.start()
        self.far[self.second.me] = total

    def finish(self):
        self.second.arrive()
        total = self.far[0]
        for slot in range(1, self.m):
            total = total + self.far[slot]
        return total

    def drain(self):
        self.first.drain()
        self.second.drain()


def plan(groups, rows, columns, width, depth, hidden):
    n, m = groups["dp"], groups["tensor"]
    dense = rows // LANES
    own = CAP // LANES
    part = CAP // m
    block = min(BLOCK, columns)
    vmem = pltpu.VMEM
    shapes = dict(
        expo=vmem((rows, columns), BF16),
        raised=vmem((rows, columns), BF16),
        cols=vmem((width, columns), BF16),
        teach=vmem((n, CAP, width), BF16),
        weight=vmem((n, own, LANES), F32),
        weights=vmem((dense, LANES), F32),
        rows_in=vmem((CAP, depth), BF16),
        w_all=vmem((depth, hidden), BF16),
        wo_all=vmem((hidden, width), BF16),
        featp=vmem((CAP, width), F32),
        grad_feats=vmem((CAP, width), BF16),
        near_f=vmem((m, part, width), F32),
        feats=vmem((part, width), F32),
        stud=vmem((n, CAP, width), BF16),
        s_prob=vmem((width, rows), BF16),
        s_target=vmem((width, rows), BF16),
        acc_a=vmem((rows, width), BF16),
        acc_b=vmem((rows, width), BF16),
        g_own=vmem((CAP, width), F32),
        g_near=vmem((n, CAP, width), BF16),
        g_part=vmem((CAP, width), BF16),
        g_far=vmem((m, part, width), BF16),
        c_out=vmem((n, own, LANES), F32),
        c_near=vmem((n, own, LANES), F32),
        c_part=vmem((own, LANES), F32),
        c_far=vmem((m, own, LANES), F32),
        colacc=vmem((8, columns), F32),
        scale=vmem((8, columns), F32),
        inverse=vmem((8, columns), F32),
        u_terms=vmem((16, rows), BF16),
        acc=vmem((CAP, LANES), F32),
        spread_a=vmem((CAP, LANES), F32),
        spread_b=vmem((CAP, LANES), F32),
        probs=vmem((dense, LANES), F32),
        targets=vmem((dense, LANES), F32),
        last=vmem((2 * dense, LANES), F32),
        stage=vmem((2, max(width, CAP), block), F32),
        wide_a=vmem((n // 2, depth // n, hidden // m), BF16),
        wide_b=vmem((n // 2, depth // n, hidden // m), BF16),
        narrow_a=vmem((n, hidden // n // m, width), BF16),
        wide_sems=pltpu.SemaphoreType.DMA((4 * (hidden // m // LANES), n)),
        pair_send=pltpu.SemaphoreType.DMA((11 + m, n)),
        pair_recv=pltpu.SemaphoreType.DMA((11 + m, n)),
        line_send=pltpu.SemaphoreType.DMA((9 + hidden // m // LANES, m + 1)),
        line_recv=pltpu.SemaphoreType.DMA((9 + hidden // m // LANES, m + 1)),
        local=pltpu.SemaphoreType.DMA((8 + depth // width,)),
    )
    for turn in range(ROUNDS):
        size = 2 * dense if turn == ROUNDS - 1 else dense
        shapes[f"value{turn}"] = vmem((size, LANES), F32)
        shapes[f"near{turn}"] = vmem((n, size, LANES), F32)
        shapes[f"part{turn}"] = vmem((size, LANES), F32)
        shapes[f"far{turn}"] = vmem((m, size, LANES), F32)
    return shapes


FOLD_T = LOG2E / TEACHER_TEMP
FOLD_S = LOG2E / STUDENT_TEMP


def balance_kernel(groups, names, *refs):
    n, m = groups["dp"], groups["tensor"]
    teach_own, weight_own, pick, tokens, w_in, w_out, proto_t, proto_s = refs[:8]
    grad_proto, loss, d_tokens, wide_out, narrow_out = refs[8:13]
    r = dict(zip(names, refs[13:]))
    rows_in = r["rows_in"]
    expo, raised, cols, w_all, wo_all, grad_feats = (
        r["expo"], r["raised"], r["cols"], r["w_all"], r["wo_all"], r["grad_feats"]
    )
    teach, weight, stud, acc, scale = r["teach"], r["weight"], r["stud"], r["acc"], r["scale"]
    acc_a, acc_b, local = r["acc_a"], r["acc_b"], r["local"]
    rows, columns = expo.shape
    width = cols.shape[0]
    dense = rows // LANES
    own = CAP // LANES
    block = r["stage"].shape[2]
    depth = w_in.shape[0]
    slab = w_all.shape[1] // m
    part = CAP // m
    me, z = lax.axis_index("dp"), lax.axis_index("tensor")
    half = n // 2
    flip = 1 - 2 * lax.rem(me, 2)

    def pair(k):
        return r["pair_send"].at[k], r["pair_recv"].at[k]

    def line(k):
        return r["line_send"].at[k], r["line_recv"].at[k]

    def place(step):
        return lax.rem(me + 2 * lax.rem(step, half), n) + flip * (step // half)

    def of_block(j):
        if isinstance(j, int):
            return slice(j * block, (j + 1) * block)
        return pl.ds(pl.multiple_of(j * block, block), block)

    def of_slot(slot):
        return pl.ds(pl.multiple_of(slot * CAP, CAP), CAP)

    def each(low, high, body, unroll=1):
        def step(j, carry):
            body(j)
            return carry

        lax.fori_loop(low, high, step, 0, unroll=unroll)

    teach_g = PairGather(n, teach_own, lambda s: teach.at[s], *pair(0))
    weight_g = PairGather(n, weight_own, lambda s: weight.at[s], *pair(1))

    def of_slab(k):
        return pl.ds(pl.multiple_of(k * slab, slab), slab)

    def of_depth(slot):
        return pl.ds(pl.multiple_of(slot * depth, depth), depth)

    def w_gather(k, index):
        lanes = of_slab(k)
        return PairGather(n, w_all.at[of_depth(me), lanes], lambda s: w_all.at[of_depth(s), lanes], *pair(index))

    w_now = w_gather(z, 2)
    w_later = [w_gather(lax.rem(z + k, m), 10 + k) for k in range(1, m)]
    tall = w_out.shape[0]
    wo_g = PairGather(n, w_out, lambda s: wo_all.at[pl.ds(pl.multiple_of(s * tall, tall), tall), :], *pair(3))
    stud_g = PairGather(n, stud.at[me], lambda s: stud.at[s], *pair(4))
    totals = [
        Total(n, m, r[f"value{k}"], r[f"near{k}"], r[f"part{k}"], r[f"far{k}"], pair(5 + k), line(2 + k))
        for k in range(ROUNDS)
    ]
    grads = Exchange("dp", n, lambda p: acc_a.at[of_slot(p), :], lambda s: r["g_near"].at[s], *pair(8))
    crosses = Exchange("dp", n, lambda p: r["c_out"].at[p], lambda s: r["c_near"].at[s], *pair(9))

    def of_part(k):
        return pl.ds(pl.multiple_of(k * part, part), part)

    feat_x = Exchange("tensor", m, lambda p: r["featp"].at[of_part(p), :], lambda s: r["near_f"].at[s], *line(0))
    stud_x = Exchange(
        "tensor", m, lambda p: stud.at[me, of_part(z), :], lambda s: stud.at[me, of_part(s), :], *line(1)
    )
    grad_x = Exchange("tensor", m, lambda p: r["g_part"].at[of_part(p), :], lambda s: r["g_far"].at[s], *line(5))
    cross_x = Exchange("tensor", m, lambda p: r["c_part"], lambda s: r["c_far"].at[s], *line(6))
    back_x = Exchange(
        "tensor", m, lambda p: grad_feats.at[of_part(z), :], lambda s: grad_feats.at[of_part(s), :], *line(7)
    )

    def unit_cols(factor, keep):
        def one(j):
            here = of_block(j)
            wide = cols[:, here].astype(F32)
            inv = 1.0 / jnp.sqrt(jnp.sum(wide * wide, axis=0, keepdims=True) + EPS)
            if keep is not None:
                keep[:, here] = jnp.broadcast_to(inv, (8, block))
            cols[:, here] = (wide * (inv * factor)).astype(BF16)

        each(0, columns // block, one)

    def teacher_chunk(slot):
        bias = jnp.where(weight[slot] > 0, 0.0, -1e4)
        spread(bias, r["spread_a"])

        def one(j):
            here = of_block(j)
            dots = jnp.dot(teach[slot], cols[:, here], preferred_element_type=F32)
            power = jnp.exp2(dots + widen(r["spread_a"][...], block))
            expo[of_slot(slot), here] = power.astype(BF16)
            total = power[:8, :]
            for start in range(8, CAP, 8):
                total = total + power[start : start + 8, :]
            r["colacc"][:, here] += total

        for j in range(columns // block):
            one(j)

    def row_pass(store, out):
        def one(k):
            def tile(i):
                here = pl.ds(pl.multiple_of(k * CAP + i * ROW_TILE, ROW_TILE), ROW_TILE)
                total = None
                for start in range(0, columns, LANES):
                    lanes = slice(start, start + LANES)
                    value = expo[here, lanes].astype(F32) * jnp.concatenate([scale[:, lanes]] * (ROW_TILE // 8), axis=0)
                    if store:
                        expo[here, lanes] = value.astype(BF16)
                    total = value if total is None else total + value
                acc[pl.ds(pl.multiple_of(i * ROW_TILE, ROW_TILE), ROW_TILE), :] = total

            each(0, CAP // ROW_TILE, tile, 2)
            gather_rows(out, k * own)

        each(0, n, one)

    def gather_rows(out, base):
        for c in range(own):
            turned = acc[c * LANES : (c + 1) * LANES, :].T
            out[pl.ds(base + c, 1), :] = jnp.sum(turned, axis=0, keepdims=True)

    def column_pass(u):
        r["u_terms"][...] = two_terms(flatten(u))

        def one(j):
            here = of_block(j)
            total = jnp.dot(r["u_terms"][...], expo[:, here], preferred_element_type=F32)
            scale[:, here] = jnp.broadcast_to(1.0 / (total[0:1, :] + total[1:2, :]), (8, block))

        for j in range(columns // block):
            one(j)

    def student_chunk(slot):
        acc[...] = jnp.zeros_like(acc)

        def one(j):
            here = of_block(j)
            for start in range(0, block, width):
                lanes = slice(j * block + start, j * block + start + width)
                power = jnp.exp2(jnp.dot(stud[slot], cols[:, lanes], preferred_element_type=F32))
                raised[of_slot(slot), lanes] = power.astype(BF16)
                acc[...] += fold_lanes(power)

        for j in range(columns // block):
            one(j)
        gather_rows(r[f"value{ROUNDS - 1}"], dense + slot * own)
        acc_a[of_slot(slot), :] = lax.dot_general(
            raised[of_slot(slot), :], cols[...], (((1,), (1,)), ((), ())), preferred_element_type=F32
        ).astype(BF16)

    def student_own():
        feat_x.arrive()
        feats = r["featp"][of_part(z), :]
        for peer in feat_x.peers:
            feats = feats + r["near_f"][peer]
        r["feats"][...] = feats
        stud[me, of_part(z), :] = unit_rows(feats)[0].astype(BF16)
        stud_x.start()

    def target_chunk(slot):
        term = lax.dot_general(
            expo[of_slot(slot), :], cols[...], (((1,), (1,)), ((), ())), preferred_element_type=F32
        )
        acc_b[of_slot(slot), :] = term.astype(BF16)
        acc[...] = fold_lanes(stud[slot].astype(F32) * term)
        gather_rows(r["c_out"].at[slot], 0)

    load_t = pltpu.make_async_copy(proto_t, cols, local.at[0])
    load_s = pltpu.make_async_copy(proto_s, cols, local.at[1])
    load_w = pltpu.make_async_copy(w_in, w_all.at[of_depth(me), :], local.at[2])
    load_w.start()
    load_t.start()
    patches = tokens.shape[0]
    in_row = block // width

    def of_width(k):
        if isinstance(k, int):
            return slice(k * width, (k + 1) * width)
        return pl.ds(pl.multiple_of(k * width, width), width)

    def token_home(k):
        return slice(k // in_row * patches, (k // in_row + 1) * patches), of_width(k % in_row)

    token_loads = [
        pltpu.make_async_copy(tokens.at[:, of_width(k)], raised.at[token_home(k)], local.at[8 + k])
        for k in range(w_all.shape[0] // width)
    ]
    for load in token_loads:
        load.start()
    greet(groups, n + m - 2)
    teach_g.start()
    weight_g.start()
    teach[me] = teach_own[...]
    weight[me] = weight_own[...]
    wo_all[pl.ds(pl.multiple_of(me * tall, tall), tall), :] = w_out[...]
    r["colacc"][...] = jnp.zeros_like(r["colacc"])
    load_t.wait()
    unit_cols(1.0, None)
    teacher_chunk(me)
    for k, load in enumerate(token_loads):
        load.wait()
        rows_in[:, of_width(k)] = jnp.dot(pick[...], raised[token_home(k)], preferred_element_type=F32).astype(BF16)
    teach_g.relay()
    weight_g.relay()
    load_w.wait()
    w_now.start()
    wo_g.start()
    each(1, half, lambda step: teacher_chunk(place(step)))

    def teacher_late(step):
        teach_g.arrive(place(step))
        weight_g.arrive(place(step))
        teacher_chunk(place(step))

    each(half, n, teacher_late)
    load_s.start()
    weights = jnp.concatenate([weight[slot] for slot in range(n)], axis=0)
    r["weights"][...] = weights
    live = (weights > 0).astype(F32)
    scale[...] = jnp.broadcast_to(1.0 / jnp.sum(r["colacc"][...], axis=0, keepdims=True), scale.shape)
    row_pass(False, r["value0"])
    totals[0].start()

    load_s.wait()
    unit_cols(FOLD_S, r["inverse"])
    w_now.relay()
    wo_g.relay()
    totals[0].turn()
    w_now.finish()
    wo_g.finish()
    pre = jnp.dot(rows_in[...], w_all[:, of_slab(z)], preferred_element_type=F32)
    hidden = gelu_parts(pre)[0].astype(BF16)
    r["featp"][...] = jnp.dot(hidden, wo_all[of_slab(z), :], preferred_element_type=F32)
    feat_x.start()
    total = totals[0].finish()
    for turn in range(1, ROUNDS - 1):
        column_pass(row_scale(live, total))
        if turn == ROUNDS - 2:
            student_own()
        row_pass(False, r[f"value{turn}"])
        totals[turn].start()
        if turn < ROUNDS - 2:
            totals[turn].turn()
            total = totals[turn].finish()
    stud_x.arrive()
    stud_g.start()
    student_chunk(me)
    stud_g.relay()
    totals[ROUNDS - 2].turn()
    each(1, half, lambda step: student_chunk(place(step)))
    stud_g.finish()
    for gather in w_later:
        gather.start()
    each(half, n, lambda step: student_chunk(place(step)))
    total = totals[ROUNDS - 2].finish()
    column_pass(row_scale(live, total))
    row_pass(True, r[f"value{ROUNDS - 1}"])
    final = totals[ROUNDS - 1]
    final.start()

    def turn_rows(slot):
        r["s_prob"][:, of_slot(slot)] = stud[slot].astype(F32).T.astype(BF16)

    each(0, n, turn_rows, 2)
    each(0, half, target_chunk)
    final.turn()
    each(half, n, target_chunk)
    load_s.start()
    crosses.start()
    sums = final.finish()
    r["last"][...] = sums
    live = (r["weights"][...] > 0).astype(F32)
    factor = r["weights"][...] * (1.0 / STUDENT_TEMP)
    u = row_scale(live, sums[:dense])
    r["probs"][...] = factor / sums[dense:]
    r["targets"][...] = factor * u

    def mix(slot):
        spread(r["probs"][pl.ds(slot * own, own), :], r["spread_a"])
        spread(r["targets"][pl.ds(slot * own, own), :], r["spread_b"])
        return acc_a[of_slot(slot), :].astype(F32) * widen(r["spread_a"][...], width) - acc_b[
            of_slot(slot), :
        ].astype(F32) * widen(r["spread_b"][...], width)

    def send_mix(step):
        peer = lax.rem(me + step, n)
        acc_a[of_slot(peer), :] = mix(peer).astype(BF16)
        grads.copy(peer, me).start()

    each(1, n, send_mix)
    r["g_own"][...] = mix(me)

    def scale_rows(slot):
        here = of_slot(slot)
        turned = r["s_prob"][:, here].astype(F32)
        base = pl.ds(slot * own, own)
        r["s_target"][:, here] = (turned * flatten(r["targets"][base, :])).astype(BF16)
        r["s_prob"][:, here] = (turned * flatten(r["probs"][base, :])).astype(BF16)

    each(0, n, scale_rows)

    def owner_sums():
        crosses.arrive()
        cross = r["c_out"][me]
        for peer in crosses.peers:
            cross = cross + r["c_near"][peer]
        r["c_part"][...] = cross
        cross_x.start()
        grads.arrive()
        grad = r["g_own"][...]
        for peer in grads.peers:
            grad = grad + r["g_near"][peer].astype(F32)
        r["g_own"][...] = grad
        r["g_part"][...] = grad.astype(BF16)
        grad_x.start()

    def owner_grads():
        cross_x.arrive()
        cross = r["c_part"][...]
        for peer in cross_x.peers:
            cross = cross + r["c_far"][peer]
        mine = pl.ds(me * own, own)
        u = row_scale((r["weights"][mine, :] > 0).astype(F32), r["last"][mine, :])
        loss[...] = jnp.log(r["last"][pl.ds(dense + me * own, own), :]) - u * cross * (1.0 / LOG2E)
        grad_x.arrive()
        grad = r["g_own"][of_part(z), :]
        for peer in grad_x.peers:
            grad = grad + r["g_far"][peer].astype(F32)
        unit, inv = unit_rows(r["feats"][...])
        grad = grad * (1.0 / FOLD_S)
        inner = jnp.sum(unit * grad, axis=1, keepdims=True)
        grad_feats[of_part(z), :] = (inv * (grad - unit * inner)).astype(BF16)
        back_x.start()


    def out_copy(j):
        return pltpu.make_async_copy(
            r["stage"].at[lax.rem(j, 2)], grad_proto.at[:, of_block(j)], local.at[4 + lax.rem(j, 2)]
        )

    def column_grad(j):
        @pl.when(j >= 2)
        def _():
            out_copy(j - 2).wait()

        here = of_block(j)
        grad = jnp.dot(r["s_prob"][...], raised[:, here], preferred_element_type=F32) - jnp.dot(
            r["s_target"][...], expo[:, here], preferred_element_type=F32
        )
        inv = r["inverse"][0:1, here]
        unit = cols[:, here].astype(F32) * inv
        r["stage"][lax.rem(j, 2)] = (grad - unit * jnp.sum(unit * grad, axis=0, keepdims=True)) * inv
        out_copy(j).start()

    blocks = columns // block
    load_s.wait()
    each(0, blocks // 2, column_grad)
    owner_sums()
    for gather in w_later:
        gather.relay()
    each(blocks // 2, blocks, column_grad)
    owner_grads()

    for gather in w_later:
        gather.finish()

    for j in range(max(0, blocks - 2), blocks):
        out_copy(j).wait()
    per = block // width
    hidden_blocks = w_all.shape[1] // width
    whole_depth = w_all.shape[0]
    pieces = slab // LANES

    def hidden_block(b):
        pre = jnp.dot(rows_in[...], w_all[:, of_width(b)], preferred_element_type=F32)
        act, slope = gelu_parts(pre)
        raised[of_slot(b), 0:width] = act.astype(BF16)
        r["stage"][b // per, 0:CAP, of_width(lax.rem(b, per))] = slope

    each(0, hidden_blocks, hidden_block, 2)

    def turn_tokens(k):
        expo[of_width(k), width : width + CAP] = rows_in[:, of_width(k)].astype(F32).T.astype(BF16)

    each(0, whole_depth // width, turn_tokens)
    own_live = (r["weights"][pl.ds(me * own, own), :] > 0).astype(F32)
    for start in range(0, patches, CAP):
        turned = pick[:, start : start + CAP].astype(F32).T
        acc_b[start : start + CAP, :] = (turned * flatten(own_live)).astype(BF16)

    for gather in [teach_g, weight_g, w_now, wo_g, stud_g] + w_later:
        gather.drain()
    for one in totals + [grads, crosses, feat_x, stud_x, grad_x, cross_x]:
        one.drain()
    back_x.arrive()
    back_x.drain()

    lane_in, lane_mid = width + CAP, 2 * width

    def back_block(b):
        grad_hidden = lax.dot_general(
            grad_feats[...], wo_all[of_width(b), :], (((1,), (1,)), ((), ())), preferred_element_type=F32
        )
        expo[of_slot(b), 0:width] = (grad_hidden * r["stage"][b // per, 0:CAP, of_width(lax.rem(b, per))]).astype(BF16)

    def out_block(b):
        raised[of_width(b), width : 2 * width] = lax.dot_general(
            raised[of_slot(b), 0:width], grad_feats[...], (((0,), (0,)), ((), ())), preferred_element_type=F32
        ).astype(BF16)

    side = lax.rem(me, 2)
    team = me // 2
    teams = [lax.rem(team + step, half) for step in range(1, half)]

    def pair_copy(q, h):
        lanes = slice(h * LANES, (h + 1) * LANES)
        return remote(
            expo.at[of_depth(2 * q + 1 - side), lane_in + h * LANES : lane_in + (h + 1) * LANES],
            r["wide_a"].at[q, :, lanes],
            r["wide_sems"].at[h, q],
            r["wide_sems"].at[pieces + h, q],
            {"dp": me + flip},
        )

    def team_copy(q, slot, h):
        lanes = slice(h * LANES, (h + 1) * LANES)
        return remote(
            raised.at[of_depth(q), lane_mid + h * LANES : lane_mid + (h + 1) * LANES],
            r["wide_b"].at[slot, :, lanes],
            r["wide_sems"].at[2 * pieces + h, q],
            r["wide_sems"].at[3 * pieces + h, slot],
            {"dp": 2 * q + side},
        )

    def own_term(q, h):
        lanes = slice(h * LANES, (h + 1) * LANES)
        mine = expo[of_depth(2 * q + side), lane_in + h * LANES : lane_in + (h + 1) * LANES]
        return mine.astype(F32) + r["wide_a"][q, :, lanes].astype(F32)

    def wide_lanes(s, h):
        return pl.ds(pl.multiple_of(s * slab + h * LANES, LANES), LANES)

    def wide_exchange(h):
        return Chain("tensor", m, lambda s: wide_out.at[:, wide_lanes(s, h)], *line(9 + h))

    wide_x = [wide_exchange(h) for h in range(pieces)]
    sub = tall // m
    narrow_n = Exchange(
        "dp",
        n,
        lambda p: raised.at[pl.ds(pl.multiple_of(p * tall + z * sub, sub), sub), width : 2 * width],
        lambda s: r["narrow_a"].at[s],
        *pair(10),
    )

    def of_sub(s):
        return pl.ds(pl.multiple_of(s * sub, sub), sub)

    narrow_x = Exchange("tensor", m, lambda p: narrow_out.at[of_sub(z), :], lambda s: narrow_out.at[of_sub(s), :], *line(8))

    for b in range(slab // width):
        mine = z * (slab // width) + b
        back_block(mine)

        def in_block(p):
            expo[of_depth(p), lane_in + b * width : lane_in + (b + 1) * width] = jnp.dot(
                expo[of_depth(p), width : width + CAP], expo[of_slot(mine), 0:width], preferred_element_type=F32
            ).astype(BF16)

        for q in teams + [team]:
            in_block(2 * q + 1 - side)
        for h in range(b * width // LANES, (b + 1) * width // LANES):
            for q in teams + [team]:
                pair_copy(q, h).start()
        for q in teams + [team]:
            in_block(2 * q + side)
    each(0, hidden_blocks, out_block, 2)
    narrow_n.start()
    for h in range(pieces):
        for q in teams:
            pair_copy(q, h).wait_recv()
            raised[of_depth(q), lane_mid + h * LANES : lane_mid + (h + 1) * LANES] = own_term(q, h).astype(BF16)
            team_copy(q, team, h).start()
        pair_copy(team, h).wait_recv()
    each(0, hidden_blocks, back_block, 2)
    for h in range(pieces):
        for q in teams:
            team_copy(q, q, h).wait_recv()
        total = own_term(team, h)
        for q in teams:
            total = total + r["wide_b"][q, :, h * LANES : (h + 1) * LANES].astype(F32)
        wide_out[:, wide_lanes(z, h)] = total.astype(BF16)
        wide_x[h].start()
    narrow_n.arrive()
    total = raised[pl.ds(pl.multiple_of(me * tall + z * sub, sub), sub), width : 2 * width].astype(F32)
    for peer in narrow_n.peers:
        total = total + r["narrow_a"][peer].astype(F32)
    narrow_out[of_sub(z), :] = total.astype(BF16)
    narrow_x.start()

    def token_slot(k):
        return pl.ds(pl.multiple_of(lax.rem(k, 2) * patches, patches), patches)

    def token_copy(k):
        return pltpu.make_async_copy(
            acc_a.at[token_slot(k), :], d_tokens.at[:, of_width(k)], local.at[6 + lax.rem(k, 2)]
        )

    def token_block(k):
        total = None
        for b in range(hidden_blocks):
            term = lax.dot_general(
                expo[b * CAP : (b + 1) * CAP, 0:width],
                w_all[of_width(k), b * width : (b + 1) * width],
                (((1,), (1,)), ((), ())),
                preferred_element_type=F32,
            )
            total = term if total is None else total + term
        @pl.when(k >= 2)
        def _():
            token_copy(k - 2).wait()

        acc_a[token_slot(k), :] = jnp.dot(
            acc_b[0:patches, :], total.astype(BF16), preferred_element_type=F32
        ).astype(BF16)
        token_copy(k).start()

    token_blocks = whole_depth // width
    for step in range(1, m):
        each(token_blocks * (step - 1) // (m - 1), token_blocks * step // (m - 1), token_block)
        for one in wide_x:
            one.relay(step)
    narrow_x.arrive()
    for one in wide_x + [narrow_n, narrow_x]:
        one.drain()
    for h in range(pieces):
        for q in teams:
            pair_copy(q, h).wait_send()
            team_copy(q, team, h).wait_send()
        pair_copy(team, h).wait_send()
    for k in range(max(0, token_blocks - 2), token_blocks):
        token_copy(k).wait()


def balance(groups, teach, weight, pick, tokens, w_in, w_out, proto_t, proto_s, ident):
    n, m = groups["dp"], groups["tensor"]
    rows, width = n * teach.shape[0], teach.shape[1]
    columns = proto_s.shape[1]
    depth, hidden = n * w_in.shape[0], w_in.shape[1]
    shapes = plan(groups, rows, columns, width, depth, hidden)
    vmem, hbm = pl.BlockSpec(memory_space=pltpu.VMEM), pl.BlockSpec(memory_space=pl.ANY)
    return pl.pallas_call(
        functools.partial(balance_kernel, groups, list(shapes)),
        name="balance",
        in_specs=[vmem, vmem, vmem, hbm, hbm, vmem, hbm, hbm],
        out_specs=[hbm, vmem, hbm, vmem, vmem],
        out_shape=[
            jax.ShapeDtypeStruct((width, columns), F32),
            jax.ShapeDtypeStruct((CAP // LANES, LANES), F32),
            jax.ShapeDtypeStruct(tokens.shape, BF16),
            jax.ShapeDtypeStruct((depth // n, hidden), BF16),
            jax.ShapeDtypeStruct((hidden // n, width), BF16),
        ],
        scratch_shapes=list(shapes.values()),
        compiler_params=pltpu.CompilerParams(
            collective_id=ident, has_side_effects=True, vmem_limit_bytes=62 * 1024 * 1024
        ),
    )(teach, weight, pick, tokens, w_in, w_out, proto_t, proto_s)


def selection(masks):
    crops, patches = masks.shape
    size = crops * patches
    flat = masks.reshape(1, size)
    before = (
        lax.broadcasted_iota(jnp.int32, (size, size), 0) < lax.broadcasted_iota(jnp.int32, (size, size), 1)
    ).astype(BF16)
    place = jnp.dot(flat.astype(BF16), before, preferred_element_type=F32).astype(jnp.int32)
    slots = lax.broadcasted_iota(jnp.int32, (CAP, size), 0)
    picked = (place == slots) & (flat > 0)
    dead = slots >= jnp.sum(flat)
    first = lax.broadcasted_iota(jnp.int32, (CAP, size), 1) == 0
    return (picked | (dead & first)).astype(BF16)


def shards(groups, tokens, teacher_feats, masks, w_in, w_out, proto_student, proto_teacher):
    pick = selection(masks)
    counts = jnp.sum(masks, axis=1)
    ends = jnp.sum(
        jnp.where(jnp.arange(counts.shape[0])[:, None] <= jnp.arange(counts.shape[0])[None, :], counts[:, None], 0),
        axis=0,
    )
    slot = jnp.arange(CAP)[:, None]
    member = ((slot >= (ends - counts)[None, :]) & (slot < ends[None, :])).astype(F32)
    inverse = 1.0 / jnp.maximum(counts, 1).astype(F32)
    weight = (GRAD_SCALE * jnp.sum(member * inverse[None, :], axis=1)).astype(BF16)
    teacher_pick = jnp.dot(pick, teacher_feats, preferred_element_type=F32)
    teacher_rows = (unit_rows(teacher_pick)[0] * FOLD_T).astype(BF16)
    grad_proto, row_loss, d_tokens, wide, narrow = balance(
        groups, teacher_rows, weight.astype(F32).reshape(-1, LANES), pick, tokens, w_in, w_out, proto_teacher, proto_student, 0
    )
    crop_loss = jnp.sum(member * row_loss.reshape(CAP)[:, None], axis=0) * inverse
    grad_in = wide.astype(F32)
    grad_out = narrow.astype(F32)
    return (d_tokens, grad_in, grad_out, grad_proto, crop_loss)


def solution(mesh):
    groups = {"dp": mesh.shape["dp"], "tensor": mesh.shape["tensor"]}
    placed = (
        P("dp", None),
        P("dp", None),
        P("dp", None),
        P("dp", None),
        P("dp", None),
        P(None, ("dp", "tensor")),
        P(None, ("dp", "tensor")),
    )
    return jax.shard_map(
        functools.partial(shards, groups),
        mesh=mesh,
        in_specs=placed,
        out_specs=(P("dp", None), P("dp", None), P("dp", None), P(None, ("dp", "tensor")), P("dp")),
        check_vma=False,
    )
```

```python
import functools

import jax
import jax.numpy as jnp
from jax import lax
from jax.experimental import pallas as pl
from jax.experimental.pallas import tpu as pltpu
from jax.sharding import PartitionSpec as P

ROUNDS = 3
CAP = 256

TEACHER_TEMP = 0.07
STUDENT_TEMP = 0.1
EPS = 1e-06
GRAD_SCALE = 65536.0
LOG2E = 1.4426950408889634
LANES = 128
BLOCK = 1024
ROW_TILE = 64
MESH = pl.DeviceIdType.MESH
F32 = jnp.float32
BF16 = jnp.bfloat16


def gelu_parts(pre):
    cdf = 0.5 * (1.0 + lax.erf(pre * 0.7071067811865476))
    pdf = jnp.exp(-0.5 * pre * pre) * 0.3989422804014327
    return (pre * cdf, cdf + pre * pdf)


def unit_rows(feats):
    inverse = lax.rsqrt(jnp.sum(feats * feats, axis=1, keepdims=True) + EPS)
    return (feats * inverse, inverse)


def unit_columns(protos):
    wide = protos.astype(F32)
    norms = jnp.sqrt(jnp.sum(wide * wide, axis=0, keepdims=True) + EPS)
    return (wide / norms, norms)


def spread(dense, out_ref):
    for c in range(dense.shape[0]):
        row = jnp.broadcast_to(dense[c : c + 1, :], (LANES, LANES))
        out_ref[c * LANES : (c + 1) * LANES, :] = row.T


def gathered(acc_ref, out_ref, base):
    for c in range(acc_ref.shape[0] // LANES):
        turned = acc_ref[c * LANES : (c + 1) * LANES, :].T
        out_ref[base + c : base + c + 1, :] = jnp.sum(turned, axis=0, keepdims=True)


def fold_lanes(values):
    total = values[:, :LANES]
    for start in range(LANES, values.shape[1], LANES):
        total = total + values[:, start : start + LANES]
    return total


def widen(values, cols):
    return jnp.concatenate([values] * (cols // LANES), axis=1)


def two_terms(row):
    high = row.astype(BF16)
    low = (row - high.astype(F32)).astype(BF16)
    return jnp.concatenate([high, low, jnp.zeros((14, row.shape[1]), BF16)], axis=0)


def flatten(dense):
    return jnp.concatenate([dense[c : c + 1, :] for c in range(dense.shape[0])], axis=1)


def row_scale(live, row_sum):
    return live / (row_sum + 1.0 - live)


def greet(groups, many, meanwhile):
    barrier = pltpu.get_barrier_semaphore()
    for axis in ("dp", "tensor"):
        me = lax.axis_index(axis)
        for step in range(1, groups[axis]):
            peer = lax.rem(me + step, groups[axis])
            pl.semaphore_signal(barrier, inc=1, device_id={axis: peer}, device_id_type=MESH)
    meanwhile()
    pl.semaphore_wait(barrier, many)


def remote(source, target, send, recv, where):
    return pltpu.make_async_remote_copy(
        src_ref=source, dst_ref=target, send_sem=send, recv_sem=recv, device_id=where, device_id_type=MESH
    )


class PairGather:
    def __init__(self, n, own, slot, send, recv):
        self.me = lax.axis_index("dp")
        self.flip = 1 - 2 * lax.rem(self.me, 2)
        self.partner = self.me + self.flip
        self.peers = [lax.rem(self.me + step, n) for step in range(2, n, 2)]
        self.own, self.slot, self.send, self.recv = own, slot, send, recv

    def copy(self, source, slot, sender, peer):
        return remote(source, self.slot(slot), self.send.at[sender], self.recv.at[slot], {"dp": peer})

    def start(self):
        for peer in self.peers + [self.partner]:
            self.copy(self.own, self.me, peer, peer).start()

    def arrive(self, slot):
        self.copy(self.own, slot, slot, slot).wait_recv()

    def forward(self, peer):
        self.copy(self.slot(peer), peer, peer + self.flip, self.partner).start()

    def relay(self):
        for peer in self.peers:
            self.arrive(peer)
            self.forward(peer)

    def finish(self):
        self.arrive(self.partner)
        for peer in self.peers:
            self.arrive(peer + self.flip)

    def drain(self):
        for peer in self.peers:
            self.copy(self.own, self.me, peer, peer).wait_send()
            self.copy(self.slot(peer), peer, peer + self.flip, self.partner).wait_send()
        self.copy(self.own, self.me, self.partner, self.partner).wait_send()


class Exchange:
    def __init__(self, axis, n, source, landing, send, recv):
        self.me = lax.axis_index(axis)
        self.axis, self.source, self.landing, self.send, self.recv = axis, source, landing, send, recv
        self.peers = [lax.rem(self.me + step, n) for step in range(1, n)]

    def copy(self, peer, slot):
        return remote(self.source(peer), self.landing(slot), self.send.at[peer], self.recv.at[slot], {self.axis: peer})

    def start(self):
        for peer in self.peers:
            self.copy(peer, self.me).start()

    def arrive(self):
        for peer in self.peers:
            self.copy(peer, peer).wait_recv()

    def drain(self):
        for peer in self.peers:
            self.copy(peer, self.me).wait_send()


class Chain:
    def __init__(self, axis, n, block, send, recv):
        self.me = lax.axis_index(axis)
        self.axis, self.n, self.block, self.send, self.recv = axis, n, block, send, recv

    def copy(self, step, way):
        index = lax.rem(self.me - way * step + self.n, self.n)
        peer = lax.rem(self.me + way + self.n, self.n)
        ref = self.block(index)
        send = self.send.at[self.n if step == 0 and way < 0 else index]
        return remote(ref, ref, send, self.recv.at[index], {self.axis: peer})

    def held(self, step, way):
        index = self.me - way * step
        return (index >= 0) & (index < self.n)

    def each_way(self, step, arrive, send, done):
        for way in (1, -1):
            held = self.held(step, way)
            beyond = self.me + way
            onward = held & (beyond >= 0) & (beyond < self.n)
            if arrive:
                pl.when(held)(lambda way=way: self.copy(step, way).wait_recv())
            if send:
                pl.when(onward)(lambda way=way: self.copy(step, way).start())
            if done:
                pl.when(onward)(lambda way=way: self.copy(step, way).wait_send())

    def start(self):
        self.each_way(0, False, True, False)

    def relay(self, step):
        self.each_way(step, True, step < self.n - 1, False)

    def drain(self):
        for step in range(self.n - 1):
            self.each_way(step, False, False, True)


class Total:
    def __init__(self, n, m, value, near, part, far, sems_n, sems_m):
        self.n, self.m = n, m
        self.value, self.near, self.part, self.far = value, near, part, far
        self.first = Exchange("dp", n, lambda peer: value, lambda slot: near.at[slot], *sems_n)
        self.second = Exchange("tensor", m, lambda peer: part, lambda slot: far.at[slot], *sems_m)

    def start(self):
        self.first.start()
        self.near[self.first.me] = self.value[...]

    def turn(self):
        self.first.arrive()
        total = self.near[0]
        for slot in range(1, self.n):
            total = total + self.near[slot]
        self.part[...] = total
        self.second.start()
        self.far[self.second.me] = total

    def finish(self):
        self.second.arrive()
        total = self.far[0]
        for slot in range(1, self.m):
            total = total + self.far[slot]
        return total

    def drain(self):
        self.first.drain()
        self.second.drain()


def plan(groups, rows, columns, width, depth, hidden):
    n, m = groups["dp"], groups["tensor"]
    dense = rows // LANES
    own = CAP // LANES
    part = CAP // m
    block = min(BLOCK, columns)
    vmem = pltpu.VMEM
    shapes = dict(
        expo=vmem((rows, columns), BF16),
        raised=vmem((rows, columns), BF16),
        cols=vmem((width, columns), BF16),
        teach=vmem((n, CAP, width), BF16),
        weight=vmem((n, own, LANES), F32),
        weights=vmem((dense, LANES), F32),
        rows_in=vmem((CAP, depth), BF16),
        w_all=vmem((depth, hidden), BF16),
        wo_all=vmem((hidden, width), BF16),
        featp=vmem((CAP, width), F32),
        grad_feats=vmem((CAP, width), BF16),
        near_f=vmem((m, part, width), F32),
        feats=vmem((part, width), F32),
        stud=vmem((n, CAP, width), BF16),
        s_prob=vmem((width, rows), BF16),
        s_target=vmem((width, rows), BF16),
        acc_a=vmem((rows, width), BF16),
        acc_b=vmem((rows, width), BF16),
        g_own=vmem((CAP, width), F32),
        g_near=vmem((n, CAP, width), BF16),
        g_part=vmem((CAP, width), BF16),
        g_far=vmem((m, part, width), BF16),
        c_out=vmem((n, own, LANES), F32),
        c_near=vmem((n, own, LANES), F32),
        c_part=vmem((own, LANES), F32),
        c_far=vmem((m, own, LANES), F32),
        colacc=vmem((8, columns), F32),
        scale=vmem((8, columns), F32),
        inverse=vmem((8, columns), F32),
        u_terms=vmem((16, rows), BF16),
        acc=vmem((CAP, LANES), F32),
        spread_a=vmem((CAP, LANES), F32),
        spread_b=vmem((CAP, LANES), F32),
        probs=vmem((dense, LANES), F32),
        targets=vmem((dense, LANES), F32),
        last=vmem((2 * dense, LANES), F32),
        stage=vmem((2, max(width, CAP), block), F32),
        wide_a=vmem((n // 2, depth // n, hidden // m), BF16),
        wide_b=vmem((n // 2, depth // n, hidden // m), BF16),
        narrow_a=vmem((n, hidden // n // m, width), BF16),
        wide_sems=pltpu.SemaphoreType.DMA((4 * (hidden // m // LANES), n)),
        pair_send=pltpu.SemaphoreType.DMA((11 + m, n)),
        pair_recv=pltpu.SemaphoreType.DMA((11 + m, n)),
        line_send=pltpu.SemaphoreType.DMA((9 + hidden // m // LANES, m + 1)),
        line_recv=pltpu.SemaphoreType.DMA((9 + hidden // m // LANES, m + 1)),
        local=pltpu.SemaphoreType.DMA((8 + depth // width,)),
    )
    for turn in range(ROUNDS):
        size = 2 * dense if turn == ROUNDS - 1 else dense
        shapes[f"value{turn}"] = vmem((size, LANES), F32)
        shapes[f"near{turn}"] = vmem((n, size, LANES), F32)
        shapes[f"part{turn}"] = vmem((size, LANES), F32)
        shapes[f"far{turn}"] = vmem((m, size, LANES), F32)
    return shapes


FOLD_T = LOG2E / TEACHER_TEMP
FOLD_S = LOG2E / STUDENT_TEMP


def balance_kernel(groups, names, *refs):
    n, m = groups["dp"], groups["tensor"]
    teach_own, weight_own, pick, tokens, w_in, w_out, proto_t, proto_s = refs[:8]
    grad_proto, loss, d_tokens, wide_out, narrow_out = refs[8:13]
    r = dict(zip(names, refs[13:]))
    rows_in = r["rows_in"]
    expo, raised, cols, w_all, wo_all, grad_feats = (
        r["expo"], r["raised"], r["cols"], r["w_all"], r["wo_all"], r["grad_feats"]
    )
    teach, weight, stud, acc, scale = r["teach"], r["weight"], r["stud"], r["acc"], r["scale"]
    acc_a, acc_b, local = r["acc_a"], r["acc_b"], r["local"]
    rows, columns = expo.shape
    width = cols.shape[0]
    dense = rows // LANES
    own = CAP // LANES
    block = r["stage"].shape[2]
    depth = w_in.shape[0]
    slab = w_all.shape[1] // m
    part = CAP // m
    me, z = lax.axis_index("dp"), lax.axis_index("tensor")
    half = n // 2
    flip = 1 - 2 * lax.rem(me, 2)

    def pair(k):
        return r["pair_send"].at[k], r["pair_recv"].at[k]

    def line(k):
        return r["line_send"].at[k], r["line_recv"].at[k]

    def place(step):
        return lax.rem(me + 2 * lax.rem(step, half), n) + flip * (step // half)

    def of_block(j):
        if isinstance(j, int):
            return slice(j * block, (j + 1) * block)
        return pl.ds(pl.multiple_of(j * block, block), block)

    def of_slot(slot):
        return pl.ds(pl.multiple_of(slot * CAP, CAP), CAP)

    def each(low, high, body, unroll=1):
        def step(j, carry):
            body(j)
            return carry

        lax.fori_loop(low, high, step, 0, unroll=unroll)

    teach_g = PairGather(n, teach_own, lambda s: teach.at[s], *pair(0))
    weight_g = PairGather(n, weight_own, lambda s: weight.at[s], *pair(1))

    def of_slab(k):
        return pl.ds(pl.multiple_of(k * slab, slab), slab)

    def of_depth(slot):
        return pl.ds(pl.multiple_of(slot * depth, depth), depth)

    def w_gather(k, index):
        lanes = of_slab(k)
        return PairGather(n, w_all.at[of_depth(me), lanes], lambda s: w_all.at[of_depth(s), lanes], *pair(index))

    w_now = w_gather(z, 2)
    w_later = [w_gather(lax.rem(z + k, m), 10 + k) for k in range(1, m)]
    tall = w_out.shape[0]
    wo_g = PairGather(n, w_out, lambda s: wo_all.at[pl.ds(pl.multiple_of(s * tall, tall), tall), :], *pair(3))
    stud_g = PairGather(n, stud.at[me], lambda s: stud.at[s], *pair(4))
    totals = [
        Total(n, m, r[f"value{k}"], r[f"near{k}"], r[f"part{k}"], r[f"far{k}"], pair(5 + k), line(2 + k))
        for k in range(ROUNDS)
    ]
    grads = Exchange("dp", n, lambda p: acc_a.at[of_slot(p), :], lambda s: r["g_near"].at[s], *pair(8))
    crosses = Exchange("dp", n, lambda p: r["c_out"].at[p], lambda s: r["c_near"].at[s], *pair(9))

    def of_part(k):
        return pl.ds(pl.multiple_of(k * part, part), part)

    feat_x = Exchange("tensor", m, lambda p: r["featp"].at[of_part(p), :], lambda s: r["near_f"].at[s], *line(0))
    stud_x = Exchange(
        "tensor", m, lambda p: stud.at[me, of_part(z), :], lambda s: stud.at[me, of_part(s), :], *line(1)
    )
    grad_x = Exchange("tensor", m, lambda p: r["g_part"].at[of_part(p), :], lambda s: r["g_far"].at[s], *line(5))
    cross_x = Exchange("tensor", m, lambda p: r["c_part"], lambda s: r["c_far"].at[s], *line(6))
    back_x = Exchange(
        "tensor", m, lambda p: grad_feats.at[of_part(z), :], lambda s: grad_feats.at[of_part(s), :], *line(7)
    )

    def unit_cols(factor, keep):
        def one(j):
            here = of_block(j)
            wide = cols[:, here].astype(F32)
            inv = 1.0 / jnp.sqrt(jnp.sum(wide * wide, axis=0, keepdims=True) + EPS)
            if keep is not None:
                keep[:, here] = jnp.broadcast_to(inv, (8, block))
            cols[:, here] = (wide * (inv * factor)).astype(BF16)

        each(0, columns // block, one)

    def teacher_chunk(slot):
        bias = jnp.where(weight[slot] > 0, 0.0, -1e4)
        spread(bias, r["spread_a"])

        def one(j):
            here = of_block(j)
            dots = jnp.dot(teach[slot], cols[:, here], preferred_element_type=F32)
            power = jnp.exp2(dots + widen(r["spread_a"][...], block))
            expo[of_slot(slot), here] = power.astype(BF16)
            total = power[:8, :]
            for start in range(8, CAP, 8):
                total = total + power[start : start + 8, :]
            r["colacc"][:, here] += total

        for j in range(columns // block):
            one(j)

    def row_pass(store, out):
        def one(k):
            def tile(i):
                here = pl.ds(pl.multiple_of(k * CAP + i * ROW_TILE, ROW_TILE), ROW_TILE)
                total = None
                for start in range(0, columns, LANES):
                    lanes = slice(start, start + LANES)
                    value = expo[here, lanes].astype(F32) * jnp.concatenate([scale[:, lanes]] * (ROW_TILE // 8), axis=0)
                    if store:
                        expo[here, lanes] = value.astype(BF16)
                    total = value if total is None else total + value
                acc[pl.ds(pl.multiple_of(i * ROW_TILE, ROW_TILE), ROW_TILE), :] = total

            each(0, CAP // ROW_TILE, tile, 2)
            gather_rows(out, k * own)

        each(0, n, one)

    def gather_rows(out, base):
        for c in range(own):
            turned = acc[c * LANES : (c + 1) * LANES, :].T
            out[pl.ds(base + c, 1), :] = jnp.sum(turned, axis=0, keepdims=True)

    def column_pass(u):
        r["u_terms"][...] = two_terms(flatten(u))

        def one(j):
            here = of_block(j)
            total = jnp.dot(r["u_terms"][...], expo[:, here], preferred_element_type=F32)
            scale[:, here] = jnp.broadcast_to(1.0 / (total[0:1, :] + total[1:2, :]), (8, block))

        for j in range(columns // block):
            one(j)

    def student_chunk(slot):
        acc[...] = jnp.zeros_like(acc)

        def one(j):
            here = of_block(j)
            for start in range(0, block, width):
                lanes = slice(j * block + start, j * block + start + width)
                power = jnp.exp2(jnp.dot(stud[slot], cols[:, lanes], preferred_element_type=F32))
                raised[of_slot(slot), lanes] = power.astype(BF16)
                acc[...] += fold_lanes(power)

        for j in range(columns // block):
            one(j)
        gather_rows(r[f"value{ROUNDS - 1}"], dense + slot * own)
        acc_a[of_slot(slot), :] = lax.dot_general(
            raised[of_slot(slot), :], cols[...], (((1,), (1,)), ((), ())), preferred_element_type=F32
        ).astype(BF16)

    def student_own():
        feat_x.arrive()
        feats = r["featp"][of_part(z), :]
        for peer in feat_x.peers:
            feats = feats + r["near_f"][peer]
        r["feats"][...] = feats
        stud[me, of_part(z), :] = unit_rows(feats)[0].astype(BF16)
        stud_x.start()

    def target_chunk(slot):
        term = lax.dot_general(
            expo[of_slot(slot), :], cols[...], (((1,), (1,)), ((), ())), preferred_element_type=F32
        )
        acc_b[of_slot(slot), :] = term.astype(BF16)
        acc[...] = fold_lanes(stud[slot].astype(F32) * term)
        gather_rows(r["c_out"].at[slot], 0)

    load_t = pltpu.make_async_copy(proto_t, cols, local.at[0])
    load_s = pltpu.make_async_copy(proto_s, cols, local.at[1])
    load_w = pltpu.make_async_copy(w_in, w_all.at[of_depth(me), :], local.at[2])
    load_w.start()
    load_t.start()
    patches = tokens.shape[0]
    in_row = block // width

    def of_width(k):
        if isinstance(k, int):
            return slice(k * width, (k + 1) * width)
        return pl.ds(pl.multiple_of(k * width, width), width)

    def token_home(k):
        return slice(k // in_row * patches, (k // in_row + 1) * patches), of_width(k % in_row)

    token_loads = [
        pltpu.make_async_copy(tokens.at[:, of_width(k)], raised.at[token_home(k)], local.at[8 + k])
        for k in range(w_all.shape[0] // width)
    ]
    for load in token_loads:
        load.start()

    def meanwhile():
        r["colacc"][...] = jnp.zeros_like(r["colacc"])
        load_t.wait()
        unit_cols(1.0, None)

    greet(groups, n + m - 2, meanwhile)
    teach_g.start()
    weight_g.start()
    teach[me] = teach_own[...]
    weight[me] = weight_own[...]
    wo_all[pl.ds(pl.multiple_of(me * tall, tall), tall), :] = w_out[...]
    teacher_chunk(me)
    for k, load in enumerate(token_loads):
        load.wait()
        rows_in[:, of_width(k)] = jnp.dot(pick[...], raised[token_home(k)], preferred_element_type=F32).astype(BF16)
    teach_g.relay()
    weight_g.relay()
    load_w.wait()
    w_now.start()
    wo_g.start()
    each(1, half, lambda step: teacher_chunk(place(step)))

    def teacher_late(step):
        teach_g.arrive(place(step))
        weight_g.arrive(place(step))
        teacher_chunk(place(step))

    each(half, n, teacher_late)
    load_s.start()
    weights = jnp.concatenate([weight[slot] for slot in range(n)], axis=0)
    r["weights"][...] = weights
    live = (weights > 0).astype(F32)
    scale[...] = jnp.broadcast_to(1.0 / jnp.sum(r["colacc"][...], axis=0, keepdims=True), scale.shape)
    row_pass(False, r["value0"])
    totals[0].start()

    load_s.wait()
    unit_cols(FOLD_S, r["inverse"])
    w_now.relay()
    wo_g.relay()
    totals[0].turn()
    w_now.finish()
    wo_g.finish()
    pre = jnp.dot(rows_in[...], w_all[:, of_slab(z)], preferred_element_type=F32)
    hidden = gelu_parts(pre)[0].astype(BF16)
    r["featp"][...] = jnp.dot(hidden, wo_all[of_slab(z), :], preferred_element_type=F32)
    feat_x.start()
    total = totals[0].finish()
    for turn in range(1, ROUNDS - 1):
        column_pass(row_scale(live, total))
        if turn == ROUNDS - 2:
            student_own()
        row_pass(False, r[f"value{turn}"])
        totals[turn].start()
        if turn < ROUNDS - 2:
            totals[turn].turn()
            total = totals[turn].finish()
    stud_x.arrive()
    stud_g.start()
    student_chunk(me)
    stud_g.relay()
    totals[ROUNDS - 2].turn()
    for gather in w_later:
        gather.start()
    each(1, half, lambda step: student_chunk(place(step)))
    stud_g.finish()
    each(half, n, lambda step: student_chunk(place(step)))
    total = totals[ROUNDS - 2].finish()
    column_pass(row_scale(live, total))
    row_pass(True, r[f"value{ROUNDS - 1}"])
    final = totals[ROUNDS - 1]
    final.start()

    def turn_rows(slot):
        r["s_prob"][:, of_slot(slot)] = stud[slot].astype(F32).T.astype(BF16)

    each(0, n, turn_rows, 2)
    each(0, half, target_chunk)
    final.turn()
    each(half, n, target_chunk)
    load_s.start()
    crosses.start()
    sums = final.finish()
    r["last"][...] = sums
    live = (r["weights"][...] > 0).astype(F32)
    factor = r["weights"][...] * (1.0 / STUDENT_TEMP)
    u = row_scale(live, sums[:dense])
    r["probs"][...] = factor / sums[dense:]
    r["targets"][...] = factor * u

    def mix(slot):
        spread(r["probs"][pl.ds(slot * own, own), :], r["spread_a"])
        spread(r["targets"][pl.ds(slot * own, own), :], r["spread_b"])
        return acc_a[of_slot(slot), :].astype(F32) * widen(r["spread_a"][...], width) - acc_b[
            of_slot(slot), :
        ].astype(F32) * widen(r["spread_b"][...], width)

    def send_mix(step):
        peer = lax.rem(me + step, n)
        acc_a[of_slot(peer), :] = mix(peer).astype(BF16)
        grads.copy(peer, me).start()

    each(1, n, send_mix)
    r["g_own"][...] = mix(me)

    def scale_rows(slot):
        here = of_slot(slot)
        turned = r["s_prob"][:, here].astype(F32)
        base = pl.ds(slot * own, own)
        r["s_target"][:, here] = (turned * flatten(r["targets"][base, :])).astype(BF16)
        r["s_prob"][:, here] = (turned * flatten(r["probs"][base, :])).astype(BF16)

    each(0, n, scale_rows)

    def owner_sums():
        crosses.arrive()
        cross = r["c_out"][me]
        for peer in crosses.peers:
            cross = cross + r["c_near"][peer]
        r["c_part"][...] = cross
        cross_x.start()
        grads.arrive()
        grad = r["g_own"][...]
        for peer in grads.peers:
            grad = grad + r["g_near"][peer].astype(F32)
        r["g_own"][...] = grad
        r["g_part"][...] = grad.astype(BF16)
        grad_x.start()

    def owner_grads():
        cross_x.arrive()
        cross = r["c_part"][...]
        for peer in cross_x.peers:
            cross = cross + r["c_far"][peer]
        mine = pl.ds(me * own, own)
        u = row_scale((r["weights"][mine, :] > 0).astype(F32), r["last"][mine, :])
        loss[...] = jnp.log(r["last"][pl.ds(dense + me * own, own), :]) - u * cross * (1.0 / LOG2E)
        grad_x.arrive()
        grad = r["g_own"][of_part(z), :]
        for peer in grad_x.peers:
            grad = grad + r["g_far"][peer].astype(F32)
        unit, inv = unit_rows(r["feats"][...])
        grad = grad * (1.0 / FOLD_S)
        inner = jnp.sum(unit * grad, axis=1, keepdims=True)
        grad_feats[of_part(z), :] = (inv * (grad - unit * inner)).astype(BF16)
        back_x.start()


    def out_copy(j):
        return pltpu.make_async_copy(
            r["stage"].at[lax.rem(j, 2)], grad_proto.at[:, of_block(j)], local.at[4 + lax.rem(j, 2)]
        )

    def column_grad(j):
        @pl.when(j >= 2)
        def _():
            out_copy(j - 2).wait()

        here = of_block(j)
        grad = jnp.dot(r["s_prob"][...], raised[:, here], preferred_element_type=F32) - jnp.dot(
            r["s_target"][...], expo[:, here], preferred_element_type=F32
        )
        inv = r["inverse"][0:1, here]
        unit = cols[:, here].astype(F32) * inv
        r["stage"][lax.rem(j, 2)] = (grad - unit * jnp.sum(unit * grad, axis=0, keepdims=True)) * inv
        out_copy(j).start()

    blocks = columns // block
    load_s.wait()
    each(0, blocks // 2, column_grad)
    owner_sums()
    for gather in w_later:
        gather.relay()
    each(blocks // 2, blocks, column_grad)
    owner_grads()

    for gather in w_later:
        gather.finish()

    for j in range(max(0, blocks - 2), blocks):
        out_copy(j).wait()
    per = block // width
    hidden_blocks = w_all.shape[1] // width
    whole_depth = w_all.shape[0]
    pieces = slab // LANES

    def hidden_block(b):
        pre = jnp.dot(rows_in[...], w_all[:, of_width(b)], preferred_element_type=F32)
        act, slope = gelu_parts(pre)
        raised[of_slot(b), 0:width] = act.astype(BF16)
        r["stage"][b // per, 0:CAP, of_width(lax.rem(b, per))] = slope

    each(0, hidden_blocks, hidden_block, 2)

    def turn_tokens(k):
        expo[of_width(k), width : width + CAP] = rows_in[:, of_width(k)].astype(F32).T.astype(BF16)

    each(0, whole_depth // width, turn_tokens)
    own_live = (r["weights"][pl.ds(me * own, own), :] > 0).astype(F32)
    for start in range(0, patches, CAP):
        turned = pick[:, start : start + CAP].astype(F32).T
        acc_b[start : start + CAP, :] = (turned * flatten(own_live)).astype(BF16)

    for gather in [teach_g, weight_g, w_now, wo_g, stud_g] + w_later:
        gather.drain()
    for one in totals + [grads, crosses, feat_x, stud_x, grad_x, cross_x]:
        one.drain()
    back_x.arrive()
    back_x.drain()

    lane_in, lane_mid = width + CAP, 2 * width

    def back_block(b):
        grad_hidden = lax.dot_general(
            grad_feats[...], wo_all[of_width(b), :], (((1,), (1,)), ((), ())), preferred_element_type=F32
        )
        expo[of_slot(b), 0:width] = (grad_hidden * r["stage"][b // per, 0:CAP, of_width(lax.rem(b, per))]).astype(BF16)

    def out_block(b):
        raised[of_width(b), width : 2 * width] = lax.dot_general(
            raised[of_slot(b), 0:width], grad_feats[...], (((0,), (0,)), ((), ())), preferred_element_type=F32
        ).astype(BF16)

    side = lax.rem(me, 2)
    team = me // 2
    teams = [lax.rem(team + step, half) for step in range(1, half)]

    def pair_copy(q, h):
        lanes = slice(h * LANES, (h + 1) * LANES)
        return remote(
            expo.at[of_depth(2 * q + 1 - side), lane_in + h * LANES : lane_in + (h + 1) * LANES],
            r["wide_a"].at[q, :, lanes],
            r["wide_sems"].at[h, q],
            r["wide_sems"].at[pieces + h, q],
            {"dp": me + flip},
        )

    def team_copy(q, slot, h):
        lanes = slice(h * LANES, (h + 1) * LANES)
        return remote(
            raised.at[of_depth(q), lane_mid + h * LANES : lane_mid + (h + 1) * LANES],
            r["wide_b"].at[slot, :, lanes],
            r["wide_sems"].at[2 * pieces + h, q],
            r["wide_sems"].at[3 * pieces + h, slot],
            {"dp": 2 * q + side},
        )

    def own_term(q, h):
        lanes = slice(h * LANES, (h + 1) * LANES)
        mine = expo[of_depth(2 * q + side), lane_in + h * LANES : lane_in + (h + 1) * LANES]
        return mine.astype(F32) + r["wide_a"][q, :, lanes].astype(F32)

    def wide_lanes(s, h):
        return pl.ds(pl.multiple_of(s * slab + h * LANES, LANES), LANES)

    def wide_exchange(h):
        return Chain("tensor", m, lambda s: wide_out.at[:, wide_lanes(s, h)], *line(9 + h))

    wide_x = [wide_exchange(h) for h in range(pieces)]
    sub = tall // m
    narrow_n = Exchange(
        "dp",
        n,
        lambda p: raised.at[pl.ds(pl.multiple_of(p * tall + z * sub, sub), sub), width : 2 * width],
        lambda s: r["narrow_a"].at[s],
        *pair(10),
    )

    def of_sub(s):
        return pl.ds(pl.multiple_of(s * sub, sub), sub)

    narrow_x = Exchange("tensor", m, lambda p: narrow_out.at[of_sub(z), :], lambda s: narrow_out.at[of_sub(s), :], *line(8))

    for b in range(slab // width):
        mine = z * (slab // width) + b
        back_block(mine)

        def in_block(p):
            expo[of_depth(p), lane_in + b * width : lane_in + (b + 1) * width] = jnp.dot(
                expo[of_depth(p), width : width + CAP], expo[of_slot(mine), 0:width], preferred_element_type=F32
            ).astype(BF16)

        for q in teams + [team]:
            in_block(2 * q + 1 - side)
        for h in range(b * width // LANES, (b + 1) * width // LANES):
            for q in teams + [team]:
                pair_copy(q, h).start()
        for q in teams + [team]:
            in_block(2 * q + side)
    each(0, hidden_blocks, out_block, 2)
    narrow_n.start()
    for h in range(pieces):
        for q in teams:
            pair_copy(q, h).wait_recv()
            raised[of_depth(q), lane_mid + h * LANES : lane_mid + (h + 1) * LANES] = own_term(q, h).astype(BF16)
            team_copy(q, team, h).start()
        pair_copy(team, h).wait_recv()
    each(0, hidden_blocks, back_block, 2)
    for h in range(pieces):
        for q in teams:
            team_copy(q, q, h).wait_recv()
        total = own_term(team, h)
        for q in teams:
            total = total + r["wide_b"][q, :, h * LANES : (h + 1) * LANES].astype(F32)
        wide_out[:, wide_lanes(z, h)] = total.astype(BF16)
        wide_x[h].start()
    narrow_n.arrive()
    total = raised[pl.ds(pl.multiple_of(me * tall + z * sub, sub), sub), width : 2 * width].astype(F32)
    for peer in narrow_n.peers:
        total = total + r["narrow_a"][peer].astype(F32)
    narrow_out[of_sub(z), :] = total.astype(BF16)
    narrow_x.start()

    def token_slot(k):
        return pl.ds(pl.multiple_of(lax.rem(k, 2) * patches, patches), patches)

    def token_copy(k):
        return pltpu.make_async_copy(
            acc_a.at[token_slot(k), :], d_tokens.at[:, of_width(k)], local.at[6 + lax.rem(k, 2)]
        )

    def token_block(k):
        total = None
        for b in range(hidden_blocks):
            term = lax.dot_general(
                expo[b * CAP : (b + 1) * CAP, 0:width],
                w_all[of_width(k), b * width : (b + 1) * width],
                (((1,), (1,)), ((), ())),
                preferred_element_type=F32,
            )
            total = term if total is None else total + term
        @pl.when(k >= 2)
        def _():
            token_copy(k - 2).wait()

        acc_a[token_slot(k), :] = jnp.dot(
            acc_b[0:patches, :], total.astype(BF16), preferred_element_type=F32
        ).astype(BF16)
        token_copy(k).start()

    token_blocks = whole_depth // width
    for step in range(1, m):
        each(token_blocks * (step - 1) // (m - 1), token_blocks * step // (m - 1), token_block)
        for one in wide_x:
            one.relay(step)
    narrow_x.arrive()
    for one in wide_x + [narrow_n, narrow_x]:
        one.drain()
    for h in range(pieces):
        for q in teams:
            pair_copy(q, h).wait_send()
            team_copy(q, team, h).wait_send()
        pair_copy(team, h).wait_send()
    for k in range(max(0, token_blocks - 2), token_blocks):
        token_copy(k).wait()


def balance(groups, teach, weight, pick, tokens, w_in, w_out, proto_t, proto_s, ident):
    n, m = groups["dp"], groups["tensor"]
    rows, width = n * teach.shape[0], teach.shape[1]
    columns = proto_s.shape[1]
    depth, hidden = n * w_in.shape[0], w_in.shape[1]
    shapes = plan(groups, rows, columns, width, depth, hidden)
    vmem, hbm = pl.BlockSpec(memory_space=pltpu.VMEM), pl.BlockSpec(memory_space=pl.ANY)
    return pl.pallas_call(
        functools.partial(balance_kernel, groups, list(shapes)),
        name="balance",
        in_specs=[vmem, vmem, vmem, hbm, hbm, vmem, hbm, hbm],
        out_specs=[hbm, vmem, hbm, vmem, vmem],
        out_shape=[
            jax.ShapeDtypeStruct((width, columns), F32),
            jax.ShapeDtypeStruct((CAP // LANES, LANES), F32),
            jax.ShapeDtypeStruct(tokens.shape, BF16),
            jax.ShapeDtypeStruct((depth // n, hidden), BF16),
            jax.ShapeDtypeStruct((hidden // n, width), BF16),
        ],
        scratch_shapes=list(shapes.values()),
        compiler_params=pltpu.CompilerParams(
            collective_id=ident, has_side_effects=True, vmem_limit_bytes=62 * 1024 * 1024
        ),
    )(teach, weight, pick, tokens, w_in, w_out, proto_t, proto_s)


def selection(masks):
    crops, patches = masks.shape
    size = crops * patches
    flat = masks.reshape(1, size)
    before = (
        lax.broadcasted_iota(jnp.int32, (size, size), 0) < lax.broadcasted_iota(jnp.int32, (size, size), 1)
    ).astype(BF16)
    place = jnp.dot(flat.astype(BF16), before, preferred_element_type=F32).astype(jnp.int32)
    slots = lax.broadcasted_iota(jnp.int32, (CAP, size), 0)
    picked = (place == slots) & (flat > 0)
    dead = slots >= jnp.sum(flat)
    first = lax.broadcasted_iota(jnp.int32, (CAP, size), 1) == 0
    return (picked | (dead & first)).astype(BF16)


def shards(groups, tokens, teacher_feats, masks, w_in, w_out, proto_student, proto_teacher):
    pick = selection(masks)
    counts = jnp.sum(masks, axis=1)
    ends = jnp.sum(
        jnp.where(jnp.arange(counts.shape[0])[:, None] <= jnp.arange(counts.shape[0])[None, :], counts[:, None], 0),
        axis=0,
    )
    slot = jnp.arange(CAP)[:, None]
    member = ((slot >= (ends - counts)[None, :]) & (slot < ends[None, :])).astype(F32)
    inverse = 1.0 / jnp.maximum(counts, 1).astype(F32)
    weight = (GRAD_SCALE * jnp.sum(member * inverse[None, :], axis=1)).astype(BF16)
    teacher_pick = jnp.dot(pick, teacher_feats, preferred_element_type=F32)
    teacher_rows = (unit_rows(teacher_pick)[0] * FOLD_T).astype(BF16)
    grad_proto, row_loss, d_tokens, wide, narrow = balance(
        groups, teacher_rows, weight.astype(F32).reshape(-1, LANES), pick, tokens, w_in, w_out, proto_teacher, proto_student, 0
    )
    crop_loss = jnp.sum(member * row_loss.reshape(CAP)[:, None], axis=0) * inverse
    grad_in = wide.astype(F32)
    grad_out = narrow.astype(F32)
    return (d_tokens, grad_in, grad_out, grad_proto, crop_loss)


def solution(mesh):
    groups = {"dp": mesh.shape["dp"], "tensor": mesh.shape["tensor"]}
    placed = (
        P("dp", None),
        P("dp", None),
        P("dp", None),
        P("dp", None),
        P("dp", None),
        P(None, ("dp", "tensor")),
        P(None, ("dp", "tensor")),
    )
    return jax.shard_map(
        functools.partial(shards, groups),
        mesh=mesh,
        in_specs=placed,
        out_specs=(P("dp", None), P("dp", None), P("dp", None), P(None, ("dp", "tensor")), P("dp")),
        check_vma=False,
    )
```
